128 devices in a mesh: gx: 8 (over z, core), gy: 16 (over y, x).
Axes of the slice: x: 4, y: 4, z: 4, core: 2. Of those that a mesh axis runs over, the one named last changes fastest.
Arguments:
- stored_vectors: bfloat16 [2, 16, 64, 8192], P(None, None, 'gx', 'gy'), may hold values from -4 to 4
- disorder: float32 [2, 64, 8192], P(None, 'gx', 'gy'), may hold values from -1.5 to 1.5
- vacancy: int32 [2, 64, 8192], P(None, 'gx', 'gy'), may hold values 0 or 1
- plan: int32 [64], replicated, may hold values from 0 to 63, as said below
Outputs:
- local_moments: float32 [4, 2, 64, 8192], P(None, None, 'gx', 'gy')
- trace_moments: float32 [4, 16], replicated
The draws below stay inside these ranges and needn't reach their ends.
Inputs may be any that keep to these rules, and one draw needn't show every extreme that they name: plan is a permutation of 0 to 63; stored block b is held by the device at gy index b // 4. The 4 lattice blocks of one device come from 4 different devices, and the 4 stored blocks of one device go to 4 different devices.
All inputs are finite; a program needn't handle non-finite values. No bound on the sum of `vacancy` on one device may be relied on, other than what follows from the above.
Results may differ from the reference program's by a relative error of at most 0.0003.
Values may be sent and summed in bfloat16 or wider, within the bound.
No kernel may reach another device: no remote copies, remote signals or barrier semaphores. Data moves between devices by JAX's collectives and lax.ppermute only.
A program may use at most 64 MiB of HBM per device.

```python
import jax
import jax.numpy as jnp

BLOCK = 128
NB = 4
R = 16
TERMS = 4
LX = 64
LY = 8192
NBLK = 64


def draw_plan(key, part):
    devices = NBLK // NB
    key_tau, key_rho, key_offset, key_slot = jax.random.split(jax.random.fold_in(key, 7), 4)
    relabel = jax.random.permutation(key_tau, devices)
    order = jax.random.permutation(key_rho, devices)
    offsets = jax.random.permutation(key_offset, devices)[:NB]
    slots = jax.random.permutation(key_slot, NB)
    receiver = jnp.arange(devices)[:, None]
    within = jnp.arange(NB)[None, :]
    source = relabel[(order[receiver] + offsets[within]) % devices]
    return (source * NB + slots[within]).reshape(-1).astype(jnp.int32)


def place_ends(drawn, rng, low, high):
    extent = drawn.shape
    place = [jax.random.randint(jax.random.fold_in(rng, axis), (), 0, extent[axis]) for axis in range(len(extent))]
    drawn = drawn.at[tuple(place)].set(low)
    longest = extent.index(max(extent))
    place[longest] = (place[longest] + 1) % extent[longest]
    return drawn.at[tuple(place)].set(high)


def shard_levels(stream_key, shape, cuts, smallest, top_value):
    loudness, own = 1.0, jax.random.fold_in(stream_key, 6)
    for position, blocks in cuts:
        heights = jnp.exp(jax.random.uniform(jax.random.fold_in(own, position), (blocks,), jnp.float32, smallest / len(cuts), top_value / len(cuts)))
        loudness = loudness * jnp.repeat(heights, shape[position] // blocks).reshape([-1 if axis == position else 1 for axis in range(len(shape))])
    return loudness


def normal_values(own_key, extent, width, most, shards=(), kind=jnp.bfloat16):
    result = jax.random.normal(own_key, extent, jnp.float32) * width
    if len(shards) > 0:
        result = shard_levels(own_key, extent, shards, -0.22, 0.18) * result
    return jnp.clip(result, min=-most, max=most).astype(kind)


def setup_inputs(seed: int = 0) -> dict:
    key_list = jax.random.split(jax.random.key(seed), 5)
    stored_vectors = normal_values(key_list[0], (2, R, LX, LY), 1.0, 4.0, ((2, 8), (3, 16)))
    disorder = jnp.clip(jax.random.uniform(key_list[1], (2, LX, LY), jnp.float32, -1.5, 1.5) * shard_levels(key_list[1], (2, LX, LY), ((1, 8), (2, 16)), -0.4, 0.0), -1.5, 1.5)
    vacancy = place_ends((jax.random.randint(key_list[2], (2, LX, LY), 0, 10) < 9).astype(jnp.int32), jax.random.fold_in(key_list[2], 1), 0, 1)
    plan = draw_plan(jax.random.fold_in(key_list[4], 71), 0)
    return {"stored_vectors": stored_vectors, "disorder": disorder, "vacancy": vacancy, "plan": plan}


HOP_NEAR = 1.0
HOP_NEXT = 0.3
TWIST_COS = 0.4535961214255773
TWIST_SIN = 0.8912073600614354
SPREAD = 6.5
NEAR_A = ((0, 0), (-1, 0), (0, -1))
NEAR_B = ((0, 0), (1, 0), (0, 1))
SECOND = ((1, 0), (-1, 1), (0, -1))


def collect_sum(fetch, field, shifts):
    total = fetch(field, shifts[0])
    for shift in shifts[1:]:
        total = total + fetch(field, shift)
    return total


def hamilton(fetch, real, imag, onsite, keep):
    backs = tuple((-a, -b) for a, b in SECOND)
    out_real = []
    out_imag = []
    for sublat, chiral, bonds in ((0, 1.0, NEAR_A), (1, -1.0, NEAR_B)):
        other = 1 - sublat
        near_real = collect_sum(fetch, real[other], bonds)
        forward_real = collect_sum(fetch, real[sublat], SECOND)
        backward_real = collect_sum(fetch, real[sublat], backs)
        centre_real = fetch(real[sublat], (0, 0))
        mixed_real = TWIST_COS * (forward_real + backward_real)
        mixed_imag = chiral * TWIST_SIN * (forward_real - backward_real)
        level = onsite[sublat][None]
        if imag is None:
            result_imag = HOP_NEXT * mixed_imag
        else:
            near_imag = collect_sum(fetch, imag[other], bonds)
            forward_imag = collect_sum(fetch, imag[sublat], SECOND)
            backward_imag = collect_sum(fetch, imag[sublat], backs)
            centre_imag = fetch(imag[sublat], (0, 0))
            mixed_real = mixed_real - chiral * TWIST_SIN * (forward_imag - backward_imag)
            mixed_imag = mixed_imag + TWIST_COS * (forward_imag + backward_imag)
            result_imag = level * centre_imag - HOP_NEAR * near_imag + HOP_NEXT * mixed_imag
        result_real = level * centre_real - HOP_NEAR * near_real + HOP_NEXT * mixed_real
        factor = keep[sublat][None] / SPREAD
        out_real.append(result_real * factor)
        out_imag.append(result_imag * factor)
    return jnp.stack(out_real), jnp.stack(out_imag)


def rolled(field, shift):
    return jnp.roll(field, (-shift[0], -shift[1]), axis=(1, 2))


def reference(stored_vectors, disorder, vacancy, plan):
    blocks = stored_vectors.reshape(2, R, LX, NBLK, BLOCK)
    lattice = jnp.take(blocks, plan.astype(jnp.int32), axis=3).reshape(2, R, LX, LY)
    keep = vacancy.astype(jnp.float32)
    start = lattice.astype(jnp.float32) * keep[:, None]
    locals_list = []
    traces = []
    previous_real, previous_imag = start, None
    current_real, current_imag = hamilton(rolled, start, None, disorder, keep)
    locals_list.append(jnp.sum(start * current_real, axis=1) / R)
    traces.append(jnp.sum(start * current_real, axis=(0, 2, 3)) / (2 * LX * LY))
    for term in range(1, TERMS):
        image_real, image_imag = hamilton(rolled, current_real, current_imag, disorder, keep)
        next_real = 2.0 * image_real - previous_real
        if previous_imag is None:
            next_imag = 2.0 * image_imag
        else:
            next_imag = 2.0 * image_imag - previous_imag
        previous_real, previous_imag = current_real, current_imag
        current_real, current_imag = next_real, next_imag
        locals_list.append(jnp.sum(start * current_real, axis=1) / R)
        traces.append(jnp.sum(start * current_real, axis=(0, 2, 3)) / (2 * LX * LY))
    return jnp.stack(locals_list), jnp.stack(traces)
```

```python
import functools

import jax
import jax.numpy as jnp
from jax import lax
from jax.experimental import pallas as pl
from jax.experimental.pallas import tpu as pltpu
from jax.sharding import PartitionSpec as P

BLOCK = 128
R = 16
TERMS = 4
HALO = 4
BLOCKS = 4
LANES = BLOCK * (BLOCKS + 1)
OWN = BLOCK * BLOCKS
WIDTH_X = 8
ROWS_X = WIDTH_X + 2 * HALO
SLOT = 2 * WIDTH_X * R
EDGE = SLOT
SITE_EDGE = SLOT + 16
SLOT_ROWS = SLOT + 32
HALF = 2 * HALO * R
PLANES = HALF + 16
MESSAGE = HALF + 16 + 4 * 2 * HALO

HOP_NEXT = 0.3
TWIST_COS = 0.4535961214255773
TWIST_SIN = 0.8912073600614354
SPREAD = 6.5
COS = HOP_NEXT * TWIST_COS
SIN = HOP_NEXT * TWIST_SIN
F32 = jnp.float32
BF16 = jnp.bfloat16


def site_planes(onsite, keep):
    high = onsite.astype(BF16).astype(F32)
    rest = onsite - high
    middle = rest.astype(BF16).astype(F32)
    low = (rest - middle).astype(BF16).astype(F32)
    return high, middle, low, keep


def lane_index(rows, lanes):
    return lax.broadcasted_iota(jnp.int32, (rows, lanes), 1)


def pack_kernel(columns, plan, stored, disorder, vacancy, out, turned, where_to):
    me = lax.axis_index("gy")
    first = me * BLOCKS

    def find(k, carry):
        held = plan[k] - first
        spot = jnp.where((held >= 0) & (held < BLOCKS), held, BLOCKS)
        where_to[spot] = k
        return carry

    lax.fori_loop(0, BLOCKS * columns, find, 0, unroll=8)

    for b in range(BLOCKS):
        block = stored[:, :, :, b * BLOCK : (b + 1) * BLOCK]
        turned[b] = block.reshape(2 * R * WIDTH_X, BLOCK).astype(F32)
    lane = lane_index(8, BLOCK)
    edges = [[jnp.zeros((8, BLOCK), F32) for _ in range(2)] for _ in range(BLOCKS)]
    slots = [where_to[b] // BLOCKS for b in range(BLOCKS)]
    for s in range(2):
        for x in range(WIDTH_X):
            q = s * WIDTH_X + x
            for b in range(BLOCKS):
                parts = []
                for h in range(2):
                    base = s * R * WIDTH_X + h * 8 * WIDTH_X + x
                    rows = turned[b, pl.ds(base, 8, stride=WIDTH_X), :]
                    parts.append(rows)
                    moved = pltpu.roll(rows, (8 * q + 4) % BLOCK, 1)
                    edges[b][h] = jnp.where(lane // 8 == q, moved, edges[b][h])
                both = jnp.concatenate(parts, axis=0).astype(BF16)
                out[slots[b], q * R : (q + 1) * R, :] = both
    last_half = lane_index(R, BLOCK) % 8 < 4
    for b in range(BLOCKS):
        spot = where_to[b]
        edge = jnp.concatenate(edges[b], axis=0)

        @pl.when(spot % BLOCKS == BLOCKS - 1)
        def _():
            slot = ((spot + 1) // BLOCKS) % columns
            old = out[slot, EDGE : EDGE + R, :].astype(F32)
            out[slot, EDGE : EDGE + R, :] = jnp.where(last_half, edge, old).astype(BF16)

        @pl.when(spot % BLOCKS == 0)
        def _():
            slot = (spot // BLOCKS + columns - 1) % columns
            old = out[slot, EDGE : EDGE + R, :].astype(F32)
            out[slot, EDGE : EDGE + R, :] = jnp.where(last_half, old, edge).astype(BF16)

    lane16 = lane_index(R, BLOCK)
    ends = []
    for ref in (disorder, vacancy):
        low = ref[:, :, 0:BLOCK].reshape(R, BLOCK).astype(F32)
        high = ref[:, :, OWN - BLOCK : OWN].reshape(R, BLOCK).astype(F32)
        ends.append(jnp.where(lane16 < BLOCK // 2, low, high))
    sites = jnp.zeros((R, BLOCK), F32)
    for p, plane in enumerate(site_planes(ends[0], ends[1])):
        sites = jnp.where(lane16 // 8 == p, pltpu.roll(plane, 8 * p + 4, 1), sites)
    sites = sites.astype(BF16)
    out[(me + 1) % columns, SITE_EDGE : SITE_EDGE + R, :] = sites
    out[(me + columns - 1) % columns, SITE_EDGE : SITE_EDGE + R, :] = sites


def edge_tiles(columns, plan, received):
    me = lax.axis_index("gy")
    total = BLOCKS * columns
    left = plan[(me * BLOCKS + total - 1) % total] // BLOCKS
    right = plan[(me * BLOCKS + BLOCKS) % total] // BLOCKS
    last_half = lane_index(R, BLOCK) % 8 < 4
    tile = jnp.where(
        last_half,
        received[left, EDGE : EDGE + R, :].astype(F32),
        received[right, EDGE : EDGE + R, :].astype(F32),
    )
    low = (me + columns - 1) % columns
    high = (me + 1) % columns
    sites = jnp.where(
        last_half,
        received[low, SITE_EDGE : SITE_EDGE + R, :].astype(F32),
        received[high, SITE_EDGE : SITE_EDGE + R, :].astype(F32),
    )
    return tile, sites


def arrange_kernel(columns, plan, received, disorder, vacancy, low_out, high_out, rows):
    me = lax.axis_index("gy")
    for b in range(BLOCKS):
        slot = plan[me * BLOCKS + b] // BLOCKS
        lanes = slice(b * BLOCK, (b + 1) * BLOCK)
        for s in range(2):
            base = s * WIDTH_X * R
            size = HALO * R
            low_out[s * size : (s + 1) * size, lanes] = received[slot, base : base + size, :]
            high_out[s * size : (s + 1) * size, lanes] = received[
                slot, base + (WIDTH_X - HALO) * R : base + WIDTH_X * R, :
            ]
    tile, sites = edge_tiles(columns, plan, received)
    for out in (low_out, high_out):
        out[HALF : HALF + R, 0:BLOCK] = tile.astype(BF16)
        out[HALF : HALF + R, BLOCK : 2 * BLOCK] = sites.astype(BF16)
        out[HALF : HALF + R, 2 * BLOCK : OWN] = jnp.zeros((R, OWN - 2 * BLOCK), BF16)
    for s in range(2):
        for p, plane in enumerate(site_planes(disorder[s], vacancy[s].astype(F32))):
            rows[0, p * 8 + s * HALO : p * 8 + (s + 1) * HALO, :] = plane[0:HALO]
            rows[1, p * 8 + s * HALO : p * 8 + (s + 1) * HALO, :] = plane[WIDTH_X - HALO :]
    low_out[PLANES:MESSAGE, :] = rows[0].astype(BF16)
    high_out[PLANES:MESSAGE, :] = rows[1].astype(BF16)


def shift_up(field):
    return pltpu.roll(field, LANES - 1, 1)


def shift_down(field):
    return pltpu.roll(field, 1, 1)


def chebyshev_kernel(
    columns, plan, received, below, above, disorder, vacancy,
    local_out, trace_out,
    level, keep, factor, start, real1, imag1, real2, imag2, real3, imag3, sums,
):
    me = lax.axis_index("gy")
    tile, sites = edge_tiles(columns, plan, received)
    lane8 = lane_index(8, BLOCK)
    in_halo = (lane8 < HALO) | (lane8 >= BLOCK - HALO)

    def unpack_sites(s, rows, onsite, kept, source, x_of):
        side_level = jnp.zeros((8, BLOCK), F32)
        for p in range(3):
            side_level = side_level + pltpu.roll(source, BLOCK - 4 - 8 * p, 1)
        side_keep = pltpu.roll(source, BLOCK - 4 - 8 * 3, 1)
        side_level = jnp.where(in_halo, side_level, 0.0)
        side_keep = jnp.where(in_halo, side_keep, 0.0)
        for i, row in enumerate(rows):
            j = x_of(i)
            lev = jnp.concatenate([onsite[i : i + 1], side_level[j : j + 1]], axis=1)
            kep = jnp.concatenate([kept[i : i + 1], side_keep[j : j + 1]], axis=1)
            level[s, row] = jnp.broadcast_to(lev, (8, LANES))
            kep = jnp.broadcast_to(kep, (8, LANES))
            keep[s, row] = kep
            factor[s, row] = kep * (1.0 / SPREAD)

    for s in range(2):
        unpack_sites(
            s, range(HALO, HALO + WIDTH_X), disorder[s], vacancy[s].astype(F32),
            sites[s * 8 : (s + 1) * 8], lambda i: i,
        )
    for ref, rows, shift in (
        (below, range(0, HALO), WIDTH_X - HALO),
        (above, range(HALO + WIDTH_X, ROWS_X), 0),
    ):
        planes = [ref[PLANES + p * 8 : PLANES + (p + 1) * 8, :].astype(F32) for p in range(4)]
        onsite = planes[0] + planes[1] + planes[2]
        far = ref[HALF : HALF + R, BLOCK : 2 * BLOCK].astype(F32)
        for s in range(2):
            part = slice(s * HALO, (s + 1) * HALO)
            unpack_sites(
                s, rows, onsite[part], planes[3][part], far[s * 8 : (s + 1) * 8],
                lambda i, shift=shift: i + shift,
            )

    def put_start(s, row, lanes, value):
        for h in range(2):
            start[s, row, h * 8 : (h + 1) * 8, lanes] = (
                value[h * 8 : (h + 1) * 8] * keep[s, row, :, lanes]
            )

    side = slice(OWN, LANES)
    for b in range(BLOCKS):
        slot = plan[me * BLOCKS + b] // BLOCKS
        for s in range(2):
            for x in range(WIDTH_X):
                q = s * WIDTH_X + x
                value = received[slot, q * R : (q + 1) * R, :].astype(F32)
                put_start(s, HALO + x, slice(b * BLOCK, (b + 1) * BLOCK), value)
    for s in range(2):
        for x in range(WIDTH_X):
            q = s * WIDTH_X + x
            put_start(s, HALO + x, side, pltpu.roll(tile, (BLOCK - 4 - 8 * q) % BLOCK, 1))
    for ref, base, shift in ((below, 0, WIDTH_X - HALO), (above, HALO + WIDTH_X, 0)):
        far = ref[HALF : HALF + R, 0:BLOCK].astype(F32)
        for s in range(2):
            for i in range(HALO):
                row = base + i
                index = (s * HALO + i) * R
                put_start(s, row, slice(0, OWN), ref[index : index + R, :].astype(F32))
                q = s * WIDTH_X + shift + i
                put_start(s, row, side, pltpu.roll(far, (BLOCK - 4 - 8 * q) % BLOCK, 1))

    def hamilton(real, imag, s, row, h, want_imag):
        part = slice(h * 8, (h + 1) * 8)
        sine = SIN if s == 0 else -SIN

        def get(ref, sub, r):
            return ref[sub, r, part, :]

        r_m, r_0, r_p = (get(real, s, row + d) for d in (-1, 0, 1))
        o_0 = get(real, 1 - s, row)
        o_s = get(real, 1 - s, row - 1 if s == 0 else row + 1)
        lev = level[s, row]
        if imag is None:
            out_r = COS * (r_p + r_m) + lev * r_0 - (o_0 + o_s)
            g0 = COS * (r_m + r_0)
            g1 = COS * (r_0 + r_p)
        else:
            i_m, i_0, i_p = (get(imag, s, row + d) for d in (-1, 0, 1))
            out_r = COS * (r_p + r_m) - sine * (i_p - i_m) + lev * r_0 - (o_0 + o_s)
            g0 = COS * (r_m + r_0) - sine * (i_m - i_0)
            g1 = COS * (r_0 + r_p) - sine * (i_0 - i_p)
        if s == 0:
            g1 = g1 - o_0
        else:
            g0 = g0 - o_0
        out_r = out_r + shift_up(g0) + shift_down(g1)
        if not want_imag:
            return out_r, None
        out_i = sine * (r_p - r_m)
        g0 = sine * (r_m - r_0)
        g1 = sine * (r_0 - r_p)
        if imag is not None:
            o_0 = get(imag, 1 - s, row)
            o_s = get(imag, 1 - s, row - 1 if s == 0 else row + 1)
            out_i = out_i + COS * (i_p + i_m) + lev * i_0 - (o_0 + o_s)
            g0 = g0 + COS * (i_m + i_0)
            g1 = g1 + COS * (i_0 + i_p)
            if s == 0:
                g1 = g1 - o_0
            else:
                g0 = g0 - o_0
        out_i = out_i + shift_up(g0) + shift_down(g1)
        return out_r, out_i

    fields = [(start, None), (real1, imag1), (real2, imag2), (real3, imag3)]

    for term in range(1, TERMS):
        real, imag = fields[term - 1]
        to_real, to_imag = fields[term]

        def body(row, carry, term=term, real=real, imag=imag, to_real=to_real, to_imag=to_imag):
            for h in range(2):
                part = slice(h * 8, (h + 1) * 8)
                for s in range(2):
                    out_r, out_i = hamilton(real, imag, s, row, h, True)
                    scale = factor[s, row]
                    if term == 1:
                        out_r, out_i = out_r * scale, out_i * scale
                    else:
                        scale = scale + scale
                        old_r, old_i = fields[term - 2]
                        out_r = out_r * scale - old_r[s, row, part, :]
                        out_i = out_i * scale
                        if old_i is not None:
                            out_i = out_i - old_i[s, row, part, :]
                    to_real[s, row, part, :] = out_r
                    to_imag[s, row, part, :] = out_i
            return carry

        lax.fori_loop(term, ROWS_X - term, body, 0)

    sums[...] = jnp.zeros_like(sums)

    def finish(x, carry):
        row = x + HALO
        own = slice(0, OWN)
        for s in range(2):
            totals = [None] * TERMS
            for h in range(2):
                part = slice(h * 8, (h + 1) * 8)
                v0 = start[s, row, part, own]
                out_r, _ = hamilton(real3, imag3, s, row, h, False)
                scale = factor[s, row]
                v4 = out_r * (scale + scale) - real2[s, row, part, :]
                values = [ref[s, row, part, own] for ref in (real1, real2, real3)]
                values.append(v4[:, own])
                for n, value in enumerate(values):
                    product = v0 * value
                    totals[n] = product if h == 0 else totals[n] + product
                    lanes = product[:, 0:BLOCK]
                    for b in range(1, BLOCKS):
                        lanes = lanes + product[:, b * BLOCK : (b + 1) * BLOCK]
                    sums[n * R + h * 8 : n * R + (h + 1) * 8, :] += lanes
            for n in range(TERMS):
                local_out[n, s, pl.ds(x, 1), :] = (
                    jnp.sum(totals[n], axis=0, keepdims=True) * (1.0 / R)
                )
        return carry

    lax.fori_loop(0, WIDTH_X, finish, 0)
    trace_out[...] = lax.dot_general(
        jnp.ones(trace_out.shape[:1] + (BLOCK,), F32), sums[...],
        (((1,), (1,)), ((), ())),
        precision=lax.Precision.HIGHEST, preferred_element_type=F32,
    )


def local(stored_vectors, disorder, vacancy, plan):
    columns = lax.axis_size("gy")
    rows = lax.axis_size("gx")
    devices = rows * columns
    smem = pl.BlockSpec(memory_space=pltpu.SMEM)
    vmem = pl.BlockSpec(memory_space=pltpu.VMEM)
    params = pltpu.CompilerParams(vmem_limit_bytes=48 * 1024 * 1024)

    outgoing = pl.pallas_call(
        functools.partial(pack_kernel, columns),
        out_shape=jax.ShapeDtypeStruct((columns, SLOT_ROWS, BLOCK), BF16),
        in_specs=[smem, vmem, vmem, vmem],
        out_specs=vmem,
        scratch_shapes=[
            pltpu.VMEM((BLOCKS, 2 * R * WIDTH_X, BLOCK), F32),
            pltpu.SMEM((BLOCKS + 1,), jnp.int32),
        ],
        compiler_params=params,
        name="pack",
    )(plan, stored_vectors, disorder, vacancy)
    received = lax.all_to_all(outgoing, "gy", split_axis=0, concat_axis=0, tiled=True)

    message = jax.ShapeDtypeStruct((MESSAGE, OWN), BF16)
    low_rows, high_rows = pl.pallas_call(
        functools.partial(arrange_kernel, columns),
        out_shape=(message, message),
        in_specs=[smem, vmem, vmem, vmem],
        out_specs=(vmem, vmem),
        scratch_shapes=[pltpu.VMEM((2, 4 * 2 * HALO, OWN), F32)],
        compiler_params=params,
        name="arrange",
    )(plan, received, disorder, vacancy)
    up = [(i, (i + 1) % rows) for i in range(rows)]
    down = [(target, source) for source, target in up]
    below = lax.ppermute(high_rows, "gx", up)
    above = lax.ppermute(low_rows, "gx", down)

    site = pltpu.VMEM((2, ROWS_X, 8, LANES), F32)
    field = pltpu.VMEM((2, ROWS_X, R, LANES), F32)
    local_moments, partial = pl.pallas_call(
        functools.partial(chebyshev_kernel, columns),
        out_shape=(
            jax.ShapeDtypeStruct((TERMS, 2, WIDTH_X, OWN), F32),
            jax.ShapeDtypeStruct((devices, TERMS * R), F32),
        ),
        in_specs=[smem, vmem, vmem, vmem, vmem, vmem],
        out_specs=(vmem, vmem),
        scratch_shapes=[site, site, site] + [field] * 7 + [pltpu.VMEM((TERMS * R, BLOCK), F32)],
        compiler_params=params,
        name="chebyshev",
    )(plan, received, below, above, disorder, vacancy)

    shared = lax.all_to_all(partial, ("gx", "gy"), split_axis=0, concat_axis=0, tiled=True)
    sites = 2 * WIDTH_X * rows * OWN * columns
    trace = jnp.sum(shared, axis=0).reshape(TERMS, R) * (1.0 / sites)
    return local_moments, trace


def solution(mesh):
    placed = (P(None, None, "gx", "gy"), P(None, "gx", "gy"), P(None, "gx", "gy"), P())
    return jax.shard_map(
        local, mesh=mesh, in_specs=placed,
        out_specs=(P(None, None, "gx", "gy"), P()), check_vma=False,
    )
```

```python
import functools

import jax
import jax.numpy as jnp
from jax import lax
from jax.experimental import pallas as pl
from jax.experimental.pallas import tpu as pltpu
from jax.sharding import PartitionSpec as P

BLOCK = 128
R = 16
TERMS = 4
HALO = 4
BLOCKS = 4
LANES = BLOCK * (BLOCKS + 1)
OWN = BLOCK * BLOCKS
WIDTH_X = 8
ROWS_X = WIDTH_X + 2 * HALO
SLOT = 2 * WIDTH_X * R
EDGE = SLOT
SITE_EDGE = SLOT + 16
SLOT_ROWS = SLOT + 32
HALF = 2 * HALO * R
PLANES = HALF + 16
MESSAGE = HALF + 16 + 4 * 2 * HALO

HOP_NEXT = 0.3
TWIST_COS = 0.4535961214255773
TWIST_SIN = 0.8912073600614354
SPREAD = 6.5
COS = HOP_NEXT * TWIST_COS
SIN = HOP_NEXT * TWIST_SIN
F32 = jnp.float32
BF16 = jnp.bfloat16


def site_planes(onsite, keep):
    high = onsite.astype(BF16).astype(F32)
    rest = onsite - high
    middle = rest.astype(BF16).astype(F32)
    low = (rest - middle).astype(BF16).astype(F32)
    return high, middle, low, keep


def lane_index(rows, lanes):
    return lax.broadcasted_iota(jnp.int32, (rows, lanes), 1)


def pack_kernel(
    columns, plan_hbm, stored_hbm, disorder_hbm, vacancy_hbm, out,
    plan, stored, disorder, vacancy, turned, where_to, arrived,
):
    copies = [
        pltpu.make_async_copy(source, target, arrived.at[i])
        for i, (source, target) in enumerate(
            ((plan_hbm, plan), (stored_hbm, stored), (disorder_hbm, disorder), (vacancy_hbm, vacancy))
        )
    ]
    for copy in copies:
        copy.start()
    me = lax.axis_index("gy")
    first = me * BLOCKS
    copies[0].wait()

    def find(k, carry):
        held = plan[k] - first
        spot = jnp.where((held >= 0) & (held < BLOCKS), held, BLOCKS)
        where_to[spot] = k
        return carry

    lax.fori_loop(0, BLOCKS * columns, find, 0, unroll=8)

    copies[1].wait()
    for b in range(BLOCKS):
        block = stored[:, :, :, b * BLOCK : (b + 1) * BLOCK]
        turned[b] = block.reshape(2 * R * WIDTH_X, BLOCK).astype(F32)
    lane = lane_index(8, BLOCK)
    edges = [[jnp.zeros((8, BLOCK), F32) for _ in range(2)] for _ in range(BLOCKS)]
    slots = [where_to[b] // BLOCKS for b in range(BLOCKS)]
    for s in range(2):
        for x in range(WIDTH_X):
            q = s * WIDTH_X + x
            for b in range(BLOCKS):
                parts = []
                for h in range(2):
                    base = s * R * WIDTH_X + h * 8 * WIDTH_X + x
                    rows = turned[b, pl.ds(base, 8, stride=WIDTH_X), :]
                    parts.append(rows)
                    moved = pltpu.roll(rows, (8 * q + 4) % BLOCK, 1)
                    edges[b][h] = jnp.where(lane // 8 == q, moved, edges[b][h])
                both = jnp.concatenate(parts, axis=0).astype(BF16)
                out[slots[b], q * R : (q + 1) * R, :] = both
    last_half = lane_index(R, BLOCK) % 8 < 4
    for b in range(BLOCKS):
        spot = where_to[b]
        edge = jnp.concatenate(edges[b], axis=0)

        @pl.when(spot % BLOCKS == BLOCKS - 1)
        def _():
            slot = ((spot + 1) // BLOCKS) % columns
            old = out[slot, EDGE : EDGE + R, :].astype(F32)
            out[slot, EDGE : EDGE + R, :] = jnp.where(last_half, edge, old).astype(BF16)

        @pl.when(spot % BLOCKS == 0)
        def _():
            slot = (spot // BLOCKS + columns - 1) % columns
            old = out[slot, EDGE : EDGE + R, :].astype(F32)
            out[slot, EDGE : EDGE + R, :] = jnp.where(last_half, old, edge).astype(BF16)

    copies[2].wait()
    copies[3].wait()
    lane16 = lane_index(R, BLOCK)
    ends = []
    for ref in (disorder, vacancy):
        low = ref[:, :, 0:BLOCK].reshape(R, BLOCK).astype(F32)
        high = ref[:, :, OWN - BLOCK : OWN].reshape(R, BLOCK).astype(F32)
        ends.append(jnp.where(lane16 < BLOCK // 2, low, high))
    sites = jnp.zeros((R, BLOCK), F32)
    for p, plane in enumerate(site_planes(ends[0], ends[1])):
        sites = jnp.where(lane16 // 8 == p, pltpu.roll(plane, 8 * p + 4, 1), sites)
    sites = sites.astype(BF16)
    out[(me + 1) % columns, SITE_EDGE : SITE_EDGE + R, :] = sites
    out[(me + columns - 1) % columns, SITE_EDGE : SITE_EDGE + R, :] = sites


def edge_tiles(columns, plan, received):
    me = lax.axis_index("gy")
    total = BLOCKS * columns
    left = plan[(me * BLOCKS + total - 1) % total] // BLOCKS
    right = plan[(me * BLOCKS + BLOCKS) % total] // BLOCKS
    last_half = lane_index(R, BLOCK) % 8 < 4
    tile = jnp.where(
        last_half,
        received[left, EDGE : EDGE + R, :].astype(F32),
        received[right, EDGE : EDGE + R, :].astype(F32),
    )
    low = (me + columns - 1) % columns
    high = (me + 1) % columns
    sites = jnp.where(
        last_half,
        received[low, SITE_EDGE : SITE_EDGE + R, :].astype(F32),
        received[high, SITE_EDGE : SITE_EDGE + R, :].astype(F32),
    )
    return tile, sites


def arrange_kernel(columns, plan, received, disorder, vacancy, low_out, high_out, rows):
    me = lax.axis_index("gy")
    for b in range(BLOCKS):
        slot = plan[me * BLOCKS + b] // BLOCKS
        lanes = slice(b * BLOCK, (b + 1) * BLOCK)
        for s in range(2):
            base = s * WIDTH_X * R
            size = HALO * R
            low_out[s * size : (s + 1) * size, lanes] = received[slot, base : base + size, :]
            high_out[s * size : (s + 1) * size, lanes] = received[
                slot, base + (WIDTH_X - HALO) * R : base + WIDTH_X * R, :
            ]
    tile, sites = edge_tiles(columns, plan, received)
    for out in (low_out, high_out):
        out[HALF : HALF + R, 0:BLOCK] = tile.astype(BF16)
        out[HALF : HALF + R, BLOCK : 2 * BLOCK] = sites.astype(BF16)
        out[HALF : HALF + R, 2 * BLOCK : OWN] = jnp.zeros((R, OWN - 2 * BLOCK), BF16)
    for s in range(2):
        for p, plane in enumerate(site_planes(disorder[s], vacancy[s].astype(F32))):
            rows[0, p * 8 + s * HALO : p * 8 + (s + 1) * HALO, :] = plane[0:HALO]
            rows[1, p * 8 + s * HALO : p * 8 + (s + 1) * HALO, :] = plane[WIDTH_X - HALO :]
    low_out[PLANES:MESSAGE, :] = rows[0].astype(BF16)
    high_out[PLANES:MESSAGE, :] = rows[1].astype(BF16)


def fill_sites(level, factor, s, rows, onsite, kept, source, first):
    lane = lane_index(8, BLOCK)
    in_halo = (lane < HALO) | (lane >= BLOCK - HALO)
    side_level = jnp.zeros((8, BLOCK), F32)
    for p in range(3):
        side_level = side_level + pltpu.roll(source, BLOCK - 4 - 8 * p, 1)
    side_keep = pltpu.roll(source, BLOCK - 4 - 8 * 3, 1)
    side_level = jnp.where(in_halo, side_level, 0.0)
    side_keep = jnp.where(in_halo, side_keep, 0.0)
    kept_rows = []
    for i, row in enumerate(rows):
        j = first + i
        lev = jnp.concatenate([onsite[i : i + 1], side_level[j : j + 1]], axis=1)
        kep = jnp.concatenate([kept[i : i + 1], side_keep[j : j + 1]], axis=1)
        level[s, row] = jnp.broadcast_to(lev, (8, LANES))
        kep = jnp.broadcast_to(kep, (8, LANES))
        factor[s, row] = kep * (1.0 / SPREAD)
        kept_rows.append(kep)
    return kept_rows


def hamilton(level, real, imag, s, row, h, want_imag):
    part = slice(h * 8, (h + 1) * 8)
    sine = SIN if s == 0 else -SIN
    aside = row - 1 if s == 0 else row + 1
    r_m, r_0, r_p = (real[s, row + d, part, :] for d in (-1, 0, 1))
    o_0 = real[1 - s, row, part, :]
    near = o_0 + real[1 - s, aside, part, :]
    lev = level[s, row]
    out_r = COS * (r_p + r_m) + lev * r_0 - near
    g0 = COS * (r_m + r_0)
    g1 = COS * (r_0 + r_p)
    if imag is not None:
        i_m, i_0, i_p = (imag[s, row + d, part, :] for d in (-1, 0, 1))
        out_r = out_r - sine * (i_p - i_m)
        g0 = g0 - sine * (i_m - i_0)
        g1 = g1 - sine * (i_0 - i_p)
    if s == 0:
        g1 = g1 - o_0
    else:
        g0 = g0 - o_0
    out_r = out_r + pltpu.roll(g0, LANES - 1, 1) + pltpu.roll(g1, 1, 1)
    if not want_imag:
        return out_r, None
    out_i = sine * (r_p - r_m)
    g0 = sine * (r_m - r_0)
    g1 = sine * (r_0 - r_p)
    if imag is not None:
        o_0 = imag[1 - s, row, part, :]
        near = o_0 + imag[1 - s, aside, part, :]
        out_i = out_i + COS * (i_p + i_m) + lev * i_0 - near
        g0 = g0 + COS * (i_m + i_0)
        g1 = g1 + COS * (i_0 + i_p)
        if s == 0:
            g1 = g1 - o_0
        else:
            g0 = g0 - o_0
    out_i = out_i + pltpu.roll(g0, LANES - 1, 1) + pltpu.roll(g1, 1, 1)
    return out_r, out_i


def advance(term, level, factor, old, now, new, row):
    for h in range(2):
        part = slice(h * 8, (h + 1) * 8)
        for s in range(2):
            out_r, out_i = hamilton(level, now[0], now[1], s, row, h, True)
            scale = factor[s, row]
            if term == 1:
                out_r, out_i = out_r * scale, out_i * scale
            else:
                scale = scale + scale
                out_r = out_r * scale - old[0][s, row, part, :]
                out_i = out_i * scale
                if old[1] is not None:
                    out_i = out_i - old[1][s, row, part, :]
            new[0][s, row, part, :] = out_r
            new[1][s, row, part, :] = out_i


def fold(product):
    lanes = product[:, 0:BLOCK]
    for b in range(1, BLOCKS):
        lanes = lanes + product[:, b * BLOCK : (b + 1) * BLOCK]
    return lanes


def trace_row(start, first, second, row, sums):
    own = slice(0, OWN)
    sums = list(sums)
    for h in range(2):
        part = slice(h * 8, (h + 1) * 8)
        for s in range(2):
            v0 = start[s, row, part, own]
            r1 = first[0][s, row, part, own]
            i1 = first[1][s, row, part, own]
            r2 = second[0][s, row, part, own]
            i2 = second[1][s, row, part, own]
            terms = (v0 * v0, v0 * r1, v0 * r2, r1 * r2 + i1 * i2, r2 * r2 + i2 * i2)
            for n, term in enumerate(terms):
                sums[n * 2 + h] = sums[n * 2 + h] + fold(term)
    return tuple(sums)


SUMS = 5


class Rows:
    def __init__(self, ref, first):
        self.ref = ref
        self.first = first

    def __getitem__(self, index):
        s, row, part, lanes = index
        return self.ref[s, row - self.first, part, lanes]

    def __setitem__(self, index, value):
        s, row, part, lanes = index
        self.ref[s, row - self.first, part, lanes] = value


def interior_kernel(
    columns, plan, received, disorder, vacancy,
    level, factor, start, real1, imag1, real2, imag2, sums,
):
    real2, imag2 = Rows(real2, 2), Rows(imag2, 2)
    me = lax.axis_index("gy")
    tile, sites = edge_tiles(columns, plan, received)
    slots = [plan[me * BLOCKS + b] // BLOCKS for b in range(BLOCKS)]
    for s in range(2):
        kept = fill_sites(
            level, factor, s, range(HALO, HALO + WIDTH_X), disorder[s],
            vacancy[s].astype(F32), sites[s * 8 : (s + 1) * 8], 0,
        )
        for x in range(WIDTH_X):
            q = s * WIDTH_X + x
            pieces = [received[slots[b], q * R : (q + 1) * R, :].astype(F32) for b in range(BLOCKS)]
            pieces.append(pltpu.roll(tile, (BLOCK - 4 - 8 * q) % BLOCK, 1))
            value = jnp.concatenate(pieces, axis=1)
            for h in range(2):
                part = slice(h * 8, (h + 1) * 8)
                start[s, HALO + x, part, :] = value[part] * kept[x]

    def one(row, carry):
        advance(1, level, factor, None, (start, None), (real1, imag1), row)
        return carry

    lax.fori_loop(HALO + 1, HALO + WIDTH_X - 1, one, 0)

    def two(row, carry):
        advance(2, level, factor, (start, None), (real1, imag1), (real2, imag2), row)
        return trace_row(start, (real1, imag1), (real2, imag2), row, carry)

    zero = jnp.zeros((8, BLOCK), F32)
    totals = lax.fori_loop(HALO + 2, HALO + WIDTH_X - 2, two, (zero,) * (2 * SUMS))
    for i, total in enumerate(totals):
        sums[i * 8 : (i + 1) * 8, :] = total


def border_kernel(
    below, above, level_in, factor_in, start_in, real1_in, imag1_in, real2_in, imag2_in, sums_in,
    level, factor, start, real1, imag1, real2, imag2, trace_out, sites_out, start_out,
):
    real2, imag2 = Rows(real2, 2), Rows(imag2, 2)
    for ref, base, shift in ((below, 0, WIDTH_X - HALO), (above, HALO + WIDTH_X, 0)):
        planes = [ref[PLANES + p * 8 : PLANES + (p + 1) * 8, :].astype(F32) for p in range(4)]
        onsite = planes[0] + planes[1] + planes[2]
        sites = ref[HALF : HALF + R, BLOCK : 2 * BLOCK].astype(F32)
        far = ref[HALF : HALF + R, 0:BLOCK].astype(F32)
        for s in range(2):
            some = slice(s * HALO, (s + 1) * HALO)
            kept = fill_sites(
                level, factor, s, range(base, base + HALO), onsite[some], planes[3][some],
                sites[s * 8 : (s + 1) * 8], shift,
            )
            for i in range(HALO):
                index = (s * HALO + i) * R
                q = s * WIDTH_X + shift + i
                side = pltpu.roll(far, (BLOCK - 4 - 8 * q) % BLOCK, 1)
                value = jnp.concatenate([ref[index : index + R, :].astype(F32), side], axis=1)
                for h in range(2):
                    part = slice(h * 8, (h + 1) * 8)
                    start[s, base + i, part, :] = value[part] * kept[i]

    def one(i, carry):
        for row in (i + 1, i + HALO + WIDTH_X - 1):
            advance(1, level, factor, None, (start, None), (real1, imag1), row)
        return carry

    lax.fori_loop(0, HALO, one, 0)

    def two(i, carry):
        for row in (i + 2, i + HALO + WIDTH_X - 2):
            advance(2, level, factor, (start, None), (real1, imag1), (real2, imag2), row)
        return carry

    lax.fori_loop(0, HALO, two, 0)
    for s in range(2):
        for row in range(ROWS_X):
            sites_out[0, s, row : row + 1, :] = level[s, row, 0:1, :]
            sites_out[1, s, row : row + 1, :] = factor[s, row, 0:1, :]
            start_out[s, row] = start[s, row].astype(BF16)
    totals = tuple(sums_in[i * 8 : (i + 1) * 8, :] for i in range(2 * SUMS))

    def trace(i, carry):
        for row in (i + HALO, i + HALO + WIDTH_X - 2):
            carry = trace_row(start, (real1, imag1), (real2, imag2), row, carry)
        return carry

    totals = lax.fori_loop(0, 2, trace, totals)
    norm, one_one, one_two, both, second = (
        jnp.concatenate(totals[2 * n : 2 * n + 2], axis=0) for n in range(SUMS)
    )
    moments = jnp.concatenate(
        [one_one, one_two, 2.0 * both - one_one, 2.0 * second - norm], axis=0
    )
    trace_out[...] = lax.dot_general(
        jnp.ones(trace_out.shape[:1] + (BLOCK,), F32), moments,
        (((1,), (1,)), ((), ())),
        precision=lax.Precision.HIGHEST, preferred_element_type=F32,
    )


def local_kernel(
    sites, kept_start, real2, imag2,
    local_out, level, factor, start, real1, imag1, real3, imag3,
):
    real2, imag2 = Rows(real2, 2), Rows(imag2, 2)
    for s in range(2):
        for row in range(2, ROWS_X - 2):
            level[s, row] = jnp.broadcast_to(sites[0, s, row : row + 1, :], (8, LANES))
            factor[s, row] = jnp.broadcast_to(sites[1, s, row : row + 1, :], (8, LANES))
            start[s, row] = kept_start[s, row].astype(F32)

    def one(row, carry):
        advance(1, level, factor, None, (start, None), (real1, imag1), row)
        return carry

    lax.fori_loop(3, ROWS_X - 3, one, 0)

    def three(row, carry):
        advance(3, level, factor, (real1, imag1), (real2, imag2), (real3, imag3), row)
        return carry

    lax.fori_loop(3, ROWS_X - 3, three, 0)

    def finish(x, carry):
        row = x + HALO
        own = slice(0, OWN)
        for s in range(2):
            totals = [None] * TERMS
            for h in range(2):
                part = slice(h * 8, (h + 1) * 8)
                v0 = start[s, row, part, own]
                out_r, _ = hamilton(level, real3, imag3, s, row, h, False)
                scale = factor[s, row]
                v4 = out_r * (scale + scale) - real2[s, row, part, :]
                values = [ref[s, row, part, own] for ref in (real1, real2, real3)]
                values.append(v4[:, own])
                for n, value in enumerate(values):
                    product = v0 * value
                    totals[n] = product if h == 0 else totals[n] + product
            for n in range(TERMS):
                local_out[n, s, pl.ds(x, 1), :] = (
                    jnp.sum(totals[n], axis=0, keepdims=True) * (1.0 / R)
                )
        return carry

    lax.fori_loop(0, WIDTH_X, finish, 0)


def total_kernel(sites, shared, out):
    total = jnp.sum(shared[...], axis=0, keepdims=True) * (1.0 / sites)
    for n in range(TERMS):
        out[n : n + 1, :] = total[:, n * R : (n + 1) * R]


def local(stored_vectors, disorder, vacancy, plan):
    columns = lax.axis_size("gy")
    rows = lax.axis_size("gx")
    devices = rows * columns
    smem = pl.BlockSpec(memory_space=pltpu.SMEM)
    vmem = pl.BlockSpec(memory_space=pltpu.VMEM)
    params = pltpu.CompilerParams(vmem_limit_bytes=8 * 1024 * 1024)

    hbm = pl.BlockSpec(memory_space=pltpu.HBM)
    outgoing = pl.pallas_call(
        functools.partial(pack_kernel, columns),
        out_shape=jax.ShapeDtypeStruct((columns, SLOT_ROWS, BLOCK), BF16),
        in_specs=[hbm] * 4,
        out_specs=vmem,
        scratch_shapes=[
            pltpu.SMEM(plan.shape, plan.dtype),
            pltpu.VMEM(stored_vectors.shape, stored_vectors.dtype),
            pltpu.VMEM(disorder.shape, disorder.dtype),
            pltpu.VMEM(vacancy.shape, vacancy.dtype),
            pltpu.VMEM((BLOCKS, 2 * R * WIDTH_X, BLOCK), F32),
            pltpu.SMEM((BLOCKS + 1,), jnp.int32),
            pltpu.SemaphoreType.DMA((4,)),
        ],
        compiler_params=pltpu.CompilerParams(vmem_limit_bytes=60 * 1024 * 1024),
        name="pack",
    )(plan, stored_vectors, disorder, vacancy)
    received = lax.all_to_all(outgoing, "gy", split_axis=0, concat_axis=0, tiled=True)

    message = jax.ShapeDtypeStruct((MESSAGE, OWN), BF16)
    low_rows, high_rows = pl.pallas_call(
        functools.partial(arrange_kernel, columns),
        out_shape=(message, message),
        in_specs=[smem, vmem, vmem, vmem],
        out_specs=(vmem, vmem),
        scratch_shapes=[pltpu.VMEM((2, 4 * 2 * HALO, OWN), F32)],
        compiler_params=params,
        name="arrange",
    )(plan, received, disorder, vacancy)
    up = [(i, (i + 1) % rows) for i in range(rows)]
    down = [(target, source) for source, target in up]
    below = lax.ppermute(high_rows, "gx", up)
    above = lax.ppermute(low_rows, "gx", down)

    site = jax.ShapeDtypeStruct((2, ROWS_X, 8, LANES), F32)
    field = jax.ShapeDtypeStruct((2, ROWS_X, R, LANES), F32)
    narrow = jax.ShapeDtypeStruct((2, ROWS_X - 4, R, LANES), F32)
    state = (site, site) + (field,) * 3 + (narrow,) * 2
    inner = pl.pallas_call(
        functools.partial(interior_kernel, columns),
        out_shape=state + (jax.ShapeDtypeStruct((2 * SUMS * 8, BLOCK), F32),),
        in_specs=[smem, vmem, vmem, vmem],
        out_specs=(vmem,) * 8,
        compiler_params=params,
        cost_estimate=pl.CostEstimate(flops=10**7, bytes_accessed=8 * 10**6, transcendentals=0),
        name="interior",
    )(plan, received, disorder, vacancy)
    outputs = pl.pallas_call(
        border_kernel,
        out_shape=state + (
            jax.ShapeDtypeStruct((devices, TERMS * R), F32),
            jax.ShapeDtypeStruct((2, 2, ROWS_X, LANES), F32),
            jax.ShapeDtypeStruct(field.shape, BF16),
        ),
        in_specs=[vmem] * 10,
        out_specs=(vmem,) * 10,
        input_output_aliases={2 + i: i for i in range(7)},
        compiler_params=params,
        name="border",
    )(below, above, *inner)
    real2, imag2, partial, sites, start = outputs[5:]
    shared = lax.all_to_all(partial, ("gx", "gy"), split_axis=0, concat_axis=0, tiled=True)
    local_moments = pl.pallas_call(
        local_kernel,
        out_shape=jax.ShapeDtypeStruct((TERMS, 2, WIDTH_X, OWN), F32),
        in_specs=[vmem] * 4,
        out_specs=vmem,
        scratch_shapes=[pltpu.VMEM(site.shape, F32)] * 2 + [pltpu.VMEM(field.shape, F32)] * 5,
        compiler_params=pltpu.CompilerParams(vmem_limit_bytes=16 * 1024 * 1024),
        cost_estimate=pl.CostEstimate(flops=10**7, bytes_accessed=8 * 10**6, transcendentals=0),
        name="local_moments",
    )(sites, start, real2, imag2)
    trace = pl.pallas_call(
        functools.partial(total_kernel, 2 * WIDTH_X * rows * OWN * columns),
        out_shape=jax.ShapeDtypeStruct((TERMS, R), F32),
        in_specs=[vmem],
        out_specs=vmem,
        compiler_params=params,
        name="total",
    )(shared)
    return local_moments, trace


def solution(mesh):
    placed = (P(None, None, "gx", "gy"), P(None, "gx", "gy"), P(None, "gx", "gy"), P())
    return jax.shard_map(
        local, mesh=mesh, in_specs=placed,
        out_specs=(P(None, None, "gx", "gy"), P()), check_vma=False,
    )
```

```python
import functools

import jax
import jax.numpy as jnp
from jax import lax
from jax.experimental import pallas as pl
from jax.experimental.pallas import tpu as pltpu
from jax.sharding import PartitionSpec as P

BLOCK = 128
R = 16
TERMS = 4
HALO = 4
BLOCKS = 4
LANES = BLOCK * (BLOCKS + 1)
OWN = BLOCK * BLOCKS
WIDTH_X = 8
ROWS_X = WIDTH_X + 2 * HALO
SLOT = 2 * WIDTH_X * R
EDGE = SLOT
SITE_EDGE = SLOT + 16
SLOT_ROWS = SLOT + 32
HALF = 2 * HALO * R
PLANES = HALF + 16
MESSAGE = HALF + 16 + 4 * 2 * HALO

HOP_NEXT = 0.3
TWIST_COS = 0.4535961214255773
TWIST_SIN = 0.8912073600614354
SPREAD = 6.5
COS = HOP_NEXT * TWIST_COS
SIN = HOP_NEXT * TWIST_SIN
F32 = jnp.float32
BF16 = jnp.bfloat16


def site_planes(onsite, keep):
    high = onsite.astype(BF16).astype(F32)
    rest = onsite - high
    middle = rest.astype(BF16).astype(F32)
    low = (rest - middle).astype(BF16).astype(F32)
    return high, middle, low, keep


def lane_index(rows, lanes):
    return lax.broadcasted_iota(jnp.int32, (rows, lanes), 1)


def pack_kernel(
    columns, plan_hbm, stored_hbm, disorder_hbm, vacancy_hbm, out,
    plan, stored, disorder, vacancy, turned, where_to, arrived,
):
    copies = [
        pltpu.make_async_copy(source, target, arrived.at[i])
        for i, (source, target) in enumerate(
            ((plan_hbm, plan), (stored_hbm, stored), (disorder_hbm, disorder), (vacancy_hbm, vacancy))
        )
    ]
    for copy in copies:
        copy.start()
    me = lax.axis_index("gy")
    first = me * BLOCKS
    copies[0].wait()

    def find(k, carry):
        held = plan[k] - first
        spot = jnp.where((held >= 0) & (held < BLOCKS), held, BLOCKS)
        where_to[spot] = k
        return carry

    lax.fori_loop(0, BLOCKS * columns, find, 0, unroll=8)

    copies[1].wait()
    for b in range(BLOCKS):
        block = stored[:, :, :, b * BLOCK : (b + 1) * BLOCK]
        turned[b] = block.reshape(2 * R * WIDTH_X, BLOCK).astype(F32)
    lane = lane_index(8, BLOCK)
    edges = [[jnp.zeros((8, BLOCK), F32) for _ in range(2)] for _ in range(BLOCKS)]
    slots = [where_to[b] // BLOCKS for b in range(BLOCKS)]
    for s in range(2):
        for x in range(WIDTH_X):
            q = s * WIDTH_X + x
            for b in range(BLOCKS):
                parts = []
                for h in range(2):
                    base = s * R * WIDTH_X + h * 8 * WIDTH_X + x
                    rows = turned[b, pl.ds(base, 8, stride=WIDTH_X), :]
                    parts.append(rows)
                    moved = pltpu.roll(rows, (8 * q + 4) % BLOCK, 1)
                    edges[b][h] = jnp.where(lane // 8 == q, moved, edges[b][h])
                both = jnp.concatenate(parts, axis=0).astype(BF16)
                out[slots[b], q * R : (q + 1) * R, :] = both
    last_half = lane_index(R, BLOCK) % 8 < 4
    for b in range(BLOCKS):
        spot = where_to[b]
        edge = jnp.concatenate(edges[b], axis=0)

        @pl.when(spot % BLOCKS == BLOCKS - 1)
        def _():
            slot = ((spot + 1) // BLOCKS) % columns
            old = out[slot, EDGE : EDGE + R, :].astype(F32)
            out[slot, EDGE : EDGE + R, :] = jnp.where(last_half, edge, old).astype(BF16)

        @pl.when(spot % BLOCKS == 0)
        def _():
            slot = (spot // BLOCKS + columns - 1) % columns
            old = out[slot, EDGE : EDGE + R, :].astype(F32)
            out[slot, EDGE : EDGE + R, :] = jnp.where(last_half, old, edge).astype(BF16)

    copies[2].wait()
    copies[3].wait()
    lane16 = lane_index(R, BLOCK)
    ends = []
    for ref in (disorder, vacancy):
        low = ref[:, :, 0:BLOCK].reshape(R, BLOCK).astype(F32)
        high = ref[:, :, OWN - BLOCK : OWN].reshape(R, BLOCK).astype(F32)
        ends.append(jnp.where(lane16 < BLOCK // 2, low, high))
    sites = jnp.zeros((R, BLOCK), F32)
    for p, plane in enumerate(site_planes(ends[0], ends[1])):
        sites = jnp.where(lane16 // 8 == p, pltpu.roll(plane, 8 * p + 4, 1), sites)
    sites = sites.astype(BF16)
    out[(me + 1) % columns, SITE_EDGE : SITE_EDGE + R, :] = sites
    out[(me + columns - 1) % columns, SITE_EDGE : SITE_EDGE + R, :] = sites


def edge_tiles(columns, plan, received):
    me = lax.axis_index("gy")
    total = BLOCKS * columns
    left = plan[(me * BLOCKS + total - 1) % total] // BLOCKS
    right = plan[(me * BLOCKS + BLOCKS) % total] // BLOCKS
    last_half = lane_index(R, BLOCK) % 8 < 4
    tile = jnp.where(
        last_half,
        received[left, EDGE : EDGE + R, :].astype(F32),
        received[right, EDGE : EDGE + R, :].astype(F32),
    )
    low = (me + columns - 1) % columns
    high = (me + 1) % columns
    sites = jnp.where(
        last_half,
        received[low, SITE_EDGE : SITE_EDGE + R, :].astype(F32),
        received[high, SITE_EDGE : SITE_EDGE + R, :].astype(F32),
    )
    return tile, sites


def arrange_kernel(columns, plan, received, disorder, vacancy, low_out, high_out, rows):
    me = lax.axis_index("gy")
    for b in range(BLOCKS):
        slot = plan[me * BLOCKS + b] // BLOCKS
        lanes = slice(b * BLOCK, (b + 1) * BLOCK)
        for s in range(2):
            base = s * WIDTH_X * R
            size = HALO * R
            low_out[s * size : (s + 1) * size, lanes] = received[slot, base : base + size, :]
            high_out[s * size : (s + 1) * size, lanes] = received[
                slot, base + (WIDTH_X - HALO) * R : base + WIDTH_X * R, :
            ]
    tile, sites = edge_tiles(columns, plan, received)
    for out in (low_out, high_out):
        out[HALF : HALF + R, 0:BLOCK] = tile.astype(BF16)
        out[HALF : HALF + R, BLOCK : 2 * BLOCK] = sites.astype(BF16)
        out[HALF : HALF + R, 2 * BLOCK : OWN] = jnp.zeros((R, OWN - 2 * BLOCK), BF16)
    for s in range(2):
        for p, plane in enumerate(site_planes(disorder[s], vacancy[s].astype(F32))):
            rows[0, p * 8 + s * HALO : p * 8 + (s + 1) * HALO, :] = plane[0:HALO]
            rows[1, p * 8 + s * HALO : p * 8 + (s + 1) * HALO, :] = plane[WIDTH_X - HALO :]
    low_out[PLANES:MESSAGE, :] = rows[0].astype(BF16)
    high_out[PLANES:MESSAGE, :] = rows[1].astype(BF16)


def fill_sites(level, factor, s, rows, onsite, kept, source, first):
    lane = lane_index(8, BLOCK)
    in_halo = (lane < HALO) | (lane >= BLOCK - HALO)
    side_level = jnp.zeros((8, BLOCK), F32)
    for p in range(3):
        side_level = side_level + pltpu.roll(source, BLOCK - 4 - 8 * p, 1)
    side_keep = pltpu.roll(source, BLOCK - 4 - 8 * 3, 1)
    side_level = jnp.where(in_halo, side_level, 0.0)
    side_keep = jnp.where(in_halo, side_keep, 0.0)
    kept_rows = []
    for i, row in enumerate(rows):
        j = first + i
        lev = jnp.concatenate([onsite[i : i + 1], side_level[j : j + 1]], axis=1)
        kep = jnp.concatenate([kept[i : i + 1], side_keep[j : j + 1]], axis=1)
        level[s, row] = jnp.broadcast_to(lev * (1.0 / COS), (8, LANES))
        kep = jnp.broadcast_to(kep, (8, LANES))
        factor[s, row] = kep * (2.0 * COS / SPREAD)
        kept_rows.append(kep)
    return kept_rows


def span(level, factor, term, old, now, new, row, count=2):
    for h in range(2):
        part = slice(h * 8, (h + 1) * 8)
        near_rows = range(-1, count + 1)
        real = [{d: now[0][s, row + d, part, :] for d in near_rows} for s in range(2)]
        fields = [real]
        if now[1] is not None:
            fields.append([{d: now[1][s, row + d, part, :] for d in near_rows} for s in range(2)])
        others = [
            [{d: f[s][d] * (1.0 / COS) for d in near_rows} for s in range(2)] for f in fields
        ]
        for s in range(2):
            ratio = SIN / COS if s == 0 else -SIN / COS
            turn = [{d: f[s][d] * ratio for d in near_rows} for f in fields]
            if len(fields) == 1:
                ahead = [real[s], turn[0]]
                back = [real[s], {d: -turn[0][d] for d in near_rows}]
            else:
                imag = fields[1][s]
                ahead = [
                    {d: real[s][d] - turn[1][d] for d in near_rows},
                    {d: imag[d] + turn[0][d] for d in near_rows},
                ]
                back = [
                    {d: real[s][d] + turn[1][d] for d in near_rows},
                    {d: imag[d] - turn[0][d] for d in near_rows},
                ]
            for c in range(2):
                if new[c] is None:
                    continue
                joint = {d: ahead[c][d - 1] + back[c][d] for d in range(count + 1)}
                for d in range(count):
                    out = ahead[c][d + 1] + back[c][d - 1]
                    up, down = joint[d], joint[d + 1]
                    if c < len(fields):
                        other = others[c][1 - s]
                        aside = d - 1 if s == 0 else d + 1
                        out = out + level[s, row + d] * fields[c][s][d]
                        out = out - (other[d] + other[aside])
                        if s == 0:
                            down = down - other[d]
                        else:
                            up = up - other[d]
                    out = out + pltpu.roll(up, LANES - 1, 1) + pltpu.roll(down, 1, 1)
                    scale = factor[s, row + d]
                    out = out * (scale * 0.5 if term == 1 else scale)
                    if term > 1 and old[c] is not None:
                        out = out - old[c][s, row + d, part, :]
                    new[c][s, row + d, part, :] = out


def fold(product):
    lanes = product[:, 0:BLOCK]
    for b in range(1, BLOCKS):
        lanes = lanes + product[:, b * BLOCK : (b + 1) * BLOCK]
    return lanes


def trace_row(start, first, second, row, sums):
    own = slice(0, OWN)
    sums = list(sums)
    for h in range(2):
        part = slice(h * 8, (h + 1) * 8)
        for s in range(2):
            v0 = start[s, row, part, own]
            r1 = first[0][s, row, part, own]
            i1 = first[1][s, row, part, own]
            r2 = second[0][s, row, part, own]
            i2 = second[1][s, row, part, own]
            terms = (v0 * v0, v0 * r1, v0 * r2, r1 * r2 + i1 * i2, r2 * r2 + i2 * i2)
            for n, term in enumerate(terms):
                sums[n * 2 + h] = sums[n * 2 + h] + fold(term)
    return tuple(sums)


SUMS = 5


class Rows:
    def __init__(self, ref, first):
        self.ref = ref
        self.first = first

    def __getitem__(self, index):
        s, row, part, lanes = index
        return self.ref[s, row - self.first, part, lanes]

    def __setitem__(self, index, value):
        s, row, part, lanes = index
        self.ref[s, row - self.first, part, lanes] = value


def interior_kernel(
    columns, plan, received, disorder, vacancy,
    level, factor, start, real1, imag1, real2, imag2, sums,
):
    real2, imag2 = Rows(real2, HALO), Rows(imag2, HALO)
    me = lax.axis_index("gy")
    tile, sites = edge_tiles(columns, plan, received)
    slots = [plan[me * BLOCKS + b] // BLOCKS for b in range(BLOCKS)]
    for s in range(2):
        kept = fill_sites(
            level, factor, s, range(HALO, HALO + WIDTH_X), disorder[s],
            vacancy[s].astype(F32), sites[s * 8 : (s + 1) * 8], 0,
        )
        for x in range(WIDTH_X):
            q = s * WIDTH_X + x
            pieces = [received[slots[b], q * R : (q + 1) * R, :].astype(F32) for b in range(BLOCKS)]
            pieces.append(pltpu.roll(tile, (BLOCK - 4 - 8 * q) % BLOCK, 1))
            value = jnp.concatenate(pieces, axis=1)
            for h in range(2):
                part = slice(h * 8, (h + 1) * 8)
                start[s, HALO + x, part, :] = value[part] * kept[x]

    def one(i, carry):
        row = HALO + 1 + 2 * i
        span(level, factor, 1, None, (start, None), (real1, imag1), row)
        return carry

    lax.fori_loop(0, 3, one, 0)

    def two(i, carry):
        row = HALO + 2 + 2 * i
        span(level, factor, 2, (start, None), (real1, imag1), (real2, imag2), row)
        for d in range(2):
            carry = trace_row(start, (real1, imag1), (real2, imag2), row + d, carry)
        return carry

    zero = jnp.zeros((8, BLOCK), F32)
    totals = lax.fori_loop(0, 2, two, (zero,) * (2 * SUMS))
    for i, total in enumerate(totals):
        sums[i * 8 : (i + 1) * 8, :] = total


def border_kernel(
    below, above, level_in, factor_in, start_in, real1_in, imag1_in, real2_in, imag2_in, sums_in,
    level, factor, start, real1, imag1, real2, imag2, trace_out, sites_out, start_out,
):
    real2, imag2 = Rows(real2, HALO), Rows(imag2, HALO)
    for ref, base, shift in ((below, 0, WIDTH_X - HALO), (above, HALO + WIDTH_X, 0)):
        planes = [ref[PLANES + p * 8 : PLANES + (p + 1) * 8, :].astype(F32) for p in range(4)]
        onsite = planes[0] + planes[1] + planes[2]
        sites = ref[HALF : HALF + R, BLOCK : 2 * BLOCK].astype(F32)
        far = ref[HALF : HALF + R, 0:BLOCK].astype(F32)
        for s in range(2):
            some = slice(s * HALO, (s + 1) * HALO)
            kept = fill_sites(
                level, factor, s, range(base, base + HALO), onsite[some], planes[3][some],
                sites[s * 8 : (s + 1) * 8], shift,
            )
            for i in range(HALO):
                index = (s * HALO + i) * R
                q = s * WIDTH_X + shift + i
                side = pltpu.roll(far, (BLOCK - 4 - 8 * q) % BLOCK, 1)
                value = jnp.concatenate([ref[index : index + R, :].astype(F32), side], axis=1)
                for h in range(2):
                    part = slice(h * 8, (h + 1) * 8)
                    start[s, base + i, part, :] = value[part] * kept[i]

    for row in (HALO - 1, HALO + WIDTH_X - 1):
        span(level, factor, 1, None, (start, None), (real1, imag1), row)
    totals = tuple(sums_in[i * 8 : (i + 1) * 8, :] for i in range(2 * SUMS))
    for row in (HALO, HALO + WIDTH_X - 2):
        span(level, factor, 2, (start, None), (real1, imag1), (real2, imag2), row)
        for d in range(2):
            totals = trace_row(start, (real1, imag1), (real2, imag2), row + d, totals)
    norm, one_one, one_two, both, second = (
        jnp.concatenate(totals[2 * n : 2 * n + 2], axis=0) for n in range(SUMS)
    )
    moments = jnp.concatenate(
        [one_one, one_two, 2.0 * both - one_one, 2.0 * second - norm], axis=0
    )
    trace_out[...] = lax.dot_general(
        jnp.ones(trace_out.shape[:1] + (BLOCK,), F32), moments,
        (((1,), (1,)), ((), ())),
        precision=lax.Precision.HIGHEST, preferred_element_type=F32,
    )
    for s in range(2):
        for row in range(ROWS_X):
            sites_out[0, s, row : row + 1, :] = level[s, row, 0:1, :]
            sites_out[1, s, row : row + 1, :] = factor[s, row, 0:1, :]
            start_out[s, row] = start[s, row].astype(BF16)


def local_kernel(
    sites, kept_start, real2_in, imag2_in,
    local_out, level, factor, start, real1, imag1, real2, imag2, real3, imag3, real4, products,
):
    real2_in, imag2_in, real4 = Rows(real2_in, HALO), Rows(imag2_in, HALO), Rows(real4, HALO)
    for s in range(2):
        for row in range(ROWS_X):
            level[s, row] = jnp.broadcast_to(sites[0, s, row : row + 1, :], (8, LANES))
            factor[s, row] = jnp.broadcast_to(sites[1, s, row : row + 1, :], (8, LANES))
            start[s, row] = kept_start[s, row].astype(F32)
        for row in range(HALO, HALO + WIDTH_X):
            real2[s, row] = real2_in[s, row, :, :]
            imag2[s, row] = imag2_in[s, row, :, :]

    def one(i, carry):
        span(level, factor, 1, None, (start, None), (real1, imag1), 2 * i + 1)
        return carry

    lax.fori_loop(0, 7, one, 0)
    for row in (2, ROWS_X - 4):
        span(level, factor, 2, (start, None), (real1, imag1), (real2, imag2), row)

    def three(i, carry):
        span(level, factor, 3, (real1, imag1), (real2, imag2), (real3, imag3), 2 * i + 3)
        return carry

    lax.fori_loop(0, 5, three, 0)

    def four(i, carry):
        row = 2 * i + HALO
        span(level, factor, 4, (real2, imag2), (real3, imag3), (real4, None), row)
        for d in range(2):
            for s in range(2):
                for n, ref in enumerate((real1, real2, real3, real4)):
                    total = None
                    for h in range(2):
                        index = (s, row + d, slice(h * 8, (h + 1) * 8), slice(0, OWN))
                        product = start[index] * ref[index]
                        total = product if h == 0 else total + product
                    for b in range(BLOCKS):
                        products[n, s, b, pl.ds(8 * (2 * i + d), 8), :] = (
                            total[:, b * BLOCK : (b + 1) * BLOCK]
                        )
        return carry

    lax.fori_loop(0, WIDTH_X // 2, four, 0)
    for n in range(TERMS):
        for s in range(2):
            for b in range(BLOCKS):
                total = products[n, s, b, pl.ds(0, WIDTH_X, stride=8), :]
                for r in range(1, 8):
                    total = total + products[n, s, b, pl.ds(r, WIDTH_X, stride=8), :]
                local_out[n, s, :, b * BLOCK : (b + 1) * BLOCK] = total * (1.0 / R)


def total_kernel(sites, shared, out):
    total = jnp.sum(shared[...], axis=0, keepdims=True) * (1.0 / sites)
    for n in range(TERMS):
        out[n : n + 1, :] = total[:, n * R : (n + 1) * R]


def local(stored_vectors, disorder, vacancy, plan):
    columns = lax.axis_size("gy")
    rows = lax.axis_size("gx")
    devices = rows * columns
    smem = pl.BlockSpec(memory_space=pltpu.SMEM)
    vmem = pl.BlockSpec(memory_space=pltpu.VMEM)
    params = pltpu.CompilerParams(vmem_limit_bytes=8 * 1024 * 1024)

    hbm = pl.BlockSpec(memory_space=pltpu.HBM)
    outgoing = pl.pallas_call(
        functools.partial(pack_kernel, columns),
        out_shape=jax.ShapeDtypeStruct((columns, SLOT_ROWS, BLOCK), BF16),
        in_specs=[hbm] * 4,
        out_specs=vmem,
        scratch_shapes=[
            pltpu.SMEM(plan.shape, plan.dtype),
            pltpu.VMEM(stored_vectors.shape, stored_vectors.dtype),
            pltpu.VMEM(disorder.shape, disorder.dtype),
            pltpu.VMEM(vacancy.shape, vacancy.dtype),
            pltpu.VMEM((BLOCKS, 2 * R * WIDTH_X, BLOCK), F32),
            pltpu.SMEM((BLOCKS + 1,), jnp.int32),
            pltpu.SemaphoreType.DMA((4,)),
        ],
        compiler_params=pltpu.CompilerParams(vmem_limit_bytes=60 * 1024 * 1024),
        name="pack",
    )(plan, stored_vectors, disorder, vacancy)
    received = lax.all_to_all(outgoing, "gy", split_axis=0, concat_axis=0, tiled=True)

    message = jax.ShapeDtypeStruct((MESSAGE, OWN), BF16)
    low_rows, high_rows = pl.pallas_call(
        functools.partial(arrange_kernel, columns),
        out_shape=(message, message),
        in_specs=[smem, vmem, vmem, vmem],
        out_specs=(vmem, vmem),
        scratch_shapes=[pltpu.VMEM((2, 4 * 2 * HALO, OWN), F32)],
        compiler_params=params,
        name="arrange",
    )(plan, received, disorder, vacancy)
    up = [(i, (i + 1) % rows) for i in range(rows)]
    down = [(target, source) for source, target in up]
    below = lax.ppermute(high_rows, "gx", up)
    above = lax.ppermute(low_rows, "gx", down)

    site = jax.ShapeDtypeStruct((2, ROWS_X, 8, LANES), F32)
    field = jax.ShapeDtypeStruct((2, ROWS_X, R, LANES), F32)
    narrow = jax.ShapeDtypeStruct((2, WIDTH_X, R, LANES), F32)
    state = (site, site) + (field,) * 3 + (narrow,) * 2
    inner = pl.pallas_call(
        functools.partial(interior_kernel, columns),
        out_shape=state + (jax.ShapeDtypeStruct((2 * SUMS * 8, BLOCK), F32),),
        in_specs=[smem, vmem, vmem, vmem],
        out_specs=(vmem,) * 8,
        compiler_params=params,
        cost_estimate=pl.CostEstimate(flops=10**7, bytes_accessed=8 * 10**6, transcendentals=0),
        name="interior",
    )(plan, received, disorder, vacancy)
    outputs = pl.pallas_call(
        border_kernel,
        out_shape=state + (
            jax.ShapeDtypeStruct((devices, TERMS * R), F32),
            jax.ShapeDtypeStruct((2, 2, ROWS_X, LANES), F32),
            jax.ShapeDtypeStruct(field.shape, BF16),
        ),
        in_specs=[vmem] * 10,
        out_specs=(vmem,) * 10,
        input_output_aliases={2 + i: i for i in range(7)},
        compiler_params=params,
        name="border",
    )(below, above, *inner)
    real2, imag2, partial, sites, start = outputs[5:]
    shared = lax.all_to_all(partial, ("gx", "gy"), split_axis=0, concat_axis=0, tiled=True)
    local_moments = pl.pallas_call(
        local_kernel,
        out_shape=jax.ShapeDtypeStruct((TERMS, 2, WIDTH_X, OWN), F32),
        in_specs=[vmem] * 4,
        out_specs=vmem,
        scratch_shapes=[pltpu.VMEM(site.shape, F32)] * 2
        + [pltpu.VMEM(field.shape, F32)] * 7
        + [
            pltpu.VMEM(narrow.shape, F32),
            pltpu.VMEM((TERMS, 2, BLOCKS, 8 * WIDTH_X, BLOCK), F32),
        ],
        compiler_params=pltpu.CompilerParams(vmem_limit_bytes=16 * 1024 * 1024),
        cost_estimate=pl.CostEstimate(flops=10**7, bytes_accessed=8 * 10**6, transcendentals=0),
        name="local_moments",
    )(sites, start, real2, imag2)
    trace = pl.pallas_call(
        functools.partial(total_kernel, 2 * WIDTH_X * rows * OWN * columns),
        out_shape=jax.ShapeDtypeStruct((TERMS, R), F32),
        in_specs=[vmem],
        out_specs=vmem,
        compiler_params=params,
        name="total",
    )(shared)
    return local_moments, trace


def solution(mesh):
    placed = (P(None, None, "gx", "gy"), P(None, "gx", "gy"), P(None, "gx", "gy"), P())
    return jax.shard_map(
        local, mesh=mesh, in_specs=placed,
        out_specs=(P(None, None, "gx", "gy"), P()), check_vma=False,
    )
```

```python
import functools

import jax
import jax.numpy as jnp
from jax import lax
from jax.experimental import pallas as pl
from jax.experimental.pallas import tpu as pltpu
from jax.sharding import PartitionSpec as P

BLOCK = 128
R = 16
TERMS = 4
HALO = 4
BLOCKS = 4
LANES = BLOCK * (BLOCKS + 1)
OWN = BLOCK * BLOCKS
WIDTH_X = 8
ROWS_X = WIDTH_X + 2 * HALO
SLOT = 2 * WIDTH_X * R
EDGE = SLOT
SITE_EDGE = SLOT + R
SLOT_ROWS = SLOT + R + 8
NEAR = 2
PART = 2 * NEAR * R
PLANES = PART
SIDES = PLANES + 4 * 2 * NEAR
NEAR_MESSAGE = SIDES + R
FAR_MESSAGE = SIDES

HOP_NEXT = 0.3
TWIST_COS = 0.4535961214255773
TWIST_SIN = 0.8912073600614354
SPREAD = 6.5
COS = HOP_NEXT * TWIST_COS
SIN = HOP_NEXT * TWIST_SIN
F32 = jnp.float32
BF16 = jnp.bfloat16


def site_planes(onsite, keep):
    high = onsite.astype(BF16).astype(F32)
    rest = onsite - high
    middle = rest.astype(BF16).astype(F32)
    low = (rest - middle).astype(BF16).astype(F32)
    return high, middle, low, keep


def lane_index(rows, lanes):
    return lax.broadcasted_iota(jnp.int32, (rows, lanes), 1)


def pack_kernel(
    columns, plan_hbm, stored_hbm, disorder_hbm, vacancy_hbm, out,
    plan, stored, disorder, vacancy, turned, where_to, arrived,
):
    copies = [
        pltpu.make_async_copy(source, target, arrived.at[i])
        for i, (source, target) in enumerate(
            ((plan_hbm, plan), (stored_hbm, stored), (disorder_hbm, disorder), (vacancy_hbm, vacancy))
        )
    ]
    for copy in copies:
        copy.start()
    me = lax.axis_index("gy")
    first = me * BLOCKS
    copies[0].wait()

    def find(k, carry):
        held = plan[k] - first
        spot = jnp.where((held >= 0) & (held < BLOCKS), held, BLOCKS)
        where_to[spot] = k
        return carry

    lax.fori_loop(0, BLOCKS * columns, find, 0, unroll=8)

    copies[1].wait()
    for b in range(BLOCKS):
        block = stored[:, :, :, b * BLOCK : (b + 1) * BLOCK]
        turned[b] = block.reshape(2 * R * WIDTH_X, BLOCK).astype(F32)
    lane = lane_index(8, BLOCK)
    edges = [[jnp.zeros((8, BLOCK), F32) for _ in range(2)] for _ in range(BLOCKS)]
    slots = [where_to[b] // BLOCKS for b in range(BLOCKS)]
    for s in range(2):
        for x in range(WIDTH_X):
            q = s * WIDTH_X + x
            for b in range(BLOCKS):
                parts = []
                for h in range(2):
                    base = s * R * WIDTH_X + h * 8 * WIDTH_X + x
                    rows = turned[b, pl.ds(base, 8, stride=WIDTH_X), :]
                    parts.append(rows)
                    moved = pltpu.roll(rows, (8 * q + 4) % BLOCK, 1)
                    edges[b][h] = jnp.where(lane // 8 == q, moved, edges[b][h])
                both = jnp.concatenate(parts, axis=0).astype(BF16)
                out[slots[b], q * R : (q + 1) * R, :] = both
    last_half = lane_index(R, BLOCK) % 8 < 4
    for b in range(BLOCKS):
        spot = where_to[b]
        edge = jnp.concatenate(edges[b], axis=0)

        @pl.when(spot % BLOCKS == BLOCKS - 1)
        def _():
            slot = ((spot + 1) // BLOCKS) % columns
            old = out[slot, EDGE : EDGE + R, :].astype(F32)
            out[slot, EDGE : EDGE + R, :] = jnp.where(last_half, edge, old).astype(BF16)

        @pl.when(spot % BLOCKS == 0)
        def _():
            slot = (spot // BLOCKS + columns - 1) % columns
            old = out[slot, EDGE : EDGE + R, :].astype(F32)
            out[slot, EDGE : EDGE + R, :] = jnp.where(last_half, old, edge).astype(BF16)

    copies[2].wait()
    copies[3].wait()
    lane16 = lane_index(R, BLOCK)
    ends = []
    for ref in (disorder, vacancy):
        low = ref[:, :, 0:BLOCK].reshape(R, BLOCK).astype(F32)
        high = ref[:, :, OWN - BLOCK : OWN].reshape(R, BLOCK).astype(F32)
        ends.append(jnp.where(lane16 < BLOCK // 2, low, high))
    sites = jnp.zeros((R, BLOCK), F32)
    for p, plane in enumerate(site_planes(ends[0], ends[1])):
        sites = jnp.where(lane16 // 8 == p, pltpu.roll(plane, 8 * p + 4, 1), sites)
    sites = jnp.where(lane < 32, sites[0:8], pltpu.roll(sites[8:16], 32, 1)).astype(BF16)
    out[(me + 1) % columns, SITE_EDGE : SITE_EDGE + 8, :] = sites
    out[(me + columns - 1) % columns, SITE_EDGE : SITE_EDGE + 8, :] = sites


def edge_tiles(columns, plan, received):
    me = lax.axis_index("gy")
    total = BLOCKS * columns
    left = plan[(me * BLOCKS + total - 1) % total] // BLOCKS
    right = plan[(me * BLOCKS + BLOCKS) % total] // BLOCKS
    last_half = lane_index(R, BLOCK) % 8 < 4
    tile = jnp.where(
        last_half,
        received[left, EDGE : EDGE + R, :].astype(F32),
        received[right, EDGE : EDGE + R, :].astype(F32),
    )
    low = (me + columns - 1) % columns
    high = (me + 1) % columns
    sites = jnp.where(
        last_half[0:8],
        received[low, SITE_EDGE : SITE_EDGE + 8, :].astype(F32),
        received[high, SITE_EDGE : SITE_EDGE + 8, :].astype(F32),
    )
    return tile, sites


def arrange_kernel(
    columns, plan, received, disorder, vacancy, low_near, high_near, low_far, high_far, planes
):
    me = lax.axis_index("gy")
    outs = ((low_near, 0), (high_near, WIDTH_X - NEAR), (low_far, NEAR), (high_far, NEAR + NEAR))
    size = NEAR * R
    for b in range(BLOCKS):
        slot = plan[me * BLOCKS + b] // BLOCKS
        lanes = slice(b * BLOCK, (b + 1) * BLOCK)
        for s in range(2):
            for out, x in outs:
                base = (s * WIDTH_X + x) * R
                out[s * size : (s + 1) * size, lanes] = received[slot, base : base + size, :]
    tile, sites = edge_tiles(columns, plan, received)
    for out in (low_near, high_near):
        out[SIDES : SIDES + R, 0:BLOCK] = tile.astype(BF16)
        out[SIDES : SIDES + 8, BLOCK : 2 * BLOCK] = sites.astype(BF16)
        out[SIDES + 8 : SIDES + R, BLOCK : 2 * BLOCK] = jnp.zeros((8, BLOCK), BF16)
        out[SIDES : SIDES + R, 2 * BLOCK : OWN] = jnp.zeros((R, OWN - 2 * BLOCK), BF16)
    for s in range(2):
        for p, plane in enumerate(site_planes(disorder[s], vacancy[s].astype(F32))):
            row = p * 2 * NEAR + s * NEAR
            for i, (_, x) in enumerate(outs):
                planes[i, row : row + NEAR, :] = plane[x : x + NEAR]
    for i, (out, _) in enumerate(outs):
        out[PLANES:SIDES, :] = planes[i].astype(BF16)


def fill_sites(level, factor, s, rows, onsite, kept, source, first):
    lane = lane_index(8, BLOCK)
    in_halo = (lane < HALO) | (lane >= BLOCK - HALO)
    side_level = jnp.zeros((8, BLOCK), F32)
    for p in range(3):
        side_level = side_level + pltpu.roll(source, BLOCK - 4 - 8 * p - 32 * s, 1)
    side_keep = pltpu.roll(source, BLOCK - 4 - 8 * 3 - 32 * s, 1)
    side_level = jnp.where(in_halo, side_level, 0.0)
    side_keep = jnp.where(in_halo, side_keep, 0.0)
    kept_rows = []
    for i, row in enumerate(rows):
        j = first + i
        lev = jnp.concatenate([onsite[i : i + 1], side_level[j : j + 1]], axis=1)
        kep = jnp.concatenate([kept[i : i + 1], side_keep[j : j + 1]], axis=1)
        level[s, row] = jnp.broadcast_to(lev * (1.0 / COS), (8, LANES))
        kep = jnp.broadcast_to(kep, (8, LANES))
        factor[s, row] = kep * (2.0 * COS / SPREAD)
        kept_rows.append(kep)
    return kept_rows


def unpack_rows(message, near, level, factor, start, base, x):
    planes = message[PLANES:SIDES, :].astype(F32)
    tile = near[SIDES : SIDES + R, 0:BLOCK].astype(F32)
    sites = near[SIDES : SIDES + 8, BLOCK : 2 * BLOCK].astype(F32)
    step = 2 * NEAR
    onsite = planes[0:step] + planes[step : 2 * step] + planes[2 * step : 3 * step]
    keep = planes[3 * step : 4 * step]
    for s in range(2):
        some = slice(s * NEAR, (s + 1) * NEAR)
        kept = fill_sites(
            level, factor, s, range(base, base + NEAR), onsite[some], keep[some], sites, x
        )
        for i in range(NEAR):
            index = (s * NEAR + i) * R
            q = s * WIDTH_X + x + i
            side = pltpu.roll(tile, (BLOCK - 4 - 8 * q) % BLOCK, 1)
            value = jnp.concatenate([message[index : index + R, :].astype(F32), side], axis=1)
            for h in range(2):
                part = slice(h * 8, (h + 1) * 8)
                start[s, base + i, part, :] = value[part] * kept[i]


def span(level, factor, term, old, now, new, row, count=2):
    for h in range(2):
        part = slice(h * 8, (h + 1) * 8)
        near_rows = range(-1, count + 1)
        real = [{d: now[0][s, row + d, part, :] for d in near_rows} for s in range(2)]
        fields = [real]
        if now[1] is not None:
            fields.append([{d: now[1][s, row + d, part, :] for d in near_rows} for s in range(2)])
        others = [
            [{d: f[s][d] * (1.0 / COS) for d in near_rows} for s in range(2)] for f in fields
        ]
        for s in range(2):
            ratio = SIN / COS if s == 0 else -SIN / COS
            turn = [{d: f[s][d] * ratio for d in near_rows} for f in fields]
            if len(fields) == 1:
                ahead = [real[s], turn[0]]
                back = [real[s], {d: -turn[0][d] for d in near_rows}]
            else:
                imag = fields[1][s]
                ahead = [
                    {d: real[s][d] - turn[1][d] for d in near_rows},
                    {d: imag[d] + turn[0][d] for d in near_rows},
                ]
                back = [
                    {d: real[s][d] + turn[1][d] for d in near_rows},
                    {d: imag[d] - turn[0][d] for d in near_rows},
                ]
            for c in range(2):
                if new[c] is None:
                    continue
                joint = {d: ahead[c][d - 1] + back[c][d] for d in range(count + 1)}
                for d in range(count):
                    out = ahead[c][d + 1] + back[c][d - 1]
                    up, down = joint[d], joint[d + 1]
                    if c < len(fields):
                        other = others[c][1 - s]
                        aside = d - 1 if s == 0 else d + 1
                        out = out + level[s, row + d] * fields[c][s][d]
                        out = out - (other[d] + other[aside])
                        if s == 0:
                            down = down - other[d]
                        else:
                            up = up - other[d]
                    out = out + pltpu.roll(up, LANES - 1, 1) + pltpu.roll(down, 1, 1)
                    scale = factor[s, row + d]
                    out = out * (scale * 0.5 if term == 1 else scale)
                    if term > 1 and old[c] is not None:
                        out = out - old[c][s, row + d, part, :]
                    new[c][s, row + d, part, :] = out


def fold(product):
    lanes = product[:, 0:BLOCK]
    for b in range(1, BLOCKS):
        lanes = lanes + product[:, b * BLOCK : (b + 1) * BLOCK]
    return lanes


def trace_row(start, first, second, row, sums):
    own = slice(0, OWN)
    sums = list(sums)
    for h in range(2):
        part = slice(h * 8, (h + 1) * 8)
        for s in range(2):
            v0 = start[s, row, part, own]
            r1 = first[0][s, row, part, own]
            i1 = first[1][s, row, part, own]
            r2 = second[0][s, row, part, own]
            i2 = second[1][s, row, part, own]
            terms = (v0 * v0, v0 * r1, v0 * r2, r1 * r2 + i1 * i2, r2 * r2 + i2 * i2)
            for n, term in enumerate(terms):
                sums[n * 2 + h] = sums[n * 2 + h] + fold(term)
    return tuple(sums)


SUMS = 5


class Rows:
    def __init__(self, ref, first):
        self.ref = ref
        self.first = first

    def __getitem__(self, index):
        s, row, part, lanes = index
        return self.ref[s, row - self.first, part, lanes]

    def __setitem__(self, index, value):
        s, row, part, lanes = index
        self.ref[s, row - self.first, part, lanes] = value


def interior_kernel(
    columns, plan, received, disorder, vacancy,
    level, factor, start, real1, imag1, real2, imag2, sums, own_sites, own_start,
):
    real2, imag2 = Rows(real2, HALO), Rows(imag2, HALO)
    me = lax.axis_index("gy")
    tile, sites = edge_tiles(columns, plan, received)
    slots = [plan[me * BLOCKS + b] // BLOCKS for b in range(BLOCKS)]
    for s in range(2):
        kept = fill_sites(
            level, factor, s, range(HALO, HALO + WIDTH_X), disorder[s],
            vacancy[s].astype(F32), sites, 0,
        )
        for x in range(WIDTH_X):
            q = s * WIDTH_X + x
            pieces = [received[slots[b], q * R : (q + 1) * R, :].astype(F32) for b in range(BLOCKS)]
            pieces.append(pltpu.roll(tile, (BLOCK - 4 - 8 * q) % BLOCK, 1))
            value = jnp.concatenate(pieces, axis=1)
            value = value * jnp.concatenate([kept[x], kept[x]], axis=0)
            start[s, HALO + x] = value
            own_start[s, x] = value.astype(BF16)
            own_sites[0, s, x : x + 1, :] = level[s, HALO + x, 0:1, :]
            own_sites[1, s, x : x + 1, :] = factor[s, HALO + x, 0:1, :]

    def one(i, carry):
        row = HALO + 1 + 2 * i
        span(level, factor, 1, None, (start, None), (real1, imag1), row)
        return carry

    lax.fori_loop(0, 3, one, 0)

    def two(i, carry):
        row = HALO + 2 + 2 * i
        span(level, factor, 2, (start, None), (real1, imag1), (real2, imag2), row)
        for d in range(2):
            carry = trace_row(start, (real1, imag1), (real2, imag2), row + d, carry)
        return carry

    zero = jnp.zeros((8, BLOCK), F32)
    totals = lax.fori_loop(0, 2, two, (zero,) * (2 * SUMS))
    for i, total in enumerate(totals):
        sums[i * 8 : (i + 1) * 8, :] = total


def border_kernel(
    below, above, level_in, factor_in, start_in, real1_in, imag1_in, real2_in, imag2_in, sums_in,
    level, factor, start, real1, imag1, real2, imag2, trace_out,
):
    real2, imag2 = Rows(real2, HALO), Rows(imag2, HALO)
    unpack_rows(below, below, level, factor, start, HALO - NEAR, WIDTH_X - NEAR)
    unpack_rows(above, above, level, factor, start, HALO + WIDTH_X, 0)
    for row in (HALO - 1, HALO + WIDTH_X - 1):
        span(level, factor, 1, None, (start, None), (real1, imag1), row)
    totals = tuple(sums_in[i * 8 : (i + 1) * 8, :] for i in range(2 * SUMS))
    for row in (HALO, HALO + WIDTH_X - 2):
        span(level, factor, 2, (start, None), (real1, imag1), (real2, imag2), row)
        for d in range(2):
            totals = trace_row(start, (real1, imag1), (real2, imag2), row + d, totals)
    norm, one_one, one_two, both, second = (
        jnp.concatenate(totals[2 * n : 2 * n + 2], axis=0) for n in range(SUMS)
    )
    moments = jnp.concatenate(
        [one_one, one_two, 2.0 * both - one_one, 2.0 * second - norm], axis=0
    )
    trace_out[...] = lax.dot_general(
        jnp.ones(trace_out.shape[:1] + (BLOCK,), F32), moments,
        (((1,), (1,)), ((), ())),
        precision=lax.Precision.HIGHEST, preferred_element_type=F32,
    )


def local_kernel(
    below, above, below_far, above_far, own_sites, own_start, real2_in, imag2_in,
    local_out, level, factor, start, real1, imag1, real2, imag2, real3, imag3, real4, products,
):
    real4 = Rows(real4, HALO)
    for s in range(2):
        for x in range(WIDTH_X):
            row = HALO + x
            level[s, row] = jnp.broadcast_to(own_sites[0, s, x : x + 1, :], (8, LANES))
            factor[s, row] = jnp.broadcast_to(own_sites[1, s, x : x + 1, :], (8, LANES))
            start[s, row] = own_start[s, x].astype(F32)
            real2[s, row] = real2_in[s, x]
            imag2[s, row] = imag2_in[s, x]
    unpack_rows(below_far, below, level, factor, start, 0, WIDTH_X - HALO)
    unpack_rows(below, below, level, factor, start, NEAR, WIDTH_X - NEAR)
    unpack_rows(above, above, level, factor, start, HALO + WIDTH_X, 0)
    unpack_rows(above_far, above, level, factor, start, HALO + WIDTH_X + NEAR, NEAR)

    def one(i, carry):
        span(level, factor, 1, None, (start, None), (real1, imag1), 2 * i + 1)
        return carry

    lax.fori_loop(0, 7, one, 0)
    for row in (2, ROWS_X - 4):
        span(level, factor, 2, (start, None), (real1, imag1), (real2, imag2), row)

    def three(i, carry):
        span(level, factor, 3, (real1, imag1), (real2, imag2), (real3, imag3), 2 * i + 3)
        return carry

    lax.fori_loop(0, 5, three, 0)

    def four(i, carry):
        row = 2 * i + HALO
        span(level, factor, 4, (real2, imag2), (real3, imag3), (real4, None), row)
        for d in range(2):
            for s in range(2):
                for n, ref in enumerate((real1, real2, real3, real4)):
                    total = None
                    for h in range(2):
                        index = (s, row + d, slice(h * 8, (h + 1) * 8), slice(0, OWN))
                        product = start[index] * ref[index]
                        total = product if h == 0 else total + product
                    for b in range(BLOCKS):
                        products[n, s, b, pl.ds(8 * (2 * i + d), 8), :] = (
                            total[:, b * BLOCK : (b + 1) * BLOCK]
                        )
        return carry

    lax.fori_loop(0, WIDTH_X // 2, four, 0)
    for n in range(TERMS):
        for s in range(2):
            for b in range(BLOCKS):
                total = products[n, s, b, pl.ds(0, WIDTH_X, stride=8), :]
                for r in range(1, 8):
                    total = total + products[n, s, b, pl.ds(r, WIDTH_X, stride=8), :]
                local_out[n, s, :, b * BLOCK : (b + 1) * BLOCK] = total * (1.0 / R)


def total_kernel(sites, shared, out):
    total = jnp.sum(shared[...], axis=0, keepdims=True) * (1.0 / sites)
    for n in range(TERMS):
        out[n : n + 1, :] = total[:, n * R : (n + 1) * R]


def local(stored_vectors, disorder, vacancy, plan):
    columns = lax.axis_size("gy")
    rows = lax.axis_size("gx")
    devices = rows * columns
    smem = pl.BlockSpec(memory_space=pltpu.SMEM)
    vmem = pl.BlockSpec(memory_space=pltpu.VMEM)
    params = pltpu.CompilerParams(vmem_limit_bytes=8 * 1024 * 1024)

    hbm = pl.BlockSpec(memory_space=pltpu.HBM)
    outgoing = pl.pallas_call(
        functools.partial(pack_kernel, columns),
        out_shape=jax.ShapeDtypeStruct((columns, SLOT_ROWS, BLOCK), BF16),
        in_specs=[hbm] * 4,
        out_specs=vmem,
        scratch_shapes=[
            pltpu.SMEM(plan.shape, plan.dtype),
            pltpu.VMEM(stored_vectors.shape, stored_vectors.dtype),
            pltpu.VMEM(disorder.shape, disorder.dtype),
            pltpu.VMEM(vacancy.shape, vacancy.dtype),
            pltpu.VMEM((BLOCKS, 2 * R * WIDTH_X, BLOCK), F32),
            pltpu.SMEM((BLOCKS + 1,), jnp.int32),
            pltpu.SemaphoreType.DMA((4,)),
        ],
        compiler_params=pltpu.CompilerParams(vmem_limit_bytes=16 * 1024 * 1024),
        name="pack",
    )(*(
        pltpu.with_memory_space_constraint(x, pltpu.HBM)
        for x in (plan, stored_vectors, disorder, vacancy)
    ))
    received = lax.all_to_all(outgoing, "gy", split_axis=0, concat_axis=0, tiled=True)

    near_message = jax.ShapeDtypeStruct((NEAR_MESSAGE, OWN), BF16)
    far_message = jax.ShapeDtypeStruct((FAR_MESSAGE, OWN), BF16)
    low_near, high_near, low_far, high_far = pl.pallas_call(
        functools.partial(arrange_kernel, columns),
        out_shape=(near_message, near_message, far_message, far_message),
        in_specs=[smem, vmem, vmem, vmem],
        out_specs=(vmem,) * 4,
        scratch_shapes=[pltpu.VMEM((4, 4 * 2 * NEAR, OWN), F32)],
        compiler_params=params,
        name="arrange",
    )(plan, received, disorder, vacancy)
    up = [(i, (i + 1) % rows) for i in range(rows)]
    down = [(target, source) for source, target in up]
    below = lax.ppermute(high_near, "gx", up)
    above = lax.ppermute(low_near, "gx", down)
    below_far = lax.ppermute(high_far, "gx", up)
    above_far = lax.ppermute(low_far, "gx", down)

    site = jax.ShapeDtypeStruct((2, ROWS_X, 8, LANES), F32)
    field = jax.ShapeDtypeStruct((2, ROWS_X, R, LANES), F32)
    narrow = jax.ShapeDtypeStruct((2, WIDTH_X, R, LANES), F32)
    state = (site, site) + (field,) * 3 + (narrow,) * 2
    *inner, own_sites, own_start = pl.pallas_call(
        functools.partial(interior_kernel, columns),
        out_shape=state + (
            jax.ShapeDtypeStruct((2 * SUMS * 8, BLOCK), F32),
            jax.ShapeDtypeStruct((2, 2, WIDTH_X, LANES), F32),
            jax.ShapeDtypeStruct((2, WIDTH_X, R, LANES), BF16),
        ),
        in_specs=[smem, vmem, vmem, vmem],
        out_specs=(vmem,) * 10,
        compiler_params=params,
        cost_estimate=pl.CostEstimate(flops=10**7, bytes_accessed=8 * 10**6, transcendentals=0),
        name="interior",
    )(plan, received, disorder, vacancy)
    outputs = pl.pallas_call(
        border_kernel,
        out_shape=state + (jax.ShapeDtypeStruct((devices, TERMS * R), F32),),
        in_specs=[vmem] * 10,
        out_specs=(vmem,) * 8,
        input_output_aliases={2 + i: i for i in range(7)},
        compiler_params=params,
        name="border",
    )(below, above, *inner)
    real2, imag2, partial = outputs[5:]
    shared = lax.all_to_all(partial, ("gx", "gy"), split_axis=0, concat_axis=0, tiled=True)
    local_moments = pl.pallas_call(
        local_kernel,
        out_shape=jax.ShapeDtypeStruct((TERMS, 2, WIDTH_X, OWN), F32),
        in_specs=[vmem] * 8,
        out_specs=vmem,
        scratch_shapes=[pltpu.VMEM(site.shape, F32)] * 2
        + [pltpu.VMEM(field.shape, F32)] * 7
        + [
            pltpu.VMEM(narrow.shape, F32),
            pltpu.VMEM((TERMS, 2, BLOCKS, 8 * WIDTH_X, BLOCK), F32),
        ],
        compiler_params=pltpu.CompilerParams(vmem_limit_bytes=16 * 1024 * 1024),
        cost_estimate=pl.CostEstimate(flops=10**7, bytes_accessed=8 * 10**6, transcendentals=0),
        name="local_moments",
    )(below, above, below_far, above_far, own_sites, own_start, real2, imag2)
    trace = pl.pallas_call(
        functools.partial(total_kernel, 2 * WIDTH_X * rows * OWN * columns),
        out_shape=jax.ShapeDtypeStruct((TERMS, R), F32),
        in_specs=[vmem],
        out_specs=vmem,
        compiler_params=params,
        name="total",
    )(shared)
    return local_moments, trace


def solution(mesh):
    placed = (P(None, None, "gx", "gy"), P(None, "gx", "gy"), P(None, "gx", "gy"), P())
    return jax.shard_map(
        local, mesh=mesh, in_specs=placed,
        out_specs=(P(None, None, "gx", "gy"), P()), check_vma=False,
    )
```

```python
import functools

import jax
import jax.numpy as jnp
from jax import lax
from jax.experimental import pallas as pl
from jax.experimental.pallas import tpu as pltpu
from jax.sharding import PartitionSpec as P

BLOCK = 128
R = 16
TERMS = 4
HALO = 4
BLOCKS = 4
LANES = BLOCK * (BLOCKS + 1)
OWN = BLOCK * BLOCKS
WIDTH_X = 8
ROWS_X = WIDTH_X + 2 * HALO
SLOT = 2 * WIDTH_X * R
EDGE = SLOT
SITE_EDGE = SLOT + R
SLOT_ROWS = SLOT + R + 8
NEAR = 2
PART = 2 * NEAR * R
PLANES = PART
SIDES = PLANES + 4 * 2 * NEAR
NEAR_MESSAGE = SIDES + R
FAR_MESSAGE = SIDES

HOP_NEXT = 0.3
TWIST_COS = 0.4535961214255773
TWIST_SIN = 0.8912073600614354
SPREAD = 6.5
COS = HOP_NEXT * TWIST_COS
SIN = HOP_NEXT * TWIST_SIN
F32 = jnp.float32
BF16 = jnp.bfloat16


def site_planes(onsite, keep):
    high = onsite.astype(BF16).astype(F32)
    rest = onsite - high
    middle = rest.astype(BF16).astype(F32)
    low = (rest - middle).astype(BF16).astype(F32)
    return high, middle, low, keep


def lane_index(rows, lanes):
    return lax.broadcasted_iota(jnp.int32, (rows, lanes), 1)


def pack_kernel(
    columns, plan_hbm, stored_hbm, disorder_hbm, vacancy_hbm, out, table,
    plan, stored, disorder, vacancy, turned, where_to, arrived,
):
    copies = [
        pltpu.make_async_copy(source, target, arrived.at[i])
        for i, (source, target) in enumerate(
            ((plan_hbm, plan), (stored_hbm, stored), (disorder_hbm, disorder), (vacancy_hbm, vacancy))
        )
    ]
    for copy in copies:
        copy.start()
    me = lax.axis_index("gy")
    first = me * BLOCKS
    copies[0].wait()

    def find(k, carry):
        held = plan[k] - first
        spot = jnp.where((held >= 0) & (held < BLOCKS), held, BLOCKS)
        where_to[spot] = k
        return carry

    lax.fori_loop(0, BLOCKS * columns, find, 0, unroll=8)

    total = BLOCKS * columns
    sources = [first + b for b in range(BLOCKS)]
    sources += [(first + total - 1) % total, (first + BLOCKS) % total]
    for i, k in enumerate(sources):
        table[i : i + 1, :] = jnp.full((1, BLOCK), plan[k] // BLOCKS, jnp.int32)
    copies[1].wait()
    for b in range(BLOCKS):
        block = stored[:, :, :, b * BLOCK : (b + 1) * BLOCK]
        turned[b] = block.reshape(2 * R * WIDTH_X, BLOCK).astype(F32)
    lane = lane_index(8, BLOCK)
    edges = [[jnp.zeros((8, BLOCK), F32) for _ in range(2)] for _ in range(BLOCKS)]
    slots = [where_to[b] // BLOCKS for b in range(BLOCKS)]
    for s in range(2):
        for x in range(WIDTH_X):
            q = s * WIDTH_X + x
            for b in range(BLOCKS):
                parts = []
                for h in range(2):
                    base = s * R * WIDTH_X + h * 8 * WIDTH_X + x
                    rows = turned[b, pl.ds(base, 8, stride=WIDTH_X), :]
                    parts.append(rows)
                    moved = pltpu.roll(rows, (8 * q + 4) % BLOCK, 1)
                    edges[b][h] = jnp.where(lane // 8 == q, moved, edges[b][h])
                both = jnp.concatenate(parts, axis=0).astype(BF16)
                out[slots[b], q * R : (q + 1) * R, :] = both
    last_half = lane_index(R, BLOCK) % 8 < 4
    for b in range(BLOCKS):
        spot = where_to[b]
        edge = jnp.concatenate(edges[b], axis=0)

        @pl.when(spot % BLOCKS == BLOCKS - 1)
        def _():
            slot = ((spot + 1) // BLOCKS) % columns
            old = out[slot, EDGE : EDGE + R, :].astype(F32)
            out[slot, EDGE : EDGE + R, :] = jnp.where(last_half, edge, old).astype(BF16)

        @pl.when(spot % BLOCKS == 0)
        def _():
            slot = (spot // BLOCKS + columns - 1) % columns
            old = out[slot, EDGE : EDGE + R, :].astype(F32)
            out[slot, EDGE : EDGE + R, :] = jnp.where(last_half, old, edge).astype(BF16)

    copies[2].wait()
    copies[3].wait()
    lane16 = lane_index(R, BLOCK)
    ends = []
    for ref in (disorder, vacancy):
        low = ref[:, :, 0:BLOCK].reshape(R, BLOCK).astype(F32)
        high = ref[:, :, OWN - BLOCK : OWN].reshape(R, BLOCK).astype(F32)
        ends.append(jnp.where(lane16 < BLOCK // 2, low, high))
    sites = jnp.zeros((R, BLOCK), F32)
    for p, plane in enumerate(site_planes(ends[0], ends[1])):
        sites = jnp.where(lane16 // 8 == p, pltpu.roll(plane, 8 * p + 4, 1), sites)
    sites = jnp.where(lane < 32, sites[0:8], pltpu.roll(sites[8:16], 32, 1)).astype(BF16)
    out[(me + 1) % columns, SITE_EDGE : SITE_EDGE + 8, :] = sites
    out[(me + columns - 1) % columns, SITE_EDGE : SITE_EDGE + 8, :] = sites


def source_of(table, i):
    return table[i : i + 1, 0:1][0, 0]


def edge_tiles(columns, table, received):
    me = lax.axis_index("gy")
    left = source_of(table, BLOCKS)
    right = source_of(table, BLOCKS + 1)
    last_half = lane_index(R, BLOCK) % 8 < 4
    tile = jnp.where(
        last_half,
        received[left, EDGE : EDGE + R, :].astype(F32),
        received[right, EDGE : EDGE + R, :].astype(F32),
    )
    low = (me + columns - 1) % columns
    high = (me + 1) % columns
    sites = jnp.where(
        last_half[0:8],
        received[low, SITE_EDGE : SITE_EDGE + 8, :].astype(F32),
        received[high, SITE_EDGE : SITE_EDGE + 8, :].astype(F32),
    )
    return tile, sites


def arrange_kernel(
    columns, table, received, disorder, vacancy, low_near, high_near, low_far, high_far, planes
):
    outs = ((low_near, 0), (high_near, WIDTH_X - NEAR), (low_far, NEAR), (high_far, NEAR + NEAR))
    size = NEAR * R
    for b in range(BLOCKS):
        slot = source_of(table, b)
        lanes = slice(b * BLOCK, (b + 1) * BLOCK)
        for s in range(2):
            for out, x in outs:
                base = (s * WIDTH_X + x) * R
                out[s * size : (s + 1) * size, lanes] = received[slot, base : base + size, :]
    tile, sites = edge_tiles(columns, table, received)
    for out in (low_near, high_near):
        out[SIDES : SIDES + R, 0:BLOCK] = tile.astype(BF16)
        out[SIDES : SIDES + 8, BLOCK : 2 * BLOCK] = sites.astype(BF16)
        out[SIDES + 8 : SIDES + R, BLOCK : 2 * BLOCK] = jnp.zeros((8, BLOCK), BF16)
        out[SIDES : SIDES + R, 2 * BLOCK : OWN] = jnp.zeros((R, OWN - 2 * BLOCK), BF16)
    for s in range(2):
        for p, plane in enumerate(site_planes(disorder[s], vacancy[s].astype(F32))):
            row = p * 2 * NEAR + s * NEAR
            for i, (_, x) in enumerate(outs):
                planes[i, row : row + NEAR, :] = plane[x : x + NEAR]
    for i, (out, _) in enumerate(outs):
        out[PLANES:SIDES, :] = planes[i].astype(BF16)


def fill_sites(level, factor, s, rows, onsite, kept, source, first):
    lane = lane_index(8, BLOCK)
    in_halo = (lane < HALO) | (lane >= BLOCK - HALO)
    side_level = jnp.zeros((8, BLOCK), F32)
    for p in range(3):
        side_level = side_level + pltpu.roll(source, BLOCK - 4 - 8 * p - 32 * s, 1)
    side_keep = pltpu.roll(source, BLOCK - 4 - 8 * 3 - 32 * s, 1)
    side_level = jnp.where(in_halo, side_level, 0.0)
    side_keep = jnp.where(in_halo, side_keep, 0.0)
    kept_rows = []
    for i, row in enumerate(rows):
        j = first + i
        lev = jnp.concatenate([onsite[i : i + 1], side_level[j : j + 1]], axis=1)
        kep = jnp.concatenate([kept[i : i + 1], side_keep[j : j + 1]], axis=1)
        level[s, row] = jnp.broadcast_to(lev * (1.0 / COS), (8, LANES))
        kep = jnp.broadcast_to(kep, (8, LANES))
        factor[s, row] = kep * (2.0 * COS / SPREAD)
        kept_rows.append(kep)
    return kept_rows


def unpack_rows(message, near, level, factor, start, base, x):
    planes = message[PLANES:SIDES, :].astype(F32)
    tile = near[SIDES : SIDES + R, 0:BLOCK].astype(F32)
    sites = near[SIDES : SIDES + 8, BLOCK : 2 * BLOCK].astype(F32)
    step = 2 * NEAR
    onsite = planes[0:step] + planes[step : 2 * step] + planes[2 * step : 3 * step]
    keep = planes[3 * step : 4 * step]
    for s in range(2):
        some = slice(s * NEAR, (s + 1) * NEAR)
        kept = fill_sites(
            level, factor, s, range(base, base + NEAR), onsite[some], keep[some], sites, x
        )
        for i in range(NEAR):
            index = (s * NEAR + i) * R
            q = s * WIDTH_X + x + i
            side = pltpu.roll(tile, (BLOCK - 4 - 8 * q) % BLOCK, 1)
            value = jnp.concatenate([message[index : index + R, :].astype(F32), side], axis=1)
            for h in range(2):
                part = slice(h * 8, (h + 1) * 8)
                start[s, base + i, part, :] = value[part] * kept[i]


def span(level, factor, term, old, now, new, row, count=2):
    for h in range(2):
        part = slice(h * 8, (h + 1) * 8)
        near_rows = range(-1, count + 1)
        real = [{d: now[0][s, row + d, part, :] for d in near_rows} for s in range(2)]
        fields = [real]
        if now[1] is not None:
            fields.append([{d: now[1][s, row + d, part, :] for d in near_rows} for s in range(2)])
        others = [
            [{d: f[s][d] * (1.0 / COS) for d in near_rows} for s in range(2)] for f in fields
        ]
        for s in range(2):
            ratio = SIN / COS if s == 0 else -SIN / COS
            turn = [{d: f[s][d] * ratio for d in near_rows} for f in fields]
            if len(fields) == 1:
                ahead = [real[s], turn[0]]
                back = [real[s], {d: -turn[0][d] for d in near_rows}]
            else:
                imag = fields[1][s]
                ahead = [
                    {d: real[s][d] - turn[1][d] for d in near_rows},
                    {d: imag[d] + turn[0][d] for d in near_rows},
                ]
                back = [
                    {d: real[s][d] + turn[1][d] for d in near_rows},
                    {d: imag[d] - turn[0][d] for d in near_rows},
                ]
            for c in range(2):
                if new[c] is None:
                    continue
                joint = {d: ahead[c][d - 1] + back[c][d] for d in range(count + 1)}
                for d in range(count):
                    out = ahead[c][d + 1] + back[c][d - 1]
                    up, down = joint[d], joint[d + 1]
                    if c < len(fields):
                        other = others[c][1 - s]
                        aside = d - 1 if s == 0 else d + 1
                        out = out + level[s, row + d] * fields[c][s][d]
                        out = out - (other[d] + other[aside])
                        if s == 0:
                            down = down - other[d]
                        else:
                            up = up - other[d]
                    out = out + pltpu.roll(up, LANES - 1, 1) + pltpu.roll(down, 1, 1)
                    scale = factor[s, row + d]
                    out = out * (scale * 0.5 if term == 1 else scale)
                    if term > 1 and old[c] is not None:
                        out = out - old[c][s, row + d, part, :]
                    new[c][s, row + d, part, :] = out


def fold(product):
    lanes = product[:, 0:BLOCK]
    for b in range(1, BLOCKS):
        lanes = lanes + product[:, b * BLOCK : (b + 1) * BLOCK]
    return lanes


def trace_row(start, first, second, row, sums):
    own = slice(0, OWN)
    sums = list(sums)
    for h in range(2):
        part = slice(h * 8, (h + 1) * 8)
        for s in range(2):
            v0 = start[s, row, part, own]
            r1 = first[0][s, row, part, own]
            i1 = first[1][s, row, part, own]
            r2 = second[0][s, row, part, own]
            i2 = second[1][s, row, part, own]
            terms = (v0 * v0, v0 * r1, v0 * r2, r1 * r2 + i1 * i2, r2 * r2 + i2 * i2)
            for n, term in enumerate(terms):
                sums[n * 2 + h] = sums[n * 2 + h] + fold(term)
    return tuple(sums)


SUMS = 5


class Rows:
    def __init__(self, ref, first):
        self.ref = ref
        self.first = first

    def __getitem__(self, index):
        s, row, part, lanes = index
        return self.ref[s, row - self.first, part, lanes]

    def __setitem__(self, index, value):
        s, row, part, lanes = index
        self.ref[s, row - self.first, part, lanes] = value


def interior_kernel(
    columns, table, received, disorder, vacancy,
    level, factor, start, real1, imag1, real2, imag2, sums, own_sites, own_start,
):
    real2, imag2 = Rows(real2, HALO), Rows(imag2, HALO)
    tile, sites = edge_tiles(columns, table, received)
    slots = [source_of(table, b) for b in range(BLOCKS)]
    for s in range(2):
        kept = fill_sites(
            level, factor, s, range(HALO, HALO + WIDTH_X), disorder[s],
            vacancy[s].astype(F32), sites, 0,
        )
        for x in range(WIDTH_X):
            q = s * WIDTH_X + x
            pieces = [received[slots[b], q * R : (q + 1) * R, :].astype(F32) for b in range(BLOCKS)]
            pieces.append(pltpu.roll(tile, (BLOCK - 4 - 8 * q) % BLOCK, 1))
            value = jnp.concatenate(pieces, axis=1)
            value = value * jnp.concatenate([kept[x], kept[x]], axis=0)
            start[s, HALO + x] = value
            own_start[s, x] = value.astype(BF16)
            own_sites[0, s, x : x + 1, :] = level[s, HALO + x, 0:1, :]
            own_sites[1, s, x : x + 1, :] = factor[s, HALO + x, 0:1, :]

    def one(i, carry):
        row = HALO + 1 + 2 * i
        span(level, factor, 1, None, (start, None), (real1, imag1), row)
        return carry

    lax.fori_loop(0, 3, one, 0)

    def two(i, carry):
        row = HALO + 2 + 2 * i
        span(level, factor, 2, (start, None), (real1, imag1), (real2, imag2), row)
        for d in range(2):
            carry = trace_row(start, (real1, imag1), (real2, imag2), row + d, carry)
        return carry

    zero = jnp.zeros((8, BLOCK), F32)
    totals = lax.fori_loop(0, 2, two, (zero,) * (2 * SUMS))
    for i, total in enumerate(totals):
        sums[i * 8 : (i + 1) * 8, :] = total


def border_kernel(
    below, above, level_in, factor_in, start_in, real1_in, imag1_in, real2_in, imag2_in, sums_in,
    level, factor, start, real1, imag1, real2, imag2, trace_out,
):
    real2, imag2 = Rows(real2, HALO), Rows(imag2, HALO)
    unpack_rows(below, below, level, factor, start, HALO - NEAR, WIDTH_X - NEAR)
    unpack_rows(above, above, level, factor, start, HALO + WIDTH_X, 0)
    for row in (HALO - 1, HALO + WIDTH_X - 1):
        span(level, factor, 1, None, (start, None), (real1, imag1), row)
    totals = tuple(sums_in[i * 8 : (i + 1) * 8, :] for i in range(2 * SUMS))
    for row in (HALO, HALO + WIDTH_X - 2):
        span(level, factor, 2, (start, None), (real1, imag1), (real2, imag2), row)
        for d in range(2):
            totals = trace_row(start, (real1, imag1), (real2, imag2), row + d, totals)
    norm, one_one, one_two, both, second = (
        jnp.concatenate(totals[2 * n : 2 * n + 2], axis=0) for n in range(SUMS)
    )
    moments = jnp.concatenate(
        [one_one, one_two, 2.0 * both - one_one, 2.0 * second - norm], axis=0
    )
    trace_out[...] = lax.dot_general(
        jnp.ones(trace_out.shape[:1] + (BLOCK,), F32), moments,
        (((1,), (1,)), ((), ())),
        precision=lax.Precision.HIGHEST, preferred_element_type=F32,
    )


def local_kernel(
    below, above, below_far, above_far, own_sites, own_start, real2_in, imag2_in,
    local_out, level, factor, start, real1, imag1, real2, imag2, real3, imag3, real4, products,
):
    real4 = Rows(real4, HALO)
    for s in range(2):
        for x in range(WIDTH_X):
            row = HALO + x
            level[s, row] = jnp.broadcast_to(own_sites[0, s, x : x + 1, :], (8, LANES))
            factor[s, row] = jnp.broadcast_to(own_sites[1, s, x : x + 1, :], (8, LANES))
            start[s, row] = own_start[s, x].astype(F32)
            real2[s, row] = real2_in[s, x]
            imag2[s, row] = imag2_in[s, x]
    unpack_rows(below_far, below, level, factor, start, 0, WIDTH_X - HALO)
    unpack_rows(below, below, level, factor, start, NEAR, WIDTH_X - NEAR)
    unpack_rows(above, above, level, factor, start, HALO + WIDTH_X, 0)
    unpack_rows(above_far, above, level, factor, start, HALO + WIDTH_X + NEAR, NEAR)

    def one(i, carry):
        span(level, factor, 1, None, (start, None), (real1, imag1), 2 * i + 1)
        return carry

    lax.fori_loop(0, 7, one, 0)
    for row in (2, ROWS_X - 4):
        span(level, factor, 2, (start, None), (real1, imag1), (real2, imag2), row)

    def three(i, carry):
        span(level, factor, 3, (real1, imag1), (real2, imag2), (real3, imag3), 2 * i + 3)
        return carry

    lax.fori_loop(0, 5, three, 0)

    def four(i, carry):
        row = 2 * i + HALO
        span(level, factor, 4, (real2, imag2), (real3, imag3), (real4, None), row)
        for d in range(2):
            for s in range(2):
                for n, ref in enumerate((real1, real2, real3, real4)):
                    total = None
                    for h in range(2):
                        index = (s, row + d, slice(h * 8, (h + 1) * 8), slice(0, OWN))
                        product = start[index] * ref[index]
                        total = product if h == 0 else total + product
                    for b in range(BLOCKS):
                        products[n, s, b, pl.ds(8 * (2 * i + d), 8), :] = (
                            total[:, b * BLOCK : (b + 1) * BLOCK]
                        )
        return carry

    lax.fori_loop(0, WIDTH_X // 2, four, 0)
    for n in range(TERMS):
        for s in range(2):
            for b in range(BLOCKS):
                total = products[n, s, b, pl.ds(0, WIDTH_X, stride=8), :]
                for r in range(1, 8):
                    total = total + products[n, s, b, pl.ds(r, WIDTH_X, stride=8), :]
                local_out[n, s, :, b * BLOCK : (b + 1) * BLOCK] = total * (1.0 / R)


def total_kernel(sites, shared, out):
    total = jnp.sum(shared[...], axis=0, keepdims=True) * (1.0 / sites)
    for n in range(TERMS):
        out[n : n + 1, :] = total[:, n * R : (n + 1) * R]


def local(stored_vectors, disorder, vacancy, plan):
    columns = lax.axis_size("gy")
    rows = lax.axis_size("gx")
    devices = rows * columns
    vmem = pl.BlockSpec(memory_space=pltpu.VMEM)
    params = pltpu.CompilerParams(vmem_limit_bytes=8 * 1024 * 1024)

    hbm = pl.BlockSpec(memory_space=pltpu.HBM)
    outgoing, table = pl.pallas_call(
        functools.partial(pack_kernel, columns),
        out_shape=(
            jax.ShapeDtypeStruct((columns, SLOT_ROWS, BLOCK), BF16),
            jax.ShapeDtypeStruct((8, BLOCK), jnp.int32),
        ),
        in_specs=[hbm] * 4,
        out_specs=(vmem, vmem),
        scratch_shapes=[
            pltpu.SMEM(plan.shape, plan.dtype),
            pltpu.VMEM(stored_vectors.shape, stored_vectors.dtype),
            pltpu.VMEM(disorder.shape, disorder.dtype),
            pltpu.VMEM(vacancy.shape, vacancy.dtype),
            pltpu.VMEM((BLOCKS, 2 * R * WIDTH_X, BLOCK), F32),
            pltpu.SMEM((BLOCKS + 1,), jnp.int32),
            pltpu.SemaphoreType.DMA((4,)),
        ],
        compiler_params=pltpu.CompilerParams(vmem_limit_bytes=16 * 1024 * 1024),
        name="pack",
    )(*(
        pltpu.with_memory_space_constraint(x, pltpu.HBM)
        for x in (plan, stored_vectors, disorder, vacancy)
    ))
    received = lax.all_to_all(outgoing, "gy", split_axis=0, concat_axis=0, tiled=True)

    near_message = jax.ShapeDtypeStruct((NEAR_MESSAGE, OWN), BF16)
    far_message = jax.ShapeDtypeStruct((FAR_MESSAGE, OWN), BF16)
    low_near, high_near, low_far, high_far = pl.pallas_call(
        functools.partial(arrange_kernel, columns),
        out_shape=(near_message, near_message, far_message, far_message),
        in_specs=[vmem] * 4,
        out_specs=(vmem,) * 4,
        scratch_shapes=[pltpu.VMEM((4, 4 * 2 * NEAR, OWN), F32)],
        compiler_params=params,
        name="arrange",
    )(table, received, disorder, vacancy)
    up = [(i, (i + 1) % rows) for i in range(rows)]
    down = [(target, source) for source, target in up]
    below = lax.ppermute(high_near, "gx", up)
    above = lax.ppermute(low_near, "gx", down)
    below_far = lax.ppermute(high_far, "gx", up)
    above_far = lax.ppermute(low_far, "gx", down)

    site = jax.ShapeDtypeStruct((2, ROWS_X, 8, LANES), F32)
    field = jax.ShapeDtypeStruct((2, ROWS_X, R, LANES), F32)
    narrow = jax.ShapeDtypeStruct((2, WIDTH_X, R, LANES), F32)
    state = (site, site) + (field,) * 3 + (narrow,) * 2
    *inner, own_sites, own_start = pl.pallas_call(
        functools.partial(interior_kernel, columns),
        out_shape=state + (
            jax.ShapeDtypeStruct((2 * SUMS * 8, BLOCK), F32),
            jax.ShapeDtypeStruct((2, 2, WIDTH_X, LANES), F32),
            jax.ShapeDtypeStruct((2, WIDTH_X, R, LANES), BF16),
        ),
        in_specs=[vmem] * 4,
        out_specs=(vmem,) * 10,
        compiler_params=params,
        cost_estimate=pl.CostEstimate(flops=10**7, bytes_accessed=8 * 10**6, transcendentals=0),
        name="interior",
    )(table, received, disorder, vacancy)
    outputs = pl.pallas_call(
        border_kernel,
        out_shape=state + (jax.ShapeDtypeStruct((devices, TERMS * R), F32),),
        in_specs=[vmem] * 10,
        out_specs=(vmem,) * 8,
        input_output_aliases={2 + i: i for i in range(7)},
        compiler_params=params,
        name="border",
    )(below, above, *inner)
    real2, imag2, partial = outputs[5:]
    shared = lax.all_to_all(partial, ("gx", "gy"), split_axis=0, concat_axis=0, tiled=True)
    local_moments = pl.pallas_call(
        local_kernel,
        out_shape=jax.ShapeDtypeStruct((TERMS, 2, WIDTH_X, OWN), F32),
        in_specs=[vmem] * 8,
        out_specs=vmem,
        scratch_shapes=[pltpu.VMEM(site.shape, F32)] * 2
        + [pltpu.VMEM(field.shape, F32)] * 7
        + [
            pltpu.VMEM(narrow.shape, F32),
            pltpu.VMEM((TERMS, 2, BLOCKS, 8 * WIDTH_X, BLOCK), F32),
        ],
        compiler_params=pltpu.CompilerParams(vmem_limit_bytes=16 * 1024 * 1024),
        cost_estimate=pl.CostEstimate(flops=10**7, bytes_accessed=8 * 10**6, transcendentals=0),
        name="local_moments",
    )(below, above, below_far, above_far, own_sites, own_start, real2, imag2)
    trace = pl.pallas_call(
        functools.partial(total_kernel, 2 * WIDTH_X * rows * OWN * columns),
        out_shape=jax.ShapeDtypeStruct((TERMS, R), F32),
        in_specs=[vmem],
        out_specs=vmem,
        compiler_params=params,
        name="total",
    )(shared)
    return local_moments, trace


def solution(mesh):
    placed = (P(None, None, "gx", "gy"), P(None, "gx", "gy"), P(None, "gx", "gy"), P())
    return jax.shard_map(
        local, mesh=mesh, in_specs=placed,
        out_specs=(P(None, None, "gx", "gy"), P()), check_vma=False,
    )
```

```python
import functools

import jax
import jax.numpy as jnp
from jax import lax
from jax.experimental import pallas as pl
from jax.experimental.pallas import tpu as pltpu
from jax.sharding import PartitionSpec as P

BLOCK = 128
R = 16
TERMS = 4
HALO = 4
BLOCKS = 4
LANES = BLOCK * (BLOCKS + 1)
OWN = BLOCK * BLOCKS
WIDTH_X = 8
ROWS_X = WIDTH_X + 2 * HALO
SLOT = 2 * WIDTH_X * R
EDGE = SLOT
SITE_EDGE = SLOT + R
SLOT_ROWS = SLOT + R + 8
NEAR = 2
PART = 2 * NEAR * R
PLANES = PART
SIDES = PLANES + 4 * 2 * NEAR
NEAR_MESSAGE = SIDES + R
FAR_MESSAGE = SIDES

HOP_NEXT = 0.3
TWIST_COS = 0.4535961214255773
TWIST_SIN = 0.8912073600614354
SPREAD = 6.5
COS = HOP_NEXT * TWIST_COS
SIN = HOP_NEXT * TWIST_SIN
F32 = jnp.float32
BF16 = jnp.bfloat16


def bfloat16_terms(value):
    high = value.astype(BF16).astype(F32)
    rest = value - high
    middle = rest.astype(BF16).astype(F32)
    return high, middle, rest - middle


def site_planes(onsite, keep):
    return (*bfloat16_terms(onsite), keep)


def lane_index(rows, lanes):
    return lax.broadcasted_iota(jnp.int32, (rows, lanes), 1)


def pack_kernel(
    columns, plan_hbm, stored_hbm, disorder_hbm, vacancy_hbm, out, table,
    plan, stored, disorder, vacancy, turned, arrived,
):
    copies = [
        pltpu.make_async_copy(source, target, arrived.at[i])
        for i, (source, target) in enumerate(
            ((plan_hbm, plan), (stored_hbm, stored), (disorder_hbm, disorder), (vacancy_hbm, vacancy))
        )
    ]
    for copy in copies:
        copy.start()
    me = lax.axis_index("gy")
    first = me * BLOCKS
    total = BLOCKS * columns
    copies[0].wait()
    place = lane_index(1, total)
    listed = plan[...]
    spots = [
        jnp.sum(jnp.where(listed == first + b, place, 0), axis=1, keepdims=True)[0, 0]
        for b in range(BLOCKS)
    ]
    source = listed // BLOCKS
    wanted = [first + b for b in range(BLOCKS)]
    wanted += [(first + total - 1) % total, (first + BLOCKS) % total]
    for i, k in enumerate(wanted):
        row = jnp.sum(jnp.where(place == k, source, 0), axis=1, keepdims=True)
        table[i : i + 1, :] = jnp.broadcast_to(row, (1, BLOCK))
    copies[1].wait()
    for b in range(BLOCKS):
        block = stored[:, :, :, b * BLOCK : (b + 1) * BLOCK]
        turned[b] = block.reshape(2 * R * WIDTH_X, BLOCK).astype(F32)
    lane = lane_index(8, BLOCK)
    edges = [[jnp.zeros((8, BLOCK), F32) for _ in range(2)] for _ in range(BLOCKS)]
    slots = [spot // BLOCKS for spot in spots]
    for s in range(2):
        for x in range(WIDTH_X):
            q = s * WIDTH_X + x
            for b in range(BLOCKS):
                parts = []
                for h in range(2):
                    base = s * R * WIDTH_X + h * 8 * WIDTH_X + x
                    rows = turned[b, pl.ds(base, 8, stride=WIDTH_X), :]
                    parts.append(rows)
                    moved = pltpu.roll(rows, (8 * q + 4) % BLOCK, 1)
                    edges[b][h] = jnp.where(lane // 8 == q, moved, edges[b][h])
                both = jnp.concatenate(parts, axis=0).astype(BF16)
                out[slots[b], q * R : (q + 1) * R, :] = both
    last_half = lane_index(R, BLOCK) % 8 < 4
    for b in range(BLOCKS):
        spot = spots[b]
        edge = jnp.concatenate(edges[b], axis=0)

        @pl.when(spot % BLOCKS == BLOCKS - 1)
        def _():
            slot = ((spot + 1) // BLOCKS) % columns
            old = out[slot, EDGE : EDGE + R, :].astype(F32)
            out[slot, EDGE : EDGE + R, :] = jnp.where(last_half, edge, old).astype(BF16)

        @pl.when(spot % BLOCKS == 0)
        def _():
            slot = (spot // BLOCKS + columns - 1) % columns
            old = out[slot, EDGE : EDGE + R, :].astype(F32)
            out[slot, EDGE : EDGE + R, :] = jnp.where(last_half, old, edge).astype(BF16)

    copies[2].wait()
    copies[3].wait()
    lane16 = lane_index(R, BLOCK)
    ends = []
    for ref in (disorder, vacancy):
        low = ref[:, :, 0:BLOCK].reshape(R, BLOCK).astype(F32)
        high = ref[:, :, OWN - BLOCK : OWN].reshape(R, BLOCK).astype(F32)
        ends.append(jnp.where(lane16 < BLOCK // 2, low, high))
    sites = jnp.zeros((R, BLOCK), F32)
    for p, plane in enumerate(site_planes(ends[0], ends[1])):
        sites = jnp.where(lane16 // 8 == p, pltpu.roll(plane, 8 * p + 4, 1), sites)
    sites = jnp.where(lane < 32, sites[0:8], pltpu.roll(sites[8:16], 32, 1)).astype(BF16)
    out[(me + 1) % columns, SITE_EDGE : SITE_EDGE + 8, :] = sites
    out[(me + columns - 1) % columns, SITE_EDGE : SITE_EDGE + 8, :] = sites


def source_of(table, i):
    return table[i : i + 1, 0:1][0, 0]


def edge_tiles(columns, table, received):
    me = lax.axis_index("gy")
    left = source_of(table, BLOCKS)
    right = source_of(table, BLOCKS + 1)
    last_half = lane_index(R, BLOCK) % 8 < 4
    tile = jnp.where(
        last_half,
        received[left, EDGE : EDGE + R, :].astype(F32),
        received[right, EDGE : EDGE + R, :].astype(F32),
    )
    low = (me + columns - 1) % columns
    high = (me + 1) % columns
    sites = jnp.where(
        last_half[0:8],
        received[low, SITE_EDGE : SITE_EDGE + 8, :].astype(F32),
        received[high, SITE_EDGE : SITE_EDGE + 8, :].astype(F32),
    )
    return tile, sites


def arrange_kernel(
    columns, table, received, disorder, vacancy, low_near, high_near, low_far, high_far, planes
):
    outs = ((low_near, 0), (high_near, WIDTH_X - NEAR), (low_far, NEAR), (high_far, NEAR + NEAR))
    size = NEAR * R
    for b in range(BLOCKS):
        slot = source_of(table, b)
        lanes = slice(b * BLOCK, (b + 1) * BLOCK)
        for s in range(2):
            for out, x in outs:
                base = (s * WIDTH_X + x) * R
                out[s * size : (s + 1) * size, lanes] = received[slot, base : base + size, :]
    tile, sites = edge_tiles(columns, table, received)
    for out in (low_near, high_near):
        out[SIDES : SIDES + R, 0:BLOCK] = tile.astype(BF16)
        out[SIDES : SIDES + 8, BLOCK : 2 * BLOCK] = sites.astype(BF16)
        out[SIDES + 8 : SIDES + R, BLOCK : 2 * BLOCK] = jnp.zeros((8, BLOCK), BF16)
        out[SIDES : SIDES + R, 2 * BLOCK : OWN] = jnp.zeros((R, OWN - 2 * BLOCK), BF16)
    for s in range(2):
        for p, plane in enumerate(site_planes(disorder[s], vacancy[s].astype(F32))):
            row = p * 2 * NEAR + s * NEAR
            for i, (_, x) in enumerate(outs):
                planes[i, row : row + NEAR, :] = plane[x : x + NEAR]
    for i, (out, _) in enumerate(outs):
        out[PLANES:SIDES, :] = planes[i].astype(BF16)


def fill_sites(level, factor, s, rows, onsite, kept, source, first):
    lane = lane_index(8, BLOCK)
    in_halo = (lane < HALO) | (lane >= BLOCK - HALO)
    side_level = jnp.zeros((8, BLOCK), F32)
    for p in range(3):
        side_level = side_level + pltpu.roll(source, BLOCK - 4 - 8 * p - 32 * s, 1)
    side_keep = pltpu.roll(source, BLOCK - 4 - 8 * 3 - 32 * s, 1)
    side_level = jnp.where(in_halo, side_level, 0.0)
    side_keep = jnp.where(in_halo, side_keep, 0.0)
    kept_rows = []
    for i, row in enumerate(rows):
        j = first + i
        lev = jnp.concatenate([onsite[i : i + 1], side_level[j : j + 1]], axis=1)
        kep = jnp.concatenate([kept[i : i + 1], side_keep[j : j + 1]], axis=1)
        level[s, row] = jnp.broadcast_to(lev * (1.0 / COS), (8, LANES))
        kep = jnp.broadcast_to(kep, (8, LANES))
        factor[s, row] = kep * (2.0 * COS / SPREAD)
        kept_rows.append(kep)
    return kept_rows


def unpack_rows(message, near, level, factor, start, base, x):
    planes = message[PLANES:SIDES, :].astype(F32)
    tile = near[SIDES : SIDES + R, 0:BLOCK].astype(F32)
    sites = near[SIDES : SIDES + 8, BLOCK : 2 * BLOCK].astype(F32)
    step = 2 * NEAR
    onsite = planes[0:step] + planes[step : 2 * step] + planes[2 * step : 3 * step]
    keep = planes[3 * step : 4 * step]
    for s in range(2):
        some = slice(s * NEAR, (s + 1) * NEAR)
        kept = fill_sites(
            level, factor, s, range(base, base + NEAR), onsite[some], keep[some], sites, x
        )
        for i in range(NEAR):
            index = (s * NEAR + i) * R
            q = s * WIDTH_X + x + i
            side = pltpu.roll(tile, (BLOCK - 4 - 8 * q) % BLOCK, 1)
            value = jnp.concatenate([message[index : index + R, :].astype(F32), side], axis=1)
            for h in range(2):
                part = slice(h * 8, (h + 1) * 8)
                start[s, base + i, part, :] = value[part] * kept[i]


def span(level, factor, term, old, now, new, row, count=2):
    for h in range(2):
        part = slice(h * 8, (h + 1) * 8)
        near_rows = range(-1, count + 1)
        real = [{d: now[0][s, row + d, part, :] for d in near_rows} for s in range(2)]
        fields = [real]
        if now[1] is not None:
            fields.append([{d: now[1][s, row + d, part, :] for d in near_rows} for s in range(2)])
        others = [
            [{d: f[s][d] * (1.0 / COS) for d in near_rows} for s in range(2)] for f in fields
        ]
        for s in range(2):
            ratio = SIN / COS if s == 0 else -SIN / COS
            turn = [{d: f[s][d] * ratio for d in near_rows} for f in fields]
            if len(fields) == 1:
                ahead = [real[s], turn[0]]
                back = [real[s], {d: -turn[0][d] for d in near_rows}]
            else:
                imag = fields[1][s]
                ahead = [
                    {d: real[s][d] - turn[1][d] for d in near_rows},
                    {d: imag[d] + turn[0][d] for d in near_rows},
                ]
                back = [
                    {d: real[s][d] + turn[1][d] for d in near_rows},
                    {d: imag[d] - turn[0][d] for d in near_rows},
                ]
            for c in range(2):
                if new[c] is None:
                    continue
                joint = {d: ahead[c][d - 1] + back[c][d] for d in range(count + 1)}
                for d in range(count):
                    out = ahead[c][d + 1] + back[c][d - 1]
                    up, down = joint[d], joint[d + 1]
                    if c < len(fields):
                        other = others[c][1 - s]
                        aside = d - 1 if s == 0 else d + 1
                        out = out + level[s, row + d] * fields[c][s][d]
                        out = out - (other[d] + other[aside])
                        if s == 0:
                            down = down - other[d]
                        else:
                            up = up - other[d]
                    out = out + pltpu.roll(up, LANES - 1, 1) + pltpu.roll(down, 1, 1)
                    scale = factor[s, row + d]
                    out = out * (scale * 0.5 if term == 1 else scale)
                    if term > 1 and old[c] is not None:
                        out = out - old[c][s, row + d, part, :]
                    new[c][s, row + d, part, :] = out


def fold(product):
    lanes = product[:, 0:BLOCK]
    for b in range(1, BLOCKS):
        lanes = lanes + product[:, b * BLOCK : (b + 1) * BLOCK]
    return lanes


def trace_row(start, first, second, row, sums):
    own = slice(0, OWN)
    sums = list(sums)
    for h in range(2):
        part = slice(h * 8, (h + 1) * 8)
        for s in range(2):
            v0 = start[s, row, part, own]
            r1 = first[0][s, row, part, own]
            i1 = first[1][s, row, part, own]
            r2 = second[0][s, row, part, own]
            i2 = second[1][s, row, part, own]
            terms = (v0 * v0, v0 * r1, v0 * r2, r1 * r2 + i1 * i2, r2 * r2 + i2 * i2)
            for n, term in enumerate(terms):
                sums[n * 2 + h] = sums[n * 2 + h] + fold(term)
    return tuple(sums)


SUMS = 5


class Rows:
    def __init__(self, ref, first):
        self.ref = ref
        self.first = first

    def __getitem__(self, index):
        s, row, *rest = index
        return self.ref[(s, row - self.first, *rest)]

    def __setitem__(self, index, value):
        s, row, *rest = index
        self.ref[(s, row - self.first, *rest)] = value


class Joined:
    def __init__(self, *pieces):
        self.at = {row: (ref, i) for ref, rows in pieces for i, row in enumerate(rows)}

    def __getitem__(self, index):
        s, row, *rest = index
        ref, i = self.at[row]
        return ref[(s, i, *rest)]

    def __setitem__(self, index, value):
        s, row, *rest = index
        ref, i = self.at[row]
        ref[(s, i, *rest)] = value


OWN_ROWS = range(HALO, HALO + WIDTH_X)
NEAR_ROWS = (2, 3, 12, 13)
FIRST_ROWS = range(5, 11)
FIRST_BORDER = (3, 4, 11, 12)
SECOND_ROWS = range(6, 10)
SECOND_BORDER = (4, 5, 10, 11)


def interior_kernel(
    columns, table, received, disorder, vacancy,
    level, factor, start, real1, imag1, real2, imag2, sums, own_sites, own_start,
):
    own_level, own_factor = level, factor
    level, factor, start = (Rows(ref, HALO) for ref in (level, factor, start))
    real1, imag1 = (Rows(ref, FIRST_ROWS[0]) for ref in (real1, imag1))
    real2, imag2 = (Rows(ref, SECOND_ROWS[0]) for ref in (real2, imag2))
    tile, sites = edge_tiles(columns, table, received)
    slots = [source_of(table, b) for b in range(BLOCKS)]
    for s in range(2):
        kept = fill_sites(
            level, factor, s, range(HALO, HALO + WIDTH_X), disorder[s],
            vacancy[s].astype(F32), sites, 0,
        )
        for x in range(WIDTH_X):
            q = s * WIDTH_X + x
            pieces = [received[slots[b], q * R : (q + 1) * R, :].astype(F32) for b in range(BLOCKS)]
            pieces.append(pltpu.roll(tile, (BLOCK - 4 - 8 * q) % BLOCK, 1))
            value = jnp.concatenate(pieces, axis=1)
            value = value * jnp.concatenate([kept[x], kept[x]], axis=0)
            start[s, HALO + x] = value
            own_start[s, x] = value.astype(BF16)
            own_sites[0, s, x : x + 1, :] = own_level[s, x, 0:1, :]
            own_sites[1, s, x : x + 1, :] = own_factor[s, x, 0:1, :]

    def one(i, carry):
        row = HALO + 1 + 2 * i
        span(level, factor, 1, None, (start, None), (real1, imag1), row)
        return carry

    lax.fori_loop(0, 3, one, 0)

    def two(i, carry):
        row = HALO + 2 + 2 * i
        span(level, factor, 2, (start, None), (real1, imag1), (real2, imag2), row)
        for d in range(2):
            carry = trace_row(start, (real1, imag1), (real2, imag2), row + d, carry)
        return carry

    zero = jnp.zeros((8, BLOCK), F32)
    totals = lax.fori_loop(0, 2, two, (zero,) * (2 * SUMS))
    for i, total in enumerate(totals):
        sums[i * 8 : (i + 1) * 8, :] = total


def border_kernel(
    below, above,
    own_level, own_factor, own_start, own_real1, own_imag1, own_real2, own_imag2, sums_in,
    border_real2, border_imag2, trace_out,
    near_level, near_factor, near_start, border_real1, border_imag1,
):
    level = Joined((own_level, OWN_ROWS), (near_level, NEAR_ROWS))
    factor = Joined((own_factor, OWN_ROWS), (near_factor, NEAR_ROWS))
    start = Joined((own_start, OWN_ROWS), (near_start, NEAR_ROWS))
    real1 = Joined((own_real1, FIRST_ROWS), (border_real1, FIRST_BORDER))
    imag1 = Joined((own_imag1, FIRST_ROWS), (border_imag1, FIRST_BORDER))
    real2 = Joined((own_real2, SECOND_ROWS), (border_real2, SECOND_BORDER))
    imag2 = Joined((own_imag2, SECOND_ROWS), (border_imag2, SECOND_BORDER))
    unpack_rows(below, below, level, factor, start, HALO - NEAR, WIDTH_X - NEAR)
    unpack_rows(above, above, level, factor, start, HALO + WIDTH_X, 0)
    for row in (HALO - 1, HALO + WIDTH_X - 1):
        span(level, factor, 1, None, (start, None), (real1, imag1), row)
    totals = tuple(sums_in[i * 8 : (i + 1) * 8, :] for i in range(2 * SUMS))
    for row in (HALO, HALO + WIDTH_X - 2):
        span(level, factor, 2, (start, None), (real1, imag1), (real2, imag2), row)
        for d in range(2):
            totals = trace_row(start, (real1, imag1), (real2, imag2), row + d, totals)
    norm, one_one, one_two, both, second = (
        jnp.concatenate(totals[2 * n : 2 * n + 2], axis=0) for n in range(SUMS)
    )
    moments = jnp.concatenate(
        [one_one, one_two, 2.0 * both - one_one, 2.0 * second - norm], axis=0
    )
    ones = jnp.ones((8, BLOCK), BF16)
    total = jnp.zeros((8, TERMS * R), F32)
    for term in bfloat16_terms(moments):
        total = total + lax.dot_general(
            ones, term.astype(BF16), (((1,), (1,)), ((), ())), preferred_element_type=F32
        )
    for i in range(trace_out.shape[0] // 8):
        trace_out[i * 8 : (i + 1) * 8, :] = total


def local_kernel(
    below, above, below_far, above_far, own_sites, own_start,
    own_real2, own_imag2, border_real2, border_imag2,
    local_out, level, factor, start, real1, imag1, real2, imag2, real3, imag3, real4, products,
):
    real4 = Rows(real4, HALO)
    for s in range(2):
        for x in range(WIDTH_X):
            row = HALO + x
            level[s, row] = jnp.broadcast_to(own_sites[0, s, x : x + 1, :], (8, LANES))
            factor[s, row] = jnp.broadcast_to(own_sites[1, s, x : x + 1, :], (8, LANES))
            start[s, row] = own_start[s, x].astype(F32)
    for ref, own, border in ((real2, own_real2, border_real2), (imag2, own_imag2, border_imag2)):
        for s in range(2):
            for source, rows in ((own, SECOND_ROWS), (border, SECOND_BORDER)):
                for i, row in enumerate(rows):
                    ref[s, row] = source[s, i]
    unpack_rows(below_far, below, level, factor, start, 0, WIDTH_X - HALO)
    unpack_rows(below, below, level, factor, start, NEAR, WIDTH_X - NEAR)
    unpack_rows(above, above, level, factor, start, HALO + WIDTH_X, 0)
    unpack_rows(above_far, above, level, factor, start, HALO + WIDTH_X + NEAR, NEAR)

    def one(i, carry):
        span(level, factor, 1, None, (start, None), (real1, imag1), 2 * i + 1)
        return carry

    lax.fori_loop(0, 7, one, 0)
    for row in (2, ROWS_X - 4):
        span(level, factor, 2, (start, None), (real1, imag1), (real2, imag2), row)

    def three(i, carry):
        span(level, factor, 3, (real1, imag1), (real2, imag2), (real3, imag3), 2 * i + 3)
        return carry

    lax.fori_loop(0, 5, three, 0)

    def four(i, carry):
        row = 2 * i + HALO
        span(level, factor, 4, (real2, imag2), (real3, imag3), (real4, None), row)
        for d in range(2):
            for s in range(2):
                for n, ref in enumerate((real1, real2, real3, real4)):
                    total = None
                    for h in range(2):
                        index = (s, row + d, slice(h * 8, (h + 1) * 8), slice(0, OWN))
                        product = start[index] * ref[index]
                        total = product if h == 0 else total + product
                    for b in range(BLOCKS):
                        products[n, s, b, pl.ds(8 * (2 * i + d), 8), :] = (
                            total[:, b * BLOCK : (b + 1) * BLOCK]
                        )
        return carry

    lax.fori_loop(0, WIDTH_X // 2, four, 0)
    for n in range(TERMS):
        for s in range(2):
            for b in range(BLOCKS):
                total = products[n, s, b, pl.ds(0, WIDTH_X, stride=8), :]
                for r in range(1, 8):
                    total = total + products[n, s, b, pl.ds(r, WIDTH_X, stride=8), :]
                local_out[n, s, :, b * BLOCK : (b + 1) * BLOCK] = total * (1.0 / R)


def total_kernel(sites, shared, out):
    total = jnp.sum(shared[...], axis=0, keepdims=True) * (1.0 / sites)
    for n in range(TERMS):
        out[n : n + 1, :] = total[:, n * R : (n + 1) * R]


def local(stored_vectors, disorder, vacancy, plan):
    columns = lax.axis_size("gy")
    rows = lax.axis_size("gx")
    devices = rows * columns
    vmem = pl.BlockSpec(memory_space=pltpu.VMEM)
    params = pltpu.CompilerParams(vmem_limit_bytes=8 * 1024 * 1024)

    hbm = pl.BlockSpec(memory_space=pltpu.HBM)
    outgoing, table = pl.pallas_call(
        functools.partial(pack_kernel, columns),
        out_shape=(
            jax.ShapeDtypeStruct((columns, SLOT_ROWS, BLOCK), BF16),
            jax.ShapeDtypeStruct((8, BLOCK), jnp.int32),
        ),
        in_specs=[hbm] * 4,
        out_specs=(vmem, vmem),
        scratch_shapes=[
            pltpu.VMEM((1,) + plan.shape, plan.dtype),
            pltpu.VMEM(stored_vectors.shape, stored_vectors.dtype),
            pltpu.VMEM(disorder.shape, disorder.dtype),
            pltpu.VMEM(vacancy.shape, vacancy.dtype),
            pltpu.VMEM((BLOCKS, 2 * R * WIDTH_X, BLOCK), F32),
            pltpu.SemaphoreType.DMA((4,)),
        ],
        compiler_params=pltpu.CompilerParams(vmem_limit_bytes=16 * 1024 * 1024),
        name="pack",
    )(*(
        pltpu.with_memory_space_constraint(x, pltpu.HBM)
        for x in (plan[None], stored_vectors, disorder, vacancy)
    ))
    received = lax.all_to_all(outgoing, "gy", split_axis=0, concat_axis=0, tiled=True)

    near_message = jax.ShapeDtypeStruct((NEAR_MESSAGE, OWN), BF16)
    far_message = jax.ShapeDtypeStruct((FAR_MESSAGE, OWN), BF16)
    low_near, high_near, low_far, high_far = pl.pallas_call(
        functools.partial(arrange_kernel, columns),
        out_shape=(near_message, near_message, far_message, far_message),
        in_specs=[vmem] * 4,
        out_specs=(vmem,) * 4,
        scratch_shapes=[pltpu.VMEM((4, 4 * 2 * NEAR, OWN), F32)],
        compiler_params=params,
        name="arrange",
    )(table, received, disorder, vacancy)
    up = [(i, (i + 1) % rows) for i in range(rows)]
    down = [(target, source) for source, target in up]
    below = lax.ppermute(high_near, "gx", up)
    above = lax.ppermute(low_near, "gx", down)
    below_far = lax.ppermute(high_far, "gx", up)
    above_far = lax.ppermute(low_far, "gx", down)

    def site(count):
        return jax.ShapeDtypeStruct((2, count, 8, LANES), F32)

    def field(count):
        return jax.ShapeDtypeStruct((2, count, R, LANES), F32)

    def scratch(shape):
        return pltpu.VMEM(shape.shape, shape.dtype)

    *inner, own_sites, own_start = pl.pallas_call(
        functools.partial(interior_kernel, columns),
        out_shape=(site(WIDTH_X), site(WIDTH_X), field(WIDTH_X))
        + (field(len(FIRST_ROWS)),) * 2
        + (field(len(SECOND_ROWS)),) * 2
        + (
            jax.ShapeDtypeStruct((2 * SUMS * 8, BLOCK), F32),
            jax.ShapeDtypeStruct((2, 2, WIDTH_X, LANES), F32),
            jax.ShapeDtypeStruct((2, WIDTH_X, R, LANES), BF16),
        ),
        in_specs=[vmem] * 4,
        out_specs=(vmem,) * 10,
        compiler_params=params,
        cost_estimate=pl.CostEstimate(flops=10**7, bytes_accessed=8 * 10**6, transcendentals=0),
        name="interior",
    )(table, received, disorder, vacancy)
    own_real2, own_imag2 = inner[5:7]
    border_real2, border_imag2, partial = pl.pallas_call(
        border_kernel,
        out_shape=(field(len(SECOND_BORDER)),) * 2
        + (jax.ShapeDtypeStruct((devices, TERMS * R), F32),),
        in_specs=[vmem] * 10,
        out_specs=(vmem,) * 3,
        scratch_shapes=[scratch(site(len(NEAR_ROWS)))] * 2
        + [scratch(field(len(NEAR_ROWS)))]
        + [scratch(field(len(FIRST_BORDER)))] * 2,
        compiler_params=params,
        name="border",
    )(below, above, *inner)
    shared = lax.all_to_all(partial, ("gx", "gy"), split_axis=0, concat_axis=0, tiled=True)
    local_moments = pl.pallas_call(
        local_kernel,
        out_shape=jax.ShapeDtypeStruct((TERMS, 2, WIDTH_X, OWN), F32),
        in_specs=[vmem] * 10,
        out_specs=vmem,
        scratch_shapes=[scratch(site(ROWS_X))] * 2
        + [scratch(field(ROWS_X))] * 7
        + [
            scratch(field(WIDTH_X)),
            pltpu.VMEM((TERMS, 2, BLOCKS, 8 * WIDTH_X, BLOCK), F32),
        ],
        compiler_params=pltpu.CompilerParams(vmem_limit_bytes=16 * 1024 * 1024),
        cost_estimate=pl.CostEstimate(flops=10**7, bytes_accessed=8 * 10**6, transcendentals=0),
        name="local_moments",
    )(
        below, above, below_far, above_far, own_sites, own_start,
        own_real2, own_imag2, border_real2, border_imag2,
    )
    trace = pl.pallas_call(
        functools.partial(total_kernel, 2 * WIDTH_X * rows * OWN * columns),
        out_shape=jax.ShapeDtypeStruct((TERMS, R), F32),
        in_specs=[vmem],
        out_specs=vmem,
        compiler_params=params,
        name="total",
    )(shared)
    return local_moments, trace


def solution(mesh):
    placed = (P(None, None, "gx", "gy"), P(None, "gx", "gy"), P(None, "gx", "gy"), P())
    return jax.shard_map(
        local, mesh=mesh, in_specs=placed,
        out_specs=(P(None, None, "gx", "gy"), P()), check_vma=False,
    )
```

```python
import functools

import jax
import jax.numpy as jnp
from jax import lax
from jax.experimental import pallas as pl
from jax.experimental.pallas import tpu as pltpu
from jax.sharding import PartitionSpec as P

BLOCK = 128
R = 16
TERMS = 4
HALO = 4
BLOCKS = 4
LANES = BLOCK * (BLOCKS + 1)
OWN = BLOCK * BLOCKS
WIDTH_X = 8
ROWS_X = WIDTH_X + 2 * HALO
SLOT = 2 * WIDTH_X * R
EDGE = SLOT
SITE_EDGE = SLOT + R
SLOT_ROWS = SLOT + R + 8
NEAR = 2
PART = 2 * NEAR * R
PLANES = PART
SIDES = PLANES + 4 * 2 * NEAR
NEAR_MESSAGE = SIDES + 8
FAR_MESSAGE = SIDES

HOP_NEXT = 0.3
TWIST_COS = 0.4535961214255773
TWIST_SIN = 0.8912073600614354
SPREAD = 6.5
COS = HOP_NEXT * TWIST_COS
SIN = HOP_NEXT * TWIST_SIN
F32 = jnp.float32
BF16 = jnp.bfloat16


def bfloat16_terms(value):
    high = value.astype(BF16).astype(F32)
    rest = value - high
    middle = rest.astype(BF16).astype(F32)
    return high, middle, rest - middle


def site_planes(onsite, keep):
    return (*bfloat16_terms(onsite), keep)


def lane_index(rows, lanes):
    return lax.broadcasted_iota(jnp.int32, (rows, lanes), 1)


def pack_kernel(
    columns, plan_hbm, stored_hbm, disorder_hbm, vacancy_hbm, out, table,
    plan, stored, disorder, vacancy, turned, arrived,
):
    copies = [
        pltpu.make_async_copy(source, target, arrived.at[i])
        for i, (source, target) in enumerate(
            ((plan_hbm, plan), (stored_hbm, stored), (disorder_hbm, disorder), (vacancy_hbm, vacancy))
        )
    ]
    for copy in copies:
        copy.start()
    me = lax.axis_index("gy")
    first = me * BLOCKS
    total = BLOCKS * columns
    copies[0].wait()
    place = lane_index(1, total)
    listed = plan[...]
    spots = [
        jnp.sum(jnp.where(listed == first + b, place, 0), axis=1, keepdims=True)[0, 0]
        for b in range(BLOCKS)
    ]
    source = listed // BLOCKS
    wanted = [first + b for b in range(BLOCKS)]
    wanted += [(first + total - 1) % total, (first + BLOCKS) % total]
    for i, k in enumerate(wanted):
        row = jnp.sum(jnp.where(place == k, source, 0), axis=1, keepdims=True)
        table[i : i + 1, :] = jnp.broadcast_to(row, (1, BLOCK))
    copies[1].wait()
    for b in range(BLOCKS):
        block = stored[:, :, :, b * BLOCK : (b + 1) * BLOCK]
        turned[b] = block.reshape(2 * R * WIDTH_X, BLOCK).astype(F32)
    lane = lane_index(8, BLOCK)
    edges = [[jnp.zeros((8, BLOCK), F32) for _ in range(2)] for _ in range(BLOCKS)]
    slots = [spot // BLOCKS for spot in spots]
    for s in range(2):
        for x in range(WIDTH_X):
            q = s * WIDTH_X + x
            for b in range(BLOCKS):
                parts = []
                for h in range(2):
                    base = s * R * WIDTH_X + h * 8 * WIDTH_X + x
                    rows = turned[b, pl.ds(base, 8, stride=WIDTH_X), :]
                    parts.append(rows)
                    moved = pltpu.roll(rows, (8 * q + 4) % BLOCK, 1)
                    edges[b][h] = jnp.where(lane // 8 == q, moved, edges[b][h])
                both = jnp.concatenate(parts, axis=0).astype(BF16)
                out[slots[b], q * R : (q + 1) * R, :] = both
    last_half = lane_index(R, BLOCK) % 8 < 4
    for b in range(BLOCKS):
        spot = spots[b]
        edge = jnp.concatenate(edges[b], axis=0)

        @pl.when(spot % BLOCKS == BLOCKS - 1)
        def _():
            slot = ((spot + 1) // BLOCKS) % columns
            old = out[slot, EDGE : EDGE + R, :].astype(F32)
            out[slot, EDGE : EDGE + R, :] = jnp.where(last_half, edge, old).astype(BF16)

        @pl.when(spot % BLOCKS == 0)
        def _():
            slot = (spot // BLOCKS + columns - 1) % columns
            old = out[slot, EDGE : EDGE + R, :].astype(F32)
            out[slot, EDGE : EDGE + R, :] = jnp.where(last_half, old, edge).astype(BF16)

    copies[2].wait()
    copies[3].wait()
    lane16 = lane_index(R, BLOCK)
    ends = []
    for ref in (disorder, vacancy):
        low = ref[:, :, 0:BLOCK].reshape(R, BLOCK).astype(F32)
        high = ref[:, :, OWN - BLOCK : OWN].reshape(R, BLOCK).astype(F32)
        ends.append(jnp.where(lane16 < BLOCK // 2, low, high))
    sites = jnp.zeros((R, BLOCK), F32)
    for p, plane in enumerate(site_planes(ends[0], ends[1])):
        sites = jnp.where(lane16 // 8 == p, pltpu.roll(plane, 8 * p + 4, 1), sites)
    sites = jnp.where(lane < 32, sites[0:8], pltpu.roll(sites[8:16], 32, 1)).astype(BF16)
    out[(me + 1) % columns, SITE_EDGE : SITE_EDGE + 8, :] = sites
    out[(me + columns - 1) % columns, SITE_EDGE : SITE_EDGE + 8, :] = sites


def source_of(table, i):
    return table[i : i + 1, 0:1][0, 0]


def edge_tiles(columns, table, received):
    me = lax.axis_index("gy")
    left = source_of(table, BLOCKS)
    right = source_of(table, BLOCKS + 1)
    last_half = lane_index(R, BLOCK) % 8 < 4
    tile = jnp.where(
        last_half,
        received[left, EDGE : EDGE + R, :].astype(F32),
        received[right, EDGE : EDGE + R, :].astype(F32),
    )
    low = (me + columns - 1) % columns
    high = (me + 1) % columns
    sites = jnp.where(
        last_half[0:8],
        received[low, SITE_EDGE : SITE_EDGE + 8, :].astype(F32),
        received[high, SITE_EDGE : SITE_EDGE + 8, :].astype(F32),
    )
    return tile, sites


def arrange_kernel(
    columns, table, received, disorder, vacancy, low_near, high_near, low_far, high_far, planes
):
    outs = ((low_near, 0), (high_near, WIDTH_X - NEAR), (low_far, NEAR), (high_far, NEAR + NEAR))
    size = NEAR * R
    for b in range(BLOCKS):
        slot = source_of(table, b)
        lanes = slice(b * BLOCK, (b + 1) * BLOCK)
        for s in range(2):
            for out, x in outs:
                base = (s * WIDTH_X + x) * R
                out[s * size : (s + 1) * size, lanes] = received[slot, base : base + size, :]
    tile, sites = edge_tiles(columns, table, received)
    for out in (low_near, high_near):
        for i, part in enumerate((tile[0:8], tile[8:16], sites, sites)):
            out[SIDES : SIDES + 8, i * BLOCK : (i + 1) * BLOCK] = part.astype(BF16)
    for s in range(2):
        for p, plane in enumerate(site_planes(disorder[s], vacancy[s].astype(F32))):
            row = p * 2 * NEAR + s * NEAR
            for i, (_, x) in enumerate(outs):
                planes[i, row : row + NEAR, :] = plane[x : x + NEAR]
    for i, (out, _) in enumerate(outs):
        out[PLANES:SIDES, :] = planes[i].astype(BF16)


def fill_sites(level, factor, s, rows, onsite, kept, source, first):
    lane = lane_index(8, BLOCK)
    in_halo = (lane < HALO) | (lane >= BLOCK - HALO)
    side_level = jnp.zeros((8, BLOCK), F32)
    for p in range(3):
        side_level = side_level + pltpu.roll(source, BLOCK - 4 - 8 * p - 32 * s, 1)
    side_keep = pltpu.roll(source, BLOCK - 4 - 8 * 3 - 32 * s, 1)
    side_level = jnp.where(in_halo, side_level, 0.0)
    side_keep = jnp.where(in_halo, side_keep, 0.0)
    kept_rows = []
    for i, row in enumerate(rows):
        j = first + i
        lev = jnp.concatenate([onsite[i : i + 1], side_level[j : j + 1]], axis=1)
        kep = jnp.concatenate([kept[i : i + 1], side_keep[j : j + 1]], axis=1)
        level[s, row] = jnp.broadcast_to(lev * (1.0 / COS), (8, LANES))
        kep = jnp.broadcast_to(kep, (8, LANES))
        factor[s, row] = kep * (2.0 * COS / SPREAD)
        kept_rows.append(kep)
    return kept_rows


def unpack_rows(message, near, level, factor, start, base, x):
    planes = message[PLANES:SIDES, :].astype(F32)
    sides = near[SIDES : SIDES + 8, :].astype(F32)
    tile = jnp.concatenate([sides[:, 0:BLOCK], sides[:, BLOCK : 2 * BLOCK]], axis=0)
    sites = sides[:, 2 * BLOCK : 3 * BLOCK]
    step = 2 * NEAR
    onsite = planes[0:step] + planes[step : 2 * step] + planes[2 * step : 3 * step]
    keep = planes[3 * step : 4 * step]
    for s in range(2):
        some = slice(s * NEAR, (s + 1) * NEAR)
        kept = fill_sites(
            level, factor, s, range(base, base + NEAR), onsite[some], keep[some], sites, x
        )
        for i in range(NEAR):
            index = (s * NEAR + i) * R
            q = s * WIDTH_X + x + i
            side = pltpu.roll(tile, (BLOCK - 4 - 8 * q) % BLOCK, 1)
            value = jnp.concatenate([message[index : index + R, :].astype(F32), side], axis=1)
            for h in range(2):
                part = slice(h * 8, (h + 1) * 8)
                start[s, base + i, part, :] = value[part] * kept[i]


def span(level, factor, term, old, now, new, row, count=2, width=LANES):
    own = slice(0, width)
    for h in range(2):
        part = slice(h * 8, (h + 1) * 8)
        near_rows = range(-1, count + 1)
        real = [{d: now[0][s, row + d, part, :] for d in near_rows} for s in range(2)]
        fields = [real]
        if now[1] is not None:
            fields.append([{d: now[1][s, row + d, part, :] for d in near_rows} for s in range(2)])
        others = [
            [{d: f[s][d] * (1.0 / COS) for d in near_rows} for s in range(2)] for f in fields
        ]
        for s in range(2):
            ratio = SIN / COS if s == 0 else -SIN / COS
            turn = [{d: f[s][d] * ratio for d in near_rows} for f in fields]
            if len(fields) == 1:
                ahead = [real[s], turn[0]]
                back = [real[s], {d: -turn[0][d] for d in near_rows}]
            else:
                imag = fields[1][s]
                ahead = [
                    {d: real[s][d] - turn[1][d] for d in near_rows},
                    {d: imag[d] + turn[0][d] for d in near_rows},
                ]
                back = [
                    {d: real[s][d] + turn[1][d] for d in near_rows},
                    {d: imag[d] - turn[0][d] for d in near_rows},
                ]
            for c in range(2):
                if new[c] is None:
                    continue
                joint = {d: ahead[c][d - 1] + back[c][d] for d in range(count + 1)}
                for d in range(count):
                    out = ahead[c][d + 1][:, own] + back[c][d - 1][:, own]
                    up, down = joint[d], joint[d + 1]
                    if c < len(fields):
                        other = others[c][1 - s]
                        aside = d - 1 if s == 0 else d + 1
                        out = out + level[s, row + d][:, own] * fields[c][s][d][:, own]
                        out = out - (other[d] + other[aside])[:, own]
                        if s == 0:
                            down = down - other[d]
                        else:
                            up = up - other[d]
                    out = out + pltpu.roll(up, LANES - 1, 1)[:, own]
                    out = out + pltpu.roll(down, 1, 1)[:, own]
                    scale = factor[s, row + d][:, own]
                    out = out * (scale * 0.5 if term == 1 else scale)
                    if term > 1 and old[c] is not None:
                        out = out - old[c][s, row + d, part, own]
                    new[c][s, row + d, part, own] = out


def fold(product):
    lanes = product[:, 0:BLOCK]
    for b in range(1, BLOCKS):
        lanes = lanes + product[:, b * BLOCK : (b + 1) * BLOCK]
    return lanes


def trace_row(start, first, second, row, sums):
    own = slice(0, OWN)
    sums = list(sums)
    for h in range(2):
        part = slice(h * 8, (h + 1) * 8)
        for s in range(2):
            v0 = start[s, row, part, own]
            r1 = first[0][s, row, part, own]
            i1 = first[1][s, row, part, own]
            r2 = second[0][s, row, part, own]
            i2 = second[1][s, row, part, own]
            terms = (v0 * v0, v0 * r1, v0 * r2, r1 * r2 + i1 * i2, r2 * r2 + i2 * i2)
            for n, term in enumerate(terms):
                sums[n * 2 + h] = sums[n * 2 + h] + fold(term)
    return tuple(sums)


SUMS = 5


class Rows:
    def __init__(self, ref, first):
        self.ref = ref
        self.first = first

    def __getitem__(self, index):
        s, row, *rest = index
        return self.ref[(s, row - self.first, *rest)]

    def __setitem__(self, index, value):
        s, row, *rest = index
        self.ref[(s, row - self.first, *rest)] = value


class Joined:
    def __init__(self, *pieces):
        self.at = {row: (ref, i) for ref, rows in pieces for i, row in enumerate(rows)}

    def __getitem__(self, index):
        s, row, *rest = index
        ref, i = self.at[row]
        return ref[(s, i, *rest)]

    def __setitem__(self, index, value):
        s, row, *rest = index
        ref, i = self.at[row]
        ref[(s, i, *rest)] = value


OWN_ROWS = range(HALO, HALO + WIDTH_X)
NEAR_ROWS = (2, 3, 12, 13)
FIRST_ROWS = range(5, 11)
FIRST_BORDER = (3, 4, 11, 12)
SECOND_ROWS = range(6, 10)
SECOND_BORDER = (4, 5, 10, 11)


def interior_kernel(
    columns, table, received, disorder, vacancy,
    level, factor, start, real1, imag1, real2, imag2, sums, own_sites, own_start,
):
    own_level, own_factor = level, factor
    level, factor, start = (Rows(ref, HALO) for ref in (level, factor, start))
    real1, imag1 = (Rows(ref, FIRST_ROWS[0]) for ref in (real1, imag1))
    real2, imag2 = (Rows(ref, SECOND_ROWS[0]) for ref in (real2, imag2))
    tile, sites = edge_tiles(columns, table, received)
    slots = [source_of(table, b) for b in range(BLOCKS)]
    for s in range(2):
        kept = fill_sites(
            level, factor, s, range(HALO, HALO + WIDTH_X), disorder[s],
            vacancy[s].astype(F32), sites, 0,
        )
        for x in range(WIDTH_X):
            q = s * WIDTH_X + x
            pieces = [received[slots[b], q * R : (q + 1) * R, :].astype(F32) for b in range(BLOCKS)]
            pieces.append(pltpu.roll(tile, (BLOCK - 4 - 8 * q) % BLOCK, 1))
            value = jnp.concatenate(pieces, axis=1)
            value = value * jnp.concatenate([kept[x], kept[x]], axis=0)
            start[s, HALO + x] = value
            own_start[s, x] = value.astype(BF16)
            own_sites[0, s, x : x + 1, :] = own_level[s, x, 0:1, :]
            own_sites[1, s, x : x + 1, :] = own_factor[s, x, 0:1, :]

    def one(i, carry):
        row = HALO + 1 + 2 * i
        span(level, factor, 1, None, (start, None), (real1, imag1), row)
        return carry

    lax.fori_loop(0, 3, one, 0)

    def two(i, carry):
        row = HALO + 2 + 2 * i
        span(level, factor, 2, (start, None), (real1, imag1), (real2, imag2), row, width=OWN)
        for d in range(2):
            carry = trace_row(start, (real1, imag1), (real2, imag2), row + d, carry)
        return carry

    zero = jnp.zeros((8, BLOCK), F32)
    totals = lax.fori_loop(0, 2, two, (zero,) * (2 * SUMS))
    for i, total in enumerate(totals):
        sums[i * 8 : (i + 1) * 8, :] = total


def border_kernel(
    below, above,
    own_level, own_factor, own_start, own_real1, own_imag1, own_real2, own_imag2, sums_in,
    trace_out,
    near_level, near_factor, near_start, border_real1, border_imag1, border_real2, border_imag2,
):
    level = Joined((own_level, OWN_ROWS), (near_level, NEAR_ROWS))
    factor = Joined((own_factor, OWN_ROWS), (near_factor, NEAR_ROWS))
    start = Joined((own_start, OWN_ROWS), (near_start, NEAR_ROWS))
    real1 = Joined((own_real1, FIRST_ROWS), (border_real1, FIRST_BORDER))
    imag1 = Joined((own_imag1, FIRST_ROWS), (border_imag1, FIRST_BORDER))
    real2 = Joined((own_real2, SECOND_ROWS), (border_real2, SECOND_BORDER))
    imag2 = Joined((own_imag2, SECOND_ROWS), (border_imag2, SECOND_BORDER))
    unpack_rows(below, below, level, factor, start, HALO - NEAR, WIDTH_X - NEAR)
    unpack_rows(above, above, level, factor, start, HALO + WIDTH_X, 0)
    for row in (HALO - 1, HALO + WIDTH_X - 1):
        span(level, factor, 1, None, (start, None), (real1, imag1), row)
    totals = tuple(sums_in[i * 8 : (i + 1) * 8, :] for i in range(2 * SUMS))
    for row in (HALO, HALO + WIDTH_X - 2):
        span(level, factor, 2, (start, None), (real1, imag1), (real2, imag2), row, width=OWN)
        for d in range(2):
            totals = trace_row(start, (real1, imag1), (real2, imag2), row + d, totals)
    norm, one_one, one_two, both, second = (
        jnp.concatenate(totals[2 * n : 2 * n + 2], axis=0) for n in range(SUMS)
    )
    moments = jnp.concatenate(
        [one_one, one_two, 2.0 * both - one_one, 2.0 * second - norm], axis=0
    )
    ones = jnp.ones((8, BLOCK), BF16)
    total = jnp.zeros((8, TERMS * R), F32)
    for term in bfloat16_terms(moments):
        total = total + lax.dot_general(
            ones, term.astype(BF16), (((1,), (1,)), ((), ())), preferred_element_type=F32
        )
    for i in range(trace_out.shape[0] // 8):
        trace_out[i * 8 : (i + 1) * 8, :] = total


def local_kernel(
    below, above, below_far, above_far, own_sites, own_start,
    local_out, level, factor, start, real1, imag1, real2, imag2, real3, imag3, real4, products,
):
    real4 = Rows(real4, HALO)
    for s in range(2):
        for x in range(WIDTH_X):
            row = HALO + x
            level[s, row] = jnp.broadcast_to(own_sites[0, s, x : x + 1, :], (8, LANES))
            factor[s, row] = jnp.broadcast_to(own_sites[1, s, x : x + 1, :], (8, LANES))
            start[s, row] = own_start[s, x].astype(F32)
    unpack_rows(below_far, below, level, factor, start, 0, WIDTH_X - HALO)
    unpack_rows(below, below, level, factor, start, NEAR, WIDTH_X - NEAR)
    unpack_rows(above, above, level, factor, start, HALO + WIDTH_X, 0)
    unpack_rows(above_far, above, level, factor, start, HALO + WIDTH_X + NEAR, NEAR)

    def one(i, carry):
        span(level, factor, 1, None, (start, None), (real1, imag1), 2 * i + 1)
        return carry

    lax.fori_loop(0, 7, one, 0)

    def two(i, carry):
        span(level, factor, 2, (start, None), (real1, imag1), (real2, imag2), 2 * i + 2)
        return carry

    lax.fori_loop(0, 6, two, 0)

    def three(i, carry):
        span(level, factor, 3, (real1, imag1), (real2, imag2), (real3, imag3), 2 * i + 3)
        return carry

    lax.fori_loop(0, 5, three, 0)

    def four(i, carry):
        row = 2 * i + HALO
        span(level, factor, 4, (real2, imag2), (real3, imag3), (real4, None), row, width=OWN)
        for d in range(2):
            for s in range(2):
                for n, ref in enumerate((real1, real2, real3, real4)):
                    total = None
                    for h in range(2):
                        index = (s, row + d, slice(h * 8, (h + 1) * 8), slice(0, OWN))
                        product = start[index] * ref[index]
                        total = product if h == 0 else total + product
                    for b in range(BLOCKS):
                        products[n, s, b, pl.ds(8 * (2 * i + d), 8), :] = (
                            total[:, b * BLOCK : (b + 1) * BLOCK]
                        )
        return carry

    lax.fori_loop(0, WIDTH_X // 2, four, 0)
    for n in range(TERMS):
        for s in range(2):
            for b in range(BLOCKS):
                total = products[n, s, b, pl.ds(0, WIDTH_X, stride=8), :]
                for r in range(1, 8):
                    total = total + products[n, s, b, pl.ds(r, WIDTH_X, stride=8), :]
                local_out[n, s, :, b * BLOCK : (b + 1) * BLOCK] = total * (1.0 / R)


def total_kernel(sites, shared, out):
    total = jnp.sum(shared[...], axis=0, keepdims=True) * (1.0 / sites)
    for n in range(TERMS):
        out[n : n + 1, :] = total[:, n * R : (n + 1) * R]


def local(stored_vectors, disorder, vacancy, plan):
    columns = lax.axis_size("gy")
    rows = lax.axis_size("gx")
    devices = rows * columns
    vmem = pl.BlockSpec(memory_space=pltpu.VMEM)
    params = pltpu.CompilerParams(vmem_limit_bytes=8 * 1024 * 1024)

    hbm = pl.BlockSpec(memory_space=pltpu.HBM)
    outgoing, table = pl.pallas_call(
        functools.partial(pack_kernel, columns),
        out_shape=(
            jax.ShapeDtypeStruct((columns, SLOT_ROWS, BLOCK), BF16),
            jax.ShapeDtypeStruct((8, BLOCK), jnp.int32),
        ),
        in_specs=[hbm] * 4,
        out_specs=(vmem, vmem),
        scratch_shapes=[
            pltpu.VMEM((1,) + plan.shape, plan.dtype),
            pltpu.VMEM(stored_vectors.shape, stored_vectors.dtype),
            pltpu.VMEM(disorder.shape, disorder.dtype),
            pltpu.VMEM(vacancy.shape, vacancy.dtype),
            pltpu.VMEM((BLOCKS, 2 * R * WIDTH_X, BLOCK), F32),
            pltpu.SemaphoreType.DMA((4,)),
        ],
        compiler_params=pltpu.CompilerParams(vmem_limit_bytes=16 * 1024 * 1024),
        name="pack",
    )(*(
        pltpu.with_memory_space_constraint(x, pltpu.HBM)
        for x in (plan[None], stored_vectors, disorder, vacancy)
    ))
    received = lax.all_to_all(outgoing, "gy", split_axis=0, concat_axis=0, tiled=True)

    near_message = jax.ShapeDtypeStruct((NEAR_MESSAGE, OWN), BF16)
    far_message = jax.ShapeDtypeStruct((FAR_MESSAGE, OWN), BF16)
    low_near, high_near, low_far, high_far = pl.pallas_call(
        functools.partial(arrange_kernel, columns),
        out_shape=(near_message, near_message, far_message, far_message),
        in_specs=[vmem] * 4,
        out_specs=(vmem,) * 4,
        scratch_shapes=[pltpu.VMEM((4, 4 * 2 * NEAR, OWN), F32)],
        compiler_params=params,
        name="arrange",
    )(table, received, disorder, vacancy)
    up = [(i, (i + 1) % rows) for i in range(rows)]
    down = [(target, source) for source, target in up]
    below = lax.ppermute(high_near, "gx", up)
    above = lax.ppermute(low_near, "gx", down)
    below_far = lax.ppermute(high_far, "gx", up)
    above_far = lax.ppermute(low_far, "gx", down)

    def site(count):
        return jax.ShapeDtypeStruct((2, count, 8, LANES), F32)

    def field(count):
        return jax.ShapeDtypeStruct((2, count, R, LANES), F32)

    def scratch(shape):
        return pltpu.VMEM(shape.shape, shape.dtype)

    *inner, own_sites, own_start = pl.pallas_call(
        functools.partial(interior_kernel, columns),
        out_shape=(site(WIDTH_X), site(WIDTH_X), field(WIDTH_X))
        + (field(len(FIRST_ROWS)),) * 2
        + (field(len(SECOND_ROWS)),) * 2
        + (
            jax.ShapeDtypeStruct((2 * SUMS * 8, BLOCK), F32),
            jax.ShapeDtypeStruct((2, 2, WIDTH_X, LANES), F32),
            jax.ShapeDtypeStruct((2, WIDTH_X, R, LANES), BF16),
        ),
        in_specs=[vmem] * 4,
        out_specs=(vmem,) * 10,
        compiler_params=params,
        cost_estimate=pl.CostEstimate(flops=10**7, bytes_accessed=8 * 10**6, transcendentals=0),
        name="interior",
    )(table, received, disorder, vacancy)
    partial = pl.pallas_call(
        border_kernel,
        out_shape=jax.ShapeDtypeStruct((devices, TERMS * R), F32),
        in_specs=[vmem] * 10,
        out_specs=vmem,
        scratch_shapes=[scratch(site(len(NEAR_ROWS)))] * 2
        + [scratch(field(len(NEAR_ROWS)))]
        + [scratch(field(len(FIRST_BORDER)))] * 2
        + [scratch(field(len(SECOND_BORDER)))] * 2,
        compiler_params=params,
        name="border",
    )(below, above, *inner)
    shared = lax.all_to_all(partial, ("gx", "gy"), split_axis=0, concat_axis=0, tiled=True)
    local_moments = pl.pallas_call(
        local_kernel,
        out_shape=jax.ShapeDtypeStruct((TERMS, 2, WIDTH_X, OWN), F32),
        in_specs=[vmem] * 6,
        out_specs=vmem,
        scratch_shapes=[scratch(site(ROWS_X))] * 2
        + [scratch(field(ROWS_X))] * 7
        + [
            scratch(field(WIDTH_X)),
            pltpu.VMEM((TERMS, 2, BLOCKS, 8 * WIDTH_X, BLOCK), F32),
        ],
        compiler_params=pltpu.CompilerParams(vmem_limit_bytes=16 * 1024 * 1024),
        cost_estimate=pl.CostEstimate(flops=10**7, bytes_accessed=8 * 10**6, transcendentals=0),
        name="local_moments",
    )(below, above, below_far, above_far, own_sites, own_start)
    trace = pl.pallas_call(
        functools.partial(total_kernel, 2 * WIDTH_X * rows * OWN * columns),
        out_shape=jax.ShapeDtypeStruct((TERMS, R), F32),
        in_specs=[vmem],
        out_specs=vmem,
        compiler_params=params,
        name="total",
    )(shared)
    return local_moments, trace


def solution(mesh):
    placed = (P(None, None, "gx", "gy"), P(None, "gx", "gy"), P(None, "gx", "gy"), P())
    return jax.shard_map(
        local, mesh=mesh, in_specs=placed,
        out_specs=(P(None, None, "gx", "gy"), P()), check_vma=False,
    )
```

```python
import functools

import jax
import jax.numpy as jnp
from jax import lax
from jax.experimental import pallas as pl
from jax.experimental.pallas import tpu as pltpu
from jax.sharding import PartitionSpec as P

BLOCK = 128
R = 16
TERMS = 4
HALO = 4
BLOCKS = 4
LANES = BLOCK * (BLOCKS + 1)
OWN = BLOCK * BLOCKS
WIDTH_X = 8
ROWS_X = WIDTH_X + 2 * HALO
SLOT = 2 * WIDTH_X * R
EDGE = SLOT
SITE_EDGE = SLOT + R
SLOT_ROWS = SLOT + R + 8
NEAR = 2
PART = 2 * NEAR * R
PLANES = PART
SIDES = PLANES + 4 * 2 * NEAR
NEAR_MESSAGE = SIDES + 8
FAR_MESSAGE = SIDES

HOP_NEXT = 0.3
TWIST_COS = 0.4535961214255773
TWIST_SIN = 0.8912073600614354
SPREAD = 6.5
COS = HOP_NEXT * TWIST_COS
SIN = HOP_NEXT * TWIST_SIN
F32 = jnp.float32
BF16 = jnp.bfloat16


def bfloat16_terms(value):
    high = value.astype(BF16).astype(F32)
    rest = value - high
    middle = rest.astype(BF16).astype(F32)
    return high, middle, rest - middle


def site_planes(onsite, keep):
    return (*bfloat16_terms(onsite), keep)


def lane_index(rows, lanes):
    return lax.broadcasted_iota(jnp.int32, (rows, lanes), 1)


def pack_kernel(
    columns, plan_hbm, stored_hbm, disorder_hbm, vacancy_hbm, out, table,
    plan, stored, disorder, vacancy, turned, arrived,
):
    copies = [
        pltpu.make_async_copy(source, target, arrived.at[i])
        for i, (source, target) in enumerate(
            ((plan_hbm, plan), (stored_hbm, stored), (disorder_hbm, disorder), (vacancy_hbm, vacancy))
        )
    ]
    for copy in copies:
        copy.start()
    me = lax.axis_index("gy")
    first = me * BLOCKS
    total = BLOCKS * columns
    copies[0].wait()
    place = lane_index(1, total)
    listed = plan[...]
    spots = [
        jnp.sum(jnp.where(listed == first + b, place, 0), axis=1, keepdims=True)[0, 0]
        for b in range(BLOCKS)
    ]
    source = listed // BLOCKS
    wanted = [first + b for b in range(BLOCKS)]
    wanted += [(first + total - 1) % total, (first + BLOCKS) % total]
    for i, k in enumerate(wanted):
        row = jnp.sum(jnp.where(place == k, source, 0), axis=1, keepdims=True)
        table[i : i + 1, :] = jnp.broadcast_to(row, (1, BLOCK))
    copies[1].wait()
    for b in range(BLOCKS):
        block = stored[:, :, :, b * BLOCK : (b + 1) * BLOCK]
        turned[b] = block.reshape(2 * R * WIDTH_X, BLOCK).astype(F32)
    lane = lane_index(8, BLOCK)
    edges = [[jnp.zeros((8, BLOCK), F32) for _ in range(2)] for _ in range(BLOCKS)]
    slots = [spot // BLOCKS for spot in spots]
    for s in range(2):
        for x in range(WIDTH_X):
            q = s * WIDTH_X + x
            for b in range(BLOCKS):
                parts = []
                for h in range(2):
                    base = s * R * WIDTH_X + h * 8 * WIDTH_X + x
                    rows = turned[b, pl.ds(base, 8, stride=WIDTH_X), :]
                    parts.append(rows)
                    moved = pltpu.roll(rows, (8 * q + 4) % BLOCK, 1)
                    edges[b][h] = jnp.where(lane // 8 == q, moved, edges[b][h])
                both = jnp.concatenate(parts, axis=0).astype(BF16)
                out[slots[b], q * R : (q + 1) * R, :] = both
    last_half = lane_index(R, BLOCK) % 8 < 4
    for b in range(BLOCKS):
        spot = spots[b]
        edge = jnp.concatenate(edges[b], axis=0)

        @pl.when(spot % BLOCKS == BLOCKS - 1)
        def _():
            slot = ((spot + 1) // BLOCKS) % columns
            old = out[slot, EDGE : EDGE + R, :].astype(F32)
            out[slot, EDGE : EDGE + R, :] = jnp.where(last_half, edge, old).astype(BF16)

        @pl.when(spot % BLOCKS == 0)
        def _():
            slot = (spot // BLOCKS + columns - 1) % columns
            old = out[slot, EDGE : EDGE + R, :].astype(F32)
            out[slot, EDGE : EDGE + R, :] = jnp.where(last_half, old, edge).astype(BF16)

    copies[2].wait()
    copies[3].wait()
    lane16 = lane_index(R, BLOCK)
    ends = []
    for ref in (disorder, vacancy):
        low = ref[:, :, 0:BLOCK].reshape(R, BLOCK).astype(F32)
        high = ref[:, :, OWN - BLOCK : OWN].reshape(R, BLOCK).astype(F32)
        ends.append(jnp.where(lane16 < BLOCK // 2, low, high))
    sites = jnp.zeros((R, BLOCK), F32)
    for p, plane in enumerate(site_planes(ends[0], ends[1])):
        sites = jnp.where(lane16 // 8 == p, pltpu.roll(plane, 8 * p + 4, 1), sites)
    sites = jnp.where(lane < 32, sites[0:8], pltpu.roll(sites[8:16], 32, 1)).astype(BF16)
    out[(me + 1) % columns, SITE_EDGE : SITE_EDGE + 8, :] = sites
    out[(me + columns - 1) % columns, SITE_EDGE : SITE_EDGE + 8, :] = sites


def source_of(table, i):
    return table[i : i + 1, 0:1][0, 0]


def edge_tiles(columns, table, received):
    me = lax.axis_index("gy")
    left = source_of(table, BLOCKS)
    right = source_of(table, BLOCKS + 1)
    last_half = lane_index(R, BLOCK) % 8 < 4
    tile = jnp.where(
        last_half,
        received[left, EDGE : EDGE + R, :].astype(F32),
        received[right, EDGE : EDGE + R, :].astype(F32),
    )
    low = (me + columns - 1) % columns
    high = (me + 1) % columns
    sites = jnp.where(
        last_half[0:8],
        received[low, SITE_EDGE : SITE_EDGE + 8, :].astype(F32),
        received[high, SITE_EDGE : SITE_EDGE + 8, :].astype(F32),
    )
    return tile, sites


def arrange_kernel(
    columns, table, received, disorder, vacancy, low_near, high_near, low_far, high_far, planes
):
    outs = ((low_near, 0), (high_near, WIDTH_X - NEAR), (low_far, NEAR), (high_far, NEAR + NEAR))
    size = NEAR * R
    for b in range(BLOCKS):
        slot = source_of(table, b)
        lanes = slice(b * BLOCK, (b + 1) * BLOCK)
        for s in range(2):
            for out, x in outs:
                base = (s * WIDTH_X + x) * R
                out[s * size : (s + 1) * size, lanes] = received[slot, base : base + size, :]
    tile, sites = edge_tiles(columns, table, received)
    for out in (low_near, high_near):
        for i, part in enumerate((tile[0:8], tile[8:16], sites, sites)):
            out[SIDES : SIDES + 8, i * BLOCK : (i + 1) * BLOCK] = part.astype(BF16)
    for s in range(2):
        for p, plane in enumerate(site_planes(disorder[s], vacancy[s].astype(F32))):
            row = p * 2 * NEAR + s * NEAR
            for i, (_, x) in enumerate(outs):
                planes[i, row : row + NEAR, :] = plane[x : x + NEAR]
    for i, (out, _) in enumerate(outs):
        out[PLANES:SIDES, :] = planes[i].astype(BF16)


def fill_sites(level, factor, s, rows, onsite, kept, source, first):
    lane = lane_index(8, BLOCK)
    in_halo = (lane < HALO) | (lane >= BLOCK - HALO)
    side_level = jnp.zeros((8, BLOCK), F32)
    for p in range(3):
        side_level = side_level + pltpu.roll(source, BLOCK - 4 - 8 * p - 32 * s, 1)
    side_keep = pltpu.roll(source, BLOCK - 4 - 8 * 3 - 32 * s, 1)
    side_level = jnp.where(in_halo, side_level, 0.0)
    side_keep = jnp.where(in_halo, side_keep, 0.0)
    kept_rows = []
    for i, row in enumerate(rows):
        j = first + i
        lev = jnp.concatenate([onsite[i : i + 1], side_level[j : j + 1]], axis=1)
        kep = jnp.concatenate([kept[i : i + 1], side_keep[j : j + 1]], axis=1)
        level[s, row] = jnp.broadcast_to(lev * (1.0 / COS), (8, LANES))
        kep = jnp.broadcast_to(kep, (8, LANES))
        factor[s, row] = kep * (2.0 * COS / SPREAD)
        kept_rows.append(kep)
    return kept_rows


def unpack_rows(message, near, level, factor, start, base, x):
    planes = message[PLANES:SIDES, :].astype(F32)
    sides = near[SIDES : SIDES + 8, :].astype(F32)
    tile = jnp.concatenate([sides[:, 0:BLOCK], sides[:, BLOCK : 2 * BLOCK]], axis=0)
    sites = sides[:, 2 * BLOCK : 3 * BLOCK]
    step = 2 * NEAR
    onsite = planes[0:step] + planes[step : 2 * step] + planes[2 * step : 3 * step]
    keep = planes[3 * step : 4 * step]
    for s in range(2):
        some = slice(s * NEAR, (s + 1) * NEAR)
        kept = fill_sites(
            level, factor, s, range(base, base + NEAR), onsite[some], keep[some], sites, x
        )
        for i in range(NEAR):
            index = (s * NEAR + i) * R
            q = s * WIDTH_X + x + i
            side = pltpu.roll(tile, (BLOCK - 4 - 8 * q) % BLOCK, 1)
            value = jnp.concatenate([message[index : index + R, :].astype(F32), side], axis=1)
            for h in range(2):
                part = slice(h * 8, (h + 1) * 8)
                start[s, base + i, part, :] = value[part] * kept[i]


def span(level, factor, term, old, now, new, row, count=2, width=LANES):
    own = slice(0, width)
    for h in range(2):
        part = slice(h * 8, (h + 1) * 8)
        near_rows = range(-1, count + 1)
        real = [{d: now[0][s, row + d, part, :] for d in near_rows} for s in range(2)]
        fields = [real]
        if now[1] is not None:
            fields.append([{d: now[1][s, row + d, part, :] for d in near_rows} for s in range(2)])
        others = [
            [{d: f[s][d] * (1.0 / COS) for d in near_rows} for s in range(2)] for f in fields
        ]
        for s in range(2):
            ratio = SIN / COS if s == 0 else -SIN / COS
            turn = [{d: f[s][d] * ratio for d in near_rows} for f in fields]
            if len(fields) == 1:
                ahead = [real[s], turn[0]]
                back = [real[s], {d: -turn[0][d] for d in near_rows}]
            else:
                imag = fields[1][s]
                ahead = [
                    {d: real[s][d] - turn[1][d] for d in near_rows},
                    {d: imag[d] + turn[0][d] for d in near_rows},
                ]
                back = [
                    {d: real[s][d] + turn[1][d] for d in near_rows},
                    {d: imag[d] - turn[0][d] for d in near_rows},
                ]
            for c in range(2):
                if new[c] is None:
                    continue
                joint = {d: ahead[c][d - 1] + back[c][d] for d in range(count + 1)}
                for d in range(count):
                    out = ahead[c][d + 1][:, own] + back[c][d - 1][:, own]
                    up, down = joint[d], joint[d + 1]
                    if c < len(fields):
                        other = others[c][1 - s]
                        aside = d - 1 if s == 0 else d + 1
                        out = out + level[s, row + d][:, own] * fields[c][s][d][:, own]
                        out = out - (other[d] + other[aside])[:, own]
                        if s == 0:
                            down = down - other[d]
                        else:
                            up = up - other[d]
                    out = out + pltpu.roll(up, LANES - 1, 1)[:, own]
                    out = out + pltpu.roll(down, 1, 1)[:, own]
                    scale = factor[s, row + d][:, own]
                    out = out * (scale * 0.5 if term == 1 else scale)
                    if term > 1 and old[c] is not None:
                        out = out - old[c][s, row + d, part, own]
                    new[c][s, row + d, part, own] = out


def fold(product):
    lanes = product[:, 0:BLOCK]
    for b in range(1, BLOCKS):
        lanes = lanes + product[:, b * BLOCK : (b + 1) * BLOCK]
    return lanes


def trace_row(start, first, second, row, sums):
    own = slice(0, OWN)
    sums = list(sums)
    for h in range(2):
        part = slice(h * 8, (h + 1) * 8)
        for s in range(2):
            v0 = start[s, row, part, own]
            r1 = first[0][s, row, part, own]
            i1 = first[1][s, row, part, own]
            r2 = second[0][s, row, part, own]
            i2 = second[1][s, row, part, own]
            terms = (v0 * v0, v0 * r1, v0 * r2, r1 * r2 + i1 * i2, r2 * r2 + i2 * i2)
            for n, term in enumerate(terms):
                sums[n * 2 + h] = sums[n * 2 + h] + fold(term)
    return tuple(sums)


SUMS = 5


class Rows:
    def __init__(self, ref, first):
        self.ref = ref
        self.first = first

    def __getitem__(self, index):
        s, row, *rest = index
        return self.ref[(s, row - self.first, *rest)]

    def __setitem__(self, index, value):
        s, row, *rest = index
        self.ref[(s, row - self.first, *rest)] = value


class Joined:
    def __init__(self, *pieces):
        self.at = {row: (ref, i) for ref, rows in pieces for i, row in enumerate(rows)}

    def __getitem__(self, index):
        s, row, *rest = index
        ref, i = self.at[row]
        return ref[(s, i, *rest)]

    def __setitem__(self, index, value):
        s, row, *rest = index
        ref, i = self.at[row]
        ref[(s, i, *rest)] = value


OWN_ROWS = range(HALO, HALO + WIDTH_X)
NEAR_ROWS = (2, 3, 12, 13)
FIRST_ROWS = range(5, 11)
FIRST_BORDER = (3, 4, 11, 12)
SECOND_ROWS = range(6, 10)
SECOND_BORDER = (4, 5, 10, 11)


def interior_kernel(
    columns, table, received, disorder, vacancy,
    level, factor, start, real1, imag1, real2, imag2, sums, own_sites, own_start,
):
    own_level, own_factor = level, factor
    level, factor, start = (Rows(ref, HALO) for ref in (level, factor, start))
    real1, imag1 = (Rows(ref, FIRST_ROWS[0]) for ref in (real1, imag1))
    real2, imag2 = (Rows(ref, SECOND_ROWS[0]) for ref in (real2, imag2))
    tile, sites = edge_tiles(columns, table, received)
    slots = [source_of(table, b) for b in range(BLOCKS)]
    for s in range(2):
        kept = fill_sites(
            level, factor, s, range(HALO, HALO + WIDTH_X), disorder[s],
            vacancy[s].astype(F32), sites, 0,
        )
        for x in range(WIDTH_X):
            q = s * WIDTH_X + x
            pieces = [received[slots[b], q * R : (q + 1) * R, :].astype(F32) for b in range(BLOCKS)]
            pieces.append(pltpu.roll(tile, (BLOCK - 4 - 8 * q) % BLOCK, 1))
            value = jnp.concatenate(pieces, axis=1)
            value = value * jnp.concatenate([kept[x], kept[x]], axis=0)
            start[s, HALO + x] = value
            own_start[s, x] = value.astype(BF16)
            own_sites[0, s, x : x + 1, :] = own_level[s, x, 0:1, :]
            own_sites[1, s, x : x + 1, :] = own_factor[s, x, 0:1, :]

    def one(i, carry):
        row = HALO + 1 + 2 * i
        span(level, factor, 1, None, (start, None), (real1, imag1), row)
        return carry

    lax.fori_loop(0, 3, one, 0)

    def two(i, carry):
        row = HALO + 2 + 2 * i
        span(level, factor, 2, (start, None), (real1, imag1), (real2, imag2), row, width=OWN)
        for d in range(2):
            carry = trace_row(start, (real1, imag1), (real2, imag2), row + d, carry)
        return carry

    zero = jnp.zeros((8, BLOCK), F32)
    totals = lax.fori_loop(0, 2, two, (zero,) * (2 * SUMS))
    for i, total in enumerate(totals):
        sums[i * 8 : (i + 1) * 8, :] = total


def border_kernel(
    below, above,
    own_level, own_factor, own_start, own_real1, own_imag1, own_real2, own_imag2, sums_in,
    trace_out,
    near_level, near_factor, near_start, border_real1, border_imag1, border_real2, border_imag2,
):
    level = Joined((own_level, OWN_ROWS), (near_level, NEAR_ROWS))
    factor = Joined((own_factor, OWN_ROWS), (near_factor, NEAR_ROWS))
    start = Joined((own_start, OWN_ROWS), (near_start, NEAR_ROWS))
    real1 = Joined((own_real1, FIRST_ROWS), (border_real1, FIRST_BORDER))
    imag1 = Joined((own_imag1, FIRST_ROWS), (border_imag1, FIRST_BORDER))
    real2 = Joined((own_real2, SECOND_ROWS), (border_real2, SECOND_BORDER))
    imag2 = Joined((own_imag2, SECOND_ROWS), (border_imag2, SECOND_BORDER))
    unpack_rows(below, below, level, factor, start, HALO - NEAR, WIDTH_X - NEAR)
    unpack_rows(above, above, level, factor, start, HALO + WIDTH_X, 0)
    for row in (HALO - 1, HALO + WIDTH_X - 1):
        span(level, factor, 1, None, (start, None), (real1, imag1), row)
    totals = tuple(sums_in[i * 8 : (i + 1) * 8, :] for i in range(2 * SUMS))
    for row in (HALO, HALO + WIDTH_X - 2):
        span(level, factor, 2, (start, None), (real1, imag1), (real2, imag2), row, width=OWN)
        for d in range(2):
            totals = trace_row(start, (real1, imag1), (real2, imag2), row + d, totals)
    norm, one_one, one_two, both, second = (
        jnp.concatenate(totals[2 * n : 2 * n + 2], axis=0) for n in range(SUMS)
    )
    moments = jnp.concatenate(
        [one_one, one_two, 2.0 * both - one_one, 2.0 * second - norm], axis=0
    )
    ones = jnp.ones((8, BLOCK), BF16)
    total = jnp.zeros((8, TERMS * R), F32)
    for term in bfloat16_terms(moments):
        total = total + lax.dot_general(
            ones, term.astype(BF16), (((1,), (1,)), ((), ())), preferred_element_type=F32
        )
    for i in range(trace_out.shape[0] // 8):
        trace_out[i * 8 : (i + 1) * 8, :] = total


def local_kernel(
    below, above, above_far, below_far, own_sites, own_start,
    local_out, level, factor, start, real1, imag1, real2, imag2, real3, imag3, real4, products,
):
    real4 = Rows(real4, HALO)
    for s in range(2):
        for x in range(WIDTH_X):
            row = HALO + x
            level[s, row] = jnp.broadcast_to(own_sites[0, s, x : x + 1, :], (8, LANES))
            factor[s, row] = jnp.broadcast_to(own_sites[1, s, x : x + 1, :], (8, LANES))
            start[s, row] = own_start[s, x].astype(F32)
    unpack_rows(below_far, below, level, factor, start, 0, WIDTH_X - HALO)
    unpack_rows(below, below, level, factor, start, NEAR, WIDTH_X - NEAR)
    unpack_rows(above, above, level, factor, start, HALO + WIDTH_X, 0)
    unpack_rows(above_far, above, level, factor, start, HALO + WIDTH_X + NEAR, NEAR)

    def one(i, carry):
        span(level, factor, 1, None, (start, None), (real1, imag1), 2 * i + 1)
        return carry

    lax.fori_loop(0, 7, one, 0)

    def two(i, carry):
        span(level, factor, 2, (start, None), (real1, imag1), (real2, imag2), 2 * i + 2)
        return carry

    lax.fori_loop(0, 6, two, 0)

    def three(i, carry):
        span(level, factor, 3, (real1, imag1), (real2, imag2), (real3, imag3), 2 * i + 3)
        return carry

    lax.fori_loop(0, 5, three, 0)

    def four(i, carry):
        row = 2 * i + HALO
        span(level, factor, 4, (real2, imag2), (real3, imag3), (real4, None), row, width=OWN)
        for d in range(2):
            for s in range(2):
                for n, ref in enumerate((real1, real2, real3, real4)):
                    total = None
                    for h in range(2):
                        index = (s, row + d, slice(h * 8, (h + 1) * 8), slice(0, OWN))
                        product = start[index] * ref[index]
                        total = product if h == 0 else total + product
                    for b in range(BLOCKS):
                        products[n, s, b, pl.ds(8 * (2 * i + d), 8), :] = (
                            total[:, b * BLOCK : (b + 1) * BLOCK]
                        )
        return carry

    lax.fori_loop(0, WIDTH_X // 2, four, 0)
    for n in range(TERMS):
        for s in range(2):
            for b in range(BLOCKS):
                total = products[n, s, b, pl.ds(0, WIDTH_X, stride=8), :]
                for r in range(1, 8):
                    total = total + products[n, s, b, pl.ds(r, WIDTH_X, stride=8), :]
                local_out[n, s, :, b * BLOCK : (b + 1) * BLOCK] = total * (1.0 / R)


def total_kernel(sites, shared, out):
    total = jnp.sum(shared[...], axis=0, keepdims=True) * (1.0 / sites)
    for n in range(TERMS):
        out[n : n + 1, :] = total[:, n * R : (n + 1) * R]


def local(stored_vectors, disorder, vacancy, plan):
    columns = lax.axis_size("gy")
    rows = lax.axis_size("gx")
    devices = rows * columns
    vmem = pl.BlockSpec(memory_space=pltpu.VMEM)
    params = pltpu.CompilerParams(vmem_limit_bytes=8 * 1024 * 1024)

    hbm = pl.BlockSpec(memory_space=pltpu.HBM)
    outgoing, table = pl.pallas_call(
        functools.partial(pack_kernel, columns),
        out_shape=(
            jax.ShapeDtypeStruct((columns, SLOT_ROWS, BLOCK), BF16),
            jax.ShapeDtypeStruct((8, BLOCK), jnp.int32),
        ),
        in_specs=[hbm] * 4,
        out_specs=(vmem, vmem),
        scratch_shapes=[
            pltpu.VMEM((1,) + plan.shape, plan.dtype),
            pltpu.VMEM(stored_vectors.shape, stored_vectors.dtype),
            pltpu.VMEM(disorder.shape, disorder.dtype),
            pltpu.VMEM(vacancy.shape, vacancy.dtype),
            pltpu.VMEM((BLOCKS, 2 * R * WIDTH_X, BLOCK), F32),
            pltpu.SemaphoreType.DMA((4,)),
        ],
        compiler_params=pltpu.CompilerParams(vmem_limit_bytes=16 * 1024 * 1024),
        name="pack",
    )(*(
        pltpu.with_memory_space_constraint(x, pltpu.HBM)
        for x in (plan[None], stored_vectors, disorder, vacancy)
    ))
    received = lax.all_to_all(outgoing, "gy", split_axis=0, concat_axis=0, tiled=True)

    near_message = jax.ShapeDtypeStruct((NEAR_MESSAGE, OWN), BF16)
    far_message = jax.ShapeDtypeStruct((FAR_MESSAGE, OWN), BF16)
    low_near, high_near, low_far, high_far = pl.pallas_call(
        functools.partial(arrange_kernel, columns),
        out_shape=(near_message, near_message, far_message, far_message),
        in_specs=[vmem] * 4,
        out_specs=(vmem,) * 4,
        scratch_shapes=[pltpu.VMEM((4, 4 * 2 * NEAR, OWN), F32)],
        compiler_params=params,
        name="arrange",
    )(table, received, disorder, vacancy)
    up = [(i, (i + 1) % rows) for i in range(rows)]
    down = [(target, source) for source, target in up]
    below = lax.ppermute(high_near, "gx", up)
    above = lax.ppermute(low_near, "gx", down)
    below_far = lax.ppermute(high_far, "gx", up)
    above_far = lax.ppermute(low_far, "gx", down)

    def site(count):
        return jax.ShapeDtypeStruct((2, count, 8, LANES), F32)

    def field(count):
        return jax.ShapeDtypeStruct((2, count, R, LANES), F32)

    def scratch(shape):
        return pltpu.VMEM(shape.shape, shape.dtype)

    *inner, own_sites, own_start = pl.pallas_call(
        functools.partial(interior_kernel, columns),
        out_shape=(site(WIDTH_X), site(WIDTH_X), field(WIDTH_X))
        + (field(len(FIRST_ROWS)),) * 2
        + (field(len(SECOND_ROWS)),) * 2
        + (
            jax.ShapeDtypeStruct((2 * SUMS * 8, BLOCK), F32),
            jax.ShapeDtypeStruct((2, 2, WIDTH_X, LANES), F32),
            jax.ShapeDtypeStruct((2, WIDTH_X, R, LANES), BF16),
        ),
        in_specs=[vmem] * 4,
        out_specs=(vmem,) * 10,
        compiler_params=params,
        cost_estimate=pl.CostEstimate(flops=10**7, bytes_accessed=8 * 10**6, transcendentals=0),
        name="interior",
    )(table, received, disorder, vacancy)
    partial = pl.pallas_call(
        border_kernel,
        out_shape=jax.ShapeDtypeStruct((devices, TERMS * R), F32),
        in_specs=[vmem] * 10,
        out_specs=vmem,
        scratch_shapes=[scratch(site(len(NEAR_ROWS)))] * 2
        + [scratch(field(len(NEAR_ROWS)))]
        + [scratch(field(len(FIRST_BORDER)))] * 2
        + [scratch(field(len(SECOND_BORDER)))] * 2,
        compiler_params=params,
        name="border",
    )(below, above, *inner)
    shared = lax.all_to_all(partial, ("gx", "gy"), split_axis=0, concat_axis=0, tiled=True)
    local_moments = pl.pallas_call(
        local_kernel,
        out_shape=jax.ShapeDtypeStruct((TERMS, 2, WIDTH_X, OWN), F32),
        in_specs=[vmem] * 6,
        out_specs=vmem,
        scratch_shapes=[scratch(site(ROWS_X))] * 2
        + [scratch(field(ROWS_X))] * 7
        + [
            scratch(field(WIDTH_X)),
            pltpu.VMEM((TERMS, 2, BLOCKS, 8 * WIDTH_X, BLOCK), F32),
        ],
        compiler_params=pltpu.CompilerParams(vmem_limit_bytes=16 * 1024 * 1024),
        cost_estimate=pl.CostEstimate(flops=10**7, bytes_accessed=8 * 10**6, transcendentals=0),
        name="local_moments",
    )(below, above, above_far, below_far, own_sites, own_start)
    trace = pl.pallas_call(
        functools.partial(total_kernel, 2 * WIDTH_X * rows * OWN * columns),
        out_shape=jax.ShapeDtypeStruct((TERMS, R), F32),
        in_specs=[vmem],
        out_specs=vmem,
        compiler_params=params,
        name="total",
    )(shared)
    return local_moments, trace


def solution(mesh):
    placed = (P(None, None, "gx", "gy"), P(None, "gx", "gy"), P(None, "gx", "gy"), P())
    return jax.shard_map(
        local, mesh=mesh, in_specs=placed,
        out_specs=(P(None, None, "gx", "gy"), P()), check_vma=False,
    )
```

```python
import functools

import jax
import jax.numpy as jnp
from jax import lax
from jax.experimental import pallas as pl
from jax.experimental.pallas import tpu as pltpu
from jax.sharding import PartitionSpec as P

BLOCK = 128
R = 16
TERMS = 4
HALO = 4
BLOCKS = 4
LANES = BLOCK * (BLOCKS + 1)
OWN = BLOCK * BLOCKS
WIDTH_X = 8
ROWS_X = WIDTH_X + 2 * HALO
SLOT = 2 * WIDTH_X * R
EDGE = SLOT
SITE_EDGE = SLOT + R
SLOT_ROWS = SLOT + R + 8
NEAR = 2
PART = 2 * NEAR * R
PLANES = PART
SIDES = PLANES + 4 * 2 * NEAR
NEAR_MESSAGE = SIDES + 8
FAR_MESSAGE = SIDES

HOP_NEXT = 0.3
TWIST_COS = 0.4535961214255773
TWIST_SIN = 0.8912073600614354
SPREAD = 6.5
COS = HOP_NEXT * TWIST_COS
SIN = HOP_NEXT * TWIST_SIN
F32 = jnp.float32
BF16 = jnp.bfloat16


def bfloat16_terms(value):
    high = value.astype(BF16).astype(F32)
    rest = value - high
    middle = rest.astype(BF16).astype(F32)
    return high, middle, rest - middle


def site_planes(onsite, keep):
    return (*bfloat16_terms(onsite), keep)


def lane_index(rows, lanes):
    return lax.broadcasted_iota(jnp.int32, (rows, lanes), 1)


def pack_kernel(
    columns, plan_hbm, stored_hbm, disorder_hbm, vacancy_hbm, out, table,
    plan, stored, disorder, vacancy, turned, arrived,
):
    copies = [
        pltpu.make_async_copy(source, target, arrived.at[i])
        for i, (source, target) in enumerate(
            ((plan_hbm, plan), (stored_hbm, stored), (disorder_hbm, disorder), (vacancy_hbm, vacancy))
        )
    ]
    for copy in copies:
        copy.start()
    me = lax.axis_index("gy")
    first = me * BLOCKS
    total = BLOCKS * columns
    for copy in copies:
        copy.wait()
    for b in range(BLOCKS):
        block = stored[:, :, :, b * BLOCK : (b + 1) * BLOCK]
        turned[b] = block.reshape(2 * R * WIDTH_X, BLOCK).astype(F32)
    place = lane_index(1, total)
    listed = plan[...]
    spots = [
        jnp.sum(jnp.where(listed == first + b, place, 0), axis=1, keepdims=True)[0, 0]
        for b in range(BLOCKS)
    ]
    source = listed // BLOCKS
    wanted = [first + b for b in range(BLOCKS)]
    wanted += [(first + total - 1) % total, (first + BLOCKS) % total]
    for i, k in enumerate(wanted):
        row = jnp.sum(jnp.where(place == k, source, 0), axis=1, keepdims=True)
        table[i : i + 1, :] = jnp.broadcast_to(row, (1, BLOCK))
    lane = lane_index(8, BLOCK)
    edges = [[jnp.zeros((8, BLOCK), F32) for _ in range(2)] for _ in range(BLOCKS)]
    slots = [spot // BLOCKS for spot in spots]
    for s in range(2):
        for x in range(WIDTH_X):
            q = s * WIDTH_X + x
            for b in range(BLOCKS):
                parts = []
                for h in range(2):
                    base = s * R * WIDTH_X + h * 8 * WIDTH_X + x
                    rows = turned[b, pl.ds(base, 8, stride=WIDTH_X), :]
                    parts.append(rows)
                    moved = pltpu.roll(rows, (8 * q + 4) % BLOCK, 1)
                    edges[b][h] = jnp.where(lane // 8 == q, moved, edges[b][h])
                both = jnp.concatenate(parts, axis=0).astype(BF16)
                out[slots[b], q * R : (q + 1) * R, :] = both
    last_half = lane_index(R, BLOCK) % 8 < 4
    for b in range(BLOCKS):
        spot = spots[b]
        edge = jnp.concatenate(edges[b], axis=0)

        @pl.when(spot % BLOCKS == BLOCKS - 1)
        def _():
            slot = ((spot + 1) // BLOCKS) % columns
            old = out[slot, EDGE : EDGE + R, :].astype(F32)
            out[slot, EDGE : EDGE + R, :] = jnp.where(last_half, edge, old).astype(BF16)

        @pl.when(spot % BLOCKS == 0)
        def _():
            slot = (spot // BLOCKS + columns - 1) % columns
            old = out[slot, EDGE : EDGE + R, :].astype(F32)
            out[slot, EDGE : EDGE + R, :] = jnp.where(last_half, old, edge).astype(BF16)

    lane16 = lane_index(R, BLOCK)
    ends = []
    for ref in (disorder, vacancy):
        low = ref[:, :, 0:BLOCK].reshape(R, BLOCK).astype(F32)
        high = ref[:, :, OWN - BLOCK : OWN].reshape(R, BLOCK).astype(F32)
        ends.append(jnp.where(lane16 < BLOCK // 2, low, high))
    sites = jnp.zeros((R, BLOCK), F32)
    for p, plane in enumerate(site_planes(ends[0], ends[1])):
        sites = jnp.where(lane16 // 8 == p, pltpu.roll(plane, 8 * p + 4, 1), sites)
    sites = jnp.where(lane < 32, sites[0:8], pltpu.roll(sites[8:16], 32, 1)).astype(BF16)
    out[(me + 1) % columns, SITE_EDGE : SITE_EDGE + 8, :] = sites
    out[(me + columns - 1) % columns, SITE_EDGE : SITE_EDGE + 8, :] = sites


def source_of(table, i):
    return table[i : i + 1, 0:1][0, 0]


def edge_tiles(columns, table, received):
    me = lax.axis_index("gy")
    left = source_of(table, BLOCKS)
    right = source_of(table, BLOCKS + 1)
    last_half = lane_index(R, BLOCK) % 8 < 4
    tile = jnp.where(
        last_half,
        received[left, EDGE : EDGE + R, :].astype(F32),
        received[right, EDGE : EDGE + R, :].astype(F32),
    )
    low = (me + columns - 1) % columns
    high = (me + 1) % columns
    sites = jnp.where(
        last_half[0:8],
        received[low, SITE_EDGE : SITE_EDGE + 8, :].astype(F32),
        received[high, SITE_EDGE : SITE_EDGE + 8, :].astype(F32),
    )
    return tile, sites


def arrange_kernel(
    columns, table, received, disorder, vacancy, low_near, high_near, low_far, high_far, planes
):
    outs = ((low_near, 0), (high_near, WIDTH_X - NEAR), (low_far, NEAR), (high_far, NEAR + NEAR))
    size = NEAR * R
    for b in range(BLOCKS):
        slot = source_of(table, b)
        lanes = slice(b * BLOCK, (b + 1) * BLOCK)
        for s in range(2):
            for out, x in outs:
                base = (s * WIDTH_X + x) * R
                out[s * size : (s + 1) * size, lanes] = received[slot, base : base + size, :]
    tile, sites = edge_tiles(columns, table, received)
    for out in (low_near, high_near):
        for i, part in enumerate((tile[0:8], tile[8:16], sites, sites)):
            out[SIDES : SIDES + 8, i * BLOCK : (i + 1) * BLOCK] = part.astype(BF16)
    for s in range(2):
        for p, plane in enumerate(site_planes(disorder[s], vacancy[s].astype(F32))):
            row = p * 2 * NEAR + s * NEAR
            for i, (_, x) in enumerate(outs):
                planes[i, row : row + NEAR, :] = plane[x : x + NEAR]
    for i, (out, _) in enumerate(outs):
        out[PLANES:SIDES, :] = planes[i].astype(BF16)


def fill_sites(level, factor, s, rows, onsite, kept, source, first):
    lane = lane_index(8, BLOCK)
    in_halo = (lane < HALO) | (lane >= BLOCK - HALO)
    side_level = jnp.zeros((8, BLOCK), F32)
    for p in range(3):
        side_level = side_level + pltpu.roll(source, BLOCK - 4 - 8 * p - 32 * s, 1)
    side_keep = pltpu.roll(source, BLOCK - 4 - 8 * 3 - 32 * s, 1)
    side_level = jnp.where(in_halo, side_level, 0.0)
    side_keep = jnp.where(in_halo, side_keep, 0.0)
    kept_rows = []
    for i, row in enumerate(rows):
        j = first + i
        lev = jnp.concatenate([onsite[i : i + 1], side_level[j : j + 1]], axis=1)
        kep = jnp.concatenate([kept[i : i + 1], side_keep[j : j + 1]], axis=1)
        level[s, row] = jnp.broadcast_to(lev * (1.0 / COS), (8, LANES))
        kep = jnp.broadcast_to(kep, (8, LANES))
        factor[s, row] = kep * (2.0 * COS / SPREAD)
        kept_rows.append(kep)
    return kept_rows


def unpack_rows(message, near, level, factor, start, base, x):
    planes = message[PLANES:SIDES, :].astype(F32)
    sides = near[SIDES : SIDES + 8, :].astype(F32)
    tile = jnp.concatenate([sides[:, 0:BLOCK], sides[:, BLOCK : 2 * BLOCK]], axis=0)
    sites = sides[:, 2 * BLOCK : 3 * BLOCK]
    step = 2 * NEAR
    onsite = planes[0:step] + planes[step : 2 * step] + planes[2 * step : 3 * step]
    keep = planes[3 * step : 4 * step]
    for s in range(2):
        some = slice(s * NEAR, (s + 1) * NEAR)
        kept = fill_sites(
            level, factor, s, range(base, base + NEAR), onsite[some], keep[some], sites, x
        )
        for i in range(NEAR):
            index = (s * NEAR + i) * R
            q = s * WIDTH_X + x + i
            side = pltpu.roll(tile, (BLOCK - 4 - 8 * q) % BLOCK, 1)
            value = jnp.concatenate([message[index : index + R, :].astype(F32), side], axis=1)
            for h in range(2):
                part = slice(h * 8, (h + 1) * 8)
                start[s, base + i, part, :] = value[part] * kept[i]


def span(level, factor, term, old, now, new, row, count=2, width=LANES):
    own = slice(0, width)
    for h in range(2):
        part = slice(h * 8, (h + 1) * 8)
        near_rows = range(-1, count + 1)
        real = [{d: now[0][s, row + d, part, :] for d in near_rows} for s in range(2)]
        fields = [real]
        if now[1] is not None:
            fields.append([{d: now[1][s, row + d, part, :] for d in near_rows} for s in range(2)])
        others = [
            [{d: f[s][d] * (1.0 / COS) for d in near_rows} for s in range(2)] for f in fields
        ]
        for s in range(2):
            ratio = SIN / COS if s == 0 else -SIN / COS
            turn = [{d: f[s][d] * ratio for d in near_rows} for f in fields]
            if len(fields) == 1:
                ahead = [real[s], turn[0]]
                back = [real[s], {d: -turn[0][d] for d in near_rows}]
            else:
                imag = fields[1][s]
                ahead = [
                    {d: real[s][d] - turn[1][d] for d in near_rows},
                    {d: imag[d] + turn[0][d] for d in near_rows},
                ]
                back = [
                    {d: real[s][d] + turn[1][d] for d in near_rows},
                    {d: imag[d] - turn[0][d] for d in near_rows},
                ]
            for c in range(2):
                if new[c] is None:
                    continue
                joint = {d: ahead[c][d - 1] + back[c][d] for d in range(count + 1)}
                for d in range(count):
                    out = ahead[c][d + 1][:, own] + back[c][d - 1][:, own]
                    up, down = joint[d], joint[d + 1]
                    if c < len(fields):
                        other = others[c][1 - s]
                        aside = d - 1 if s == 0 else d + 1
                        out = out + level[s, row + d][:, own] * fields[c][s][d][:, own]
                        out = out - (other[d] + other[aside])[:, own]
                        if s == 0:
                            down = down - other[d]
                        else:
                            up = up - other[d]
                    out = out + pltpu.roll(up, LANES - 1, 1)[:, own]
                    out = out + pltpu.roll(down, 1, 1)[:, own]
                    scale = factor[s, row + d][:, own]
                    out = out * (scale * 0.5 if term == 1 else scale)
                    if term > 1 and old[c] is not None:
                        out = out - old[c][s, row + d, part, own]
                    new[c][s, row + d, part, own] = out


def fold(product):
    lanes = product[:, 0:BLOCK]
    for b in range(1, BLOCKS):
        lanes = lanes + product[:, b * BLOCK : (b + 1) * BLOCK]
    return lanes


def trace_row(start, first, second, row, sums):
    own = slice(0, OWN)
    sums = list(sums)
    for h in range(2):
        part = slice(h * 8, (h + 1) * 8)
        for s in range(2):
            v0 = start[s, row, part, own]
            r1 = first[0][s, row, part, own]
            i1 = first[1][s, row, part, own]
            r2 = second[0][s, row, part, own]
            i2 = second[1][s, row, part, own]
            terms = (v0 * v0, v0 * r1, v0 * r2, r1 * r2 + i1 * i2, r2 * r2 + i2 * i2)
            for n, term in enumerate(terms):
                sums[n * 2 + h] = sums[n * 2 + h] + fold(term)
    return tuple(sums)


SUMS = 5


class Rows:
    def __init__(self, ref, first):
        self.ref = ref
        self.first = first

    def __getitem__(self, index):
        s, row, *rest = index
        return self.ref[(s, row - self.first, *rest)]

    def __setitem__(self, index, value):
        s, row, *rest = index
        self.ref[(s, row - self.first, *rest)] = value


class Joined:
    def __init__(self, *pieces):
        self.at = {row: (ref, i) for ref, rows in pieces for i, row in enumerate(rows)}

    def __getitem__(self, index):
        s, row, *rest = index
        ref, i = self.at[row]
        return ref[(s, i, *rest)]

    def __setitem__(self, index, value):
        s, row, *rest = index
        ref, i = self.at[row]
        ref[(s, i, *rest)] = value


OWN_ROWS = range(HALO, HALO + WIDTH_X)
NEAR_ROWS = (2, 3, 12, 13)
FIRST_ROWS = range(5, 11)
FIRST_BORDER = (3, 4, 11, 12)
SECOND_ROWS = range(6, 10)
SECOND_BORDER = (4, 5, 10, 11)


def interior_kernel(
    columns, table, received, disorder, vacancy,
    level, factor, start, real1, imag1, real2, imag2, sums, own_sites, own_start,
):
    own_level, own_factor = level, factor
    level, factor, start = (Rows(ref, HALO) for ref in (level, factor, start))
    real1, imag1 = (Rows(ref, FIRST_ROWS[0]) for ref in (real1, imag1))
    real2, imag2 = (Rows(ref, SECOND_ROWS[0]) for ref in (real2, imag2))
    tile, sites = edge_tiles(columns, table, received)
    slots = [source_of(table, b) for b in range(BLOCKS)]
    for s in range(2):
        kept = fill_sites(
            level, factor, s, range(HALO, HALO + WIDTH_X), disorder[s],
            vacancy[s].astype(F32), sites, 0,
        )
        for x in range(WIDTH_X):
            q = s * WIDTH_X + x
            pieces = [received[slots[b], q * R : (q + 1) * R, :].astype(F32) for b in range(BLOCKS)]
            pieces.append(pltpu.roll(tile, (BLOCK - 4 - 8 * q) % BLOCK, 1))
            value = jnp.concatenate(pieces, axis=1)
            value = value * jnp.concatenate([kept[x], kept[x]], axis=0)
            start[s, HALO + x] = value
            own_start[s, x] = value.astype(BF16)
            own_sites[0, s, x : x + 1, :] = own_level[s, x, 0:1, :]
            own_sites[1, s, x : x + 1, :] = own_factor[s, x, 0:1, :]

    def one(i, carry):
        row = HALO + 1 + 2 * i
        span(level, factor, 1, None, (start, None), (real1, imag1), row)
        return carry

    lax.fori_loop(0, 3, one, 0)

    def two(i, carry):
        row = HALO + 2 + 2 * i
        span(level, factor, 2, (start, None), (real1, imag1), (real2, imag2), row, width=OWN)
        for d in range(2):
            carry = trace_row(start, (real1, imag1), (real2, imag2), row + d, carry)
        return carry

    zero = jnp.zeros((8, BLOCK), F32)
    totals = lax.fori_loop(0, 2, two, (zero,) * (2 * SUMS))
    for i, total in enumerate(totals):
        sums[i * 8 : (i + 1) * 8, :] = total


def border_kernel(
    below, above,
    own_level, own_factor, own_start, own_real1, own_imag1, own_real2, own_imag2, sums_in,
    trace_out,
    near_level, near_factor, near_start, border_real1, border_imag1, border_real2, border_imag2,
):
    level = Joined((own_level, OWN_ROWS), (near_level, NEAR_ROWS))
    factor = Joined((own_factor, OWN_ROWS), (near_factor, NEAR_ROWS))
    start = Joined((own_start, OWN_ROWS), (near_start, NEAR_ROWS))
    real1 = Joined((own_real1, FIRST_ROWS), (border_real1, FIRST_BORDER))
    imag1 = Joined((own_imag1, FIRST_ROWS), (border_imag1, FIRST_BORDER))
    real2 = Joined((own_real2, SECOND_ROWS), (border_real2, SECOND_BORDER))
    imag2 = Joined((own_imag2, SECOND_ROWS), (border_imag2, SECOND_BORDER))
    unpack_rows(below, below, level, factor, start, HALO - NEAR, WIDTH_X - NEAR)
    unpack_rows(above, above, level, factor, start, HALO + WIDTH_X, 0)
    for row in (HALO - 1, HALO + WIDTH_X - 1):
        span(level, factor, 1, None, (start, None), (real1, imag1), row)
    totals = tuple(sums_in[i * 8 : (i + 1) * 8, :] for i in range(2 * SUMS))
    for row in (HALO, HALO + WIDTH_X - 2):
        span(level, factor, 2, (start, None), (real1, imag1), (real2, imag2), row, width=OWN)
        for d in range(2):
            totals = trace_row(start, (real1, imag1), (real2, imag2), row + d, totals)
    norm, one_one, one_two, both, second = (
        jnp.concatenate(totals[2 * n : 2 * n + 2], axis=0) for n in range(SUMS)
    )
    moments = jnp.concatenate(
        [one_one, one_two, 2.0 * both - one_one, 2.0 * second - norm], axis=0
    )
    ones = jnp.ones((8, BLOCK), BF16)
    total = jnp.zeros((8, TERMS * R), F32)
    for term in bfloat16_terms(moments):
        total = total + lax.dot_general(
            ones, term.astype(BF16), (((1,), (1,)), ((), ())), preferred_element_type=F32
        )
    for i in range(trace_out.shape[0] // 8):
        trace_out[i * 8 : (i + 1) * 8, :] = total


def local_kernel(
    below, above, above_far, below_far, own_sites, own_start,
    local_out, level, factor, start, real1, imag1, real2, imag2, real3, imag3, real4, products,
):
    real4 = Rows(real4, HALO)
    for s in range(2):
        for x in range(WIDTH_X):
            row = HALO + x
            level[s, row] = jnp.broadcast_to(own_sites[0, s, x : x + 1, :], (8, LANES))
            factor[s, row] = jnp.broadcast_to(own_sites[1, s, x : x + 1, :], (8, LANES))
            start[s, row] = own_start[s, x].astype(F32)
    unpack_rows(below_far, below, level, factor, start, 0, WIDTH_X - HALO)
    unpack_rows(below, below, level, factor, start, NEAR, WIDTH_X - NEAR)
    unpack_rows(above, above, level, factor, start, HALO + WIDTH_X, 0)
    unpack_rows(above_far, above, level, factor, start, HALO + WIDTH_X + NEAR, NEAR)

    def one(i, carry):
        span(level, factor, 1, None, (start, None), (real1, imag1), 2 * i + 1)
        return carry

    lax.fori_loop(0, 7, one, 0)

    def two(i, carry):
        span(level, factor, 2, (start, None), (real1, imag1), (real2, imag2), 2 * i + 2)
        return carry

    lax.fori_loop(0, 6, two, 0)

    def three(i, carry):
        span(level, factor, 3, (real1, imag1), (real2, imag2), (real3, imag3), 2 * i + 3)
        return carry

    lax.fori_loop(0, 5, three, 0)

    def four(i, carry):
        row = 2 * i + HALO
        span(level, factor, 4, (real2, imag2), (real3, imag3), (real4, None), row, width=OWN)
        for d in range(2):
            for s in range(2):
                for n, ref in enumerate((real1, real2, real3, real4)):
                    total = None
                    for h in range(2):
                        index = (s, row + d, slice(h * 8, (h + 1) * 8), slice(0, OWN))
                        product = start[index] * ref[index]
                        total = product if h == 0 else total + product
                    for b in range(BLOCKS):
                        products[n, s, b, pl.ds(8 * (2 * i + d), 8), :] = (
                            total[:, b * BLOCK : (b + 1) * BLOCK]
                        )
        return carry

    lax.fori_loop(0, WIDTH_X // 2, four, 0)
    for n in range(TERMS):
        for s in range(2):
            for b in range(BLOCKS):
                total = products[n, s, b, pl.ds(0, WIDTH_X, stride=8), :]
                for r in range(1, 8):
                    total = total + products[n, s, b, pl.ds(r, WIDTH_X, stride=8), :]
                local_out[n, s, :, b * BLOCK : (b + 1) * BLOCK] = total * (1.0 / R)


def total_kernel(sites, shared, out):
    total = jnp.sum(shared[...], axis=0, keepdims=True) * (1.0 / sites)
    for n in range(TERMS):
        out[n : n + 1, :] = total[:, n * R : (n + 1) * R]


def local(stored_vectors, disorder, vacancy, plan):
    columns = lax.axis_size("gy")
    rows = lax.axis_size("gx")
    devices = rows * columns
    vmem = pl.BlockSpec(memory_space=pltpu.VMEM)
    params = pltpu.CompilerParams(vmem_limit_bytes=8 * 1024 * 1024)

    hbm = pl.BlockSpec(memory_space=pltpu.HBM)
    outgoing, table = pl.pallas_call(
        functools.partial(pack_kernel, columns),
        out_shape=(
            jax.ShapeDtypeStruct((columns, SLOT_ROWS, BLOCK), BF16),
            jax.ShapeDtypeStruct((8, BLOCK), jnp.int32),
        ),
        in_specs=[hbm] * 4,
        out_specs=(vmem, vmem),
        scratch_shapes=[
            pltpu.VMEM((1,) + plan.shape, plan.dtype),
            pltpu.VMEM(stored_vectors.shape, stored_vectors.dtype),
            pltpu.VMEM(disorder.shape, disorder.dtype),
            pltpu.VMEM(vacancy.shape, vacancy.dtype),
            pltpu.VMEM((BLOCKS, 2 * R * WIDTH_X, BLOCK), F32),
            pltpu.SemaphoreType.DMA((4,)),
        ],
        compiler_params=pltpu.CompilerParams(vmem_limit_bytes=16 * 1024 * 1024),
        name="pack",
    )(*(
        pltpu.with_memory_space_constraint(x, pltpu.HBM)
        for x in (plan[None], stored_vectors, disorder, vacancy)
    ))
    received = lax.all_to_all(outgoing, "gy", split_axis=0, concat_axis=0, tiled=True)

    near_message = jax.ShapeDtypeStruct((NEAR_MESSAGE, OWN), BF16)
    far_message = jax.ShapeDtypeStruct((FAR_MESSAGE, OWN), BF16)
    low_near, high_near, low_far, high_far = pl.pallas_call(
        functools.partial(arrange_kernel, columns),
        out_shape=(near_message, near_message, far_message, far_message),
        in_specs=[vmem] * 4,
        out_specs=(vmem,) * 4,
        scratch_shapes=[pltpu.VMEM((4, 4 * 2 * NEAR, OWN), F32)],
        compiler_params=params,
        name="arrange",
    )(table, received, disorder, vacancy)
    up = [(i, (i + 1) % rows) for i in range(rows)]
    down = [(target, source) for source, target in up]
    below = lax.ppermute(high_near, "gx", up)
    above = lax.ppermute(low_near, "gx", down)
    below_far = lax.ppermute(high_far, "gx", up)
    above_far = lax.ppermute(low_far, "gx", down)

    def site(count):
        return jax.ShapeDtypeStruct((2, count, 8, LANES), F32)

    def field(count):
        return jax.ShapeDtypeStruct((2, count, R, LANES), F32)

    def scratch(shape):
        return pltpu.VMEM(shape.shape, shape.dtype)

    *inner, own_sites, own_start = pl.pallas_call(
        functools.partial(interior_kernel, columns),
        out_shape=(site(WIDTH_X), site(WIDTH_X), field(WIDTH_X))
        + (field(len(FIRST_ROWS)),) * 2
        + (field(len(SECOND_ROWS)),) * 2
        + (
            jax.ShapeDtypeStruct((2 * SUMS * 8, BLOCK), F32),
            jax.ShapeDtypeStruct((2, 2, WIDTH_X, LANES), F32),
            jax.ShapeDtypeStruct((2, WIDTH_X, R, LANES), BF16),
        ),
        in_specs=[vmem] * 4,
        out_specs=(vmem,) * 10,
        compiler_params=params,
        cost_estimate=pl.CostEstimate(flops=10**7, bytes_accessed=8 * 10**6, transcendentals=0),
        name="interior",
    )(table, received, disorder, vacancy)
    partial = pl.pallas_call(
        border_kernel,
        out_shape=jax.ShapeDtypeStruct((devices, TERMS * R), F32),
        in_specs=[vmem] * 10,
        out_specs=vmem,
        scratch_shapes=[scratch(site(len(NEAR_ROWS)))] * 2
        + [scratch(field(len(NEAR_ROWS)))]
        + [scratch(field(len(FIRST_BORDER)))] * 2
        + [scratch(field(len(SECOND_BORDER)))] * 2,
        compiler_params=params,
        name="border",
    )(below, above, *inner)
    shared = lax.all_to_all(partial, ("gx", "gy"), split_axis=0, concat_axis=0, tiled=True)
    local_moments = pl.pallas_call(
        local_kernel,
        out_shape=jax.ShapeDtypeStruct((TERMS, 2, WIDTH_X, OWN), F32),
        in_specs=[vmem] * 6,
        out_specs=vmem,
        scratch_shapes=[scratch(site(ROWS_X))] * 2
        + [scratch(field(ROWS_X))] * 7
        + [
            scratch(field(WIDTH_X)),
            pltpu.VMEM((TERMS, 2, BLOCKS, 8 * WIDTH_X, BLOCK), F32),
        ],
        compiler_params=pltpu.CompilerParams(vmem_limit_bytes=16 * 1024 * 1024),
        cost_estimate=pl.CostEstimate(flops=10**7, bytes_accessed=8 * 10**6, transcendentals=0),
        name="local_moments",
    )(below, above, above_far, below_far, own_sites, own_start)
    trace = pl.pallas_call(
        functools.partial(total_kernel, 2 * WIDTH_X * rows * OWN * columns),
        out_shape=jax.ShapeDtypeStruct((TERMS, R), F32),
        in_specs=[vmem],
        out_specs=vmem,
        compiler_params=params,
        name="total",
    )(shared)
    return local_moments, trace


def solution(mesh):
    placed = (P(None, None, "gx", "gy"), P(None, "gx", "gy"), P(None, "gx", "gy"), P())
    return jax.shard_map(
        local, mesh=mesh, in_specs=placed,
        out_specs=(P(None, None, "gx", "gy"), P()), check_vma=False,
    )
```

```python
import functools

import jax
import jax.numpy as jnp
from jax import lax
from jax.experimental import pallas as pl
from jax.experimental.pallas import tpu as pltpu
from jax.sharding import PartitionSpec as P

BLOCK = 128
R = 16
TERMS = 4
HALO = 4
BLOCKS = 4
LANES = BLOCK * (BLOCKS + 1)
OWN = BLOCK * BLOCKS
WIDTH_X = 8
ROWS_X = WIDTH_X + 2 * HALO
SLOT = 2 * WIDTH_X * R
EDGE = SLOT
SITE_EDGE = SLOT + R
SLOT_ROWS = SLOT + R + 8
NEAR = 2
PART = 2 * NEAR * R
PLANES = PART
SIDES = PLANES + 4 * 2 * NEAR
NEAR_MESSAGE = SIDES + 8
FAR_MESSAGE = SIDES

HOP_NEXT = 0.3
TWIST_COS = 0.4535961214255773
TWIST_SIN = 0.8912073600614354
SPREAD = 6.5
COS = HOP_NEXT * TWIST_COS
SIN = HOP_NEXT * TWIST_SIN
F32 = jnp.float32
BF16 = jnp.bfloat16


def bfloat16_terms(value):
    high = value.astype(BF16).astype(F32)
    rest = value - high
    middle = rest.astype(BF16).astype(F32)
    return high, middle, rest - middle


def site_planes(onsite, keep):
    return (*bfloat16_terms(onsite), keep)


def lane_index(rows, lanes):
    return lax.broadcasted_iota(jnp.int32, (rows, lanes), 1)


def pack_kernel(
    columns, plan_hbm, stored_hbm, disorder_hbm, vacancy_hbm, out, table,
    plan, stored, disorder, vacancy, turned, arrived,
):
    copies = [
        pltpu.make_async_copy(source, target, arrived.at[i])
        for i, (source, target) in enumerate(
            ((plan_hbm, plan), (stored_hbm, stored), (disorder_hbm, disorder), (vacancy_hbm, vacancy))
        )
    ]
    for copy in copies:
        copy.start()
    me = lax.axis_index("gy")
    first = me * BLOCKS
    total = BLOCKS * columns
    copies[0].wait()
    place = lane_index(1, total)
    listed = plan[...]
    spots = [
        jnp.sum(jnp.where(listed == first + b, place, 0), axis=1, keepdims=True)[0, 0]
        for b in range(BLOCKS)
    ]
    source = listed // BLOCKS
    wanted = [first + b for b in range(BLOCKS)]
    wanted += [(first + total - 1) % total, (first + BLOCKS) % total]
    for i, k in enumerate(wanted):
        row = jnp.sum(jnp.where(place == k, source, 0), axis=1, keepdims=True)
        table[i : i + 1, :] = jnp.broadcast_to(row, (1, BLOCK))
    copies[1].wait()
    for b in range(BLOCKS):
        block = stored[:, :, :, b * BLOCK : (b + 1) * BLOCK]
        turned[b] = block.reshape(2 * R * WIDTH_X, BLOCK).astype(F32)
    lane = lane_index(8, BLOCK)
    edges = [[jnp.zeros((8, BLOCK), F32) for _ in range(2)] for _ in range(BLOCKS)]
    slots = [spot // BLOCKS for spot in spots]
    for s in range(2):
        for x in range(WIDTH_X):
            q = s * WIDTH_X + x
            for b in range(BLOCKS):
                parts = []
                for h in range(2):
                    base = s * R * WIDTH_X + h * 8 * WIDTH_X + x
                    rows = turned[b, pl.ds(base, 8, stride=WIDTH_X), :]
                    parts.append(rows)
                    moved = pltpu.roll(rows, (8 * q + 4) % BLOCK, 1)
                    edges[b][h] = jnp.where(lane // 8 == q, moved, edges[b][h])
                both = jnp.concatenate(parts, axis=0).astype(BF16)
                out[slots[b], q * R : (q + 1) * R, :] = both
    last_half = lane_index(R, BLOCK) % 8 < 4
    for b in range(BLOCKS):
        spot = spots[b]
        edge = jnp.concatenate(edges[b], axis=0)

        @pl.when(spot % BLOCKS == BLOCKS - 1)
        def _():
            slot = ((spot + 1) // BLOCKS) % columns
            old = out[slot, EDGE : EDGE + R, :].astype(F32)
            out[slot, EDGE : EDGE + R, :] = jnp.where(last_half, edge, old).astype(BF16)

        @pl.when(spot % BLOCKS == 0)
        def _():
            slot = (spot // BLOCKS + columns - 1) % columns
            old = out[slot, EDGE : EDGE + R, :].astype(F32)
            out[slot, EDGE : EDGE + R, :] = jnp.where(last_half, old, edge).astype(BF16)

    copies[2].wait()
    copies[3].wait()
    lane16 = lane_index(R, BLOCK)
    ends = []
    for ref in (disorder, vacancy):
        low = ref[:, :, 0:BLOCK].reshape(R, BLOCK).astype(F32)
        high = ref[:, :, OWN - BLOCK : OWN].reshape(R, BLOCK).astype(F32)
        ends.append(jnp.where(lane16 < BLOCK // 2, low, high))
    sites = jnp.zeros((R, BLOCK), F32)
    for p, plane in enumerate(site_planes(ends[0], ends[1])):
        sites = jnp.where(lane16 // 8 == p, pltpu.roll(plane, 8 * p + 4, 1), sites)
    sites = jnp.where(lane < 32, sites[0:8], pltpu.roll(sites[8:16], 32, 1)).astype(BF16)
    out[(me + 1) % columns, SITE_EDGE : SITE_EDGE + 8, :] = sites
    out[(me + columns - 1) % columns, SITE_EDGE : SITE_EDGE + 8, :] = sites


def source_of(table, i):
    return table[i : i + 1, 0:1][0, 0]


def edge_tiles(columns, table, received):
    me = lax.axis_index("gy")
    left = source_of(table, BLOCKS)
    right = source_of(table, BLOCKS + 1)
    last_half = lane_index(R, BLOCK) % 8 < 4
    tile = jnp.where(
        last_half,
        received[left, EDGE : EDGE + R, :].astype(F32),
        received[right, EDGE : EDGE + R, :].astype(F32),
    )
    low = (me + columns - 1) % columns
    high = (me + 1) % columns
    sites = jnp.where(
        last_half[0:8],
        received[low, SITE_EDGE : SITE_EDGE + 8, :].astype(F32),
        received[high, SITE_EDGE : SITE_EDGE + 8, :].astype(F32),
    )
    return tile, sites


def arrange_kernel(
    columns, table, received, disorder, vacancy, low_near, high_near, low_far, high_far, planes
):
    outs = ((low_near, 0), (high_near, WIDTH_X - NEAR), (low_far, NEAR), (high_far, NEAR + NEAR))
    size = NEAR * R
    for b in range(BLOCKS):
        slot = source_of(table, b)
        lanes = slice(b * BLOCK, (b + 1) * BLOCK)
        for s in range(2):
            for out, x in outs:
                base = (s * WIDTH_X + x) * R
                out[s * size : (s + 1) * size, lanes] = received[slot, base : base + size, :]
    tile, sites = edge_tiles(columns, table, received)
    for out in (low_near, high_near):
        for i, part in enumerate((tile[0:8], tile[8:16], sites, sites)):
            out[SIDES : SIDES + 8, i * BLOCK : (i + 1) * BLOCK] = part.astype(BF16)
    for s in range(2):
        for p, plane in enumerate(site_planes(disorder[s], vacancy[s].astype(F32))):
            row = p * 2 * NEAR + s * NEAR
            for i, (_, x) in enumerate(outs):
                planes[i, row : row + NEAR, :] = plane[x : x + NEAR]
    for i, (out, _) in enumerate(outs):
        out[PLANES:SIDES, :] = planes[i].astype(BF16)


def fill_sites(level, factor, s, rows, onsite, kept, source, first):
    lane = lane_index(8, BLOCK)
    in_halo = (lane < HALO) | (lane >= BLOCK - HALO)
    side_level = jnp.zeros((8, BLOCK), F32)
    for p in range(3):
        side_level = side_level + pltpu.roll(source, BLOCK - 4 - 8 * p - 32 * s, 1)
    side_keep = pltpu.roll(source, BLOCK - 4 - 8 * 3 - 32 * s, 1)
    side_level = jnp.where(in_halo, side_level, 0.0)
    side_keep = jnp.where(in_halo, side_keep, 0.0)
    kept_rows = []
    for i, row in enumerate(rows):
        j = first + i
        lev = jnp.concatenate([onsite[i : i + 1], side_level[j : j + 1]], axis=1)
        kep = jnp.concatenate([kept[i : i + 1], side_keep[j : j + 1]], axis=1)
        level[s, row] = jnp.broadcast_to(lev * (1.0 / COS), (8, LANES))
        kep = jnp.broadcast_to(kep, (8, LANES))
        factor[s, row] = kep * (2.0 * COS / SPREAD)
        kept_rows.append(kep)
    return kept_rows


def unpack_rows(message, near, level, factor, start, base, x):
    planes = message[PLANES:SIDES, :].astype(F32)
    sides = near[SIDES : SIDES + 8, :].astype(F32)
    tile = jnp.concatenate([sides[:, 0:BLOCK], sides[:, BLOCK : 2 * BLOCK]], axis=0)
    sites = sides[:, 2 * BLOCK : 3 * BLOCK]
    step = 2 * NEAR
    onsite = planes[0:step] + planes[step : 2 * step] + planes[2 * step : 3 * step]
    keep = planes[3 * step : 4 * step]
    for s in range(2):
        some = slice(s * NEAR, (s + 1) * NEAR)
        kept = fill_sites(
            level, factor, s, range(base, base + NEAR), onsite[some], keep[some], sites, x
        )
        for i in range(NEAR):
            index = (s * NEAR + i) * R
            q = s * WIDTH_X + x + i
            side = pltpu.roll(tile, (BLOCK - 4 - 8 * q) % BLOCK, 1)
            value = jnp.concatenate([message[index : index + R, :].astype(F32), side], axis=1)
            for h in range(2):
                part = slice(h * 8, (h + 1) * 8)
                start[s, base + i, part, :] = value[part] * kept[i]


def span(level, factor, term, old, now, new, row, count=2, width=LANES):
    own = slice(0, width)
    for h in range(2):
        part = slice(h * 8, (h + 1) * 8)
        near_rows = range(-1, count + 1)
        real = [{d: now[0][s, row + d, part, :] for d in near_rows} for s in range(2)]
        fields = [real]
        if now[1] is not None:
            fields.append([{d: now[1][s, row + d, part, :] for d in near_rows} for s in range(2)])
        others = [
            [{d: f[s][d] * (1.0 / COS) for d in near_rows} for s in range(2)] for f in fields
        ]
        for s in range(2):
            ratio = SIN / COS if s == 0 else -SIN / COS
            turn = [{d: f[s][d] * ratio for d in near_rows} for f in fields]
            if len(fields) == 1:
                ahead = [real[s], turn[0]]
                back = [real[s], {d: -turn[0][d] for d in near_rows}]
            else:
                imag = fields[1][s]
                ahead = [
                    {d: real[s][d] - turn[1][d] for d in near_rows},
                    {d: imag[d] + turn[0][d] for d in near_rows},
                ]
                back = [
                    {d: real[s][d] + turn[1][d] for d in near_rows},
                    {d: imag[d] - turn[0][d] for d in near_rows},
                ]
            for c in range(2):
                if new[c] is None:
                    continue
                joint = {d: ahead[c][d - 1] + back[c][d] for d in range(count + 1)}
                for d in range(count):
                    out = ahead[c][d + 1][:, own] + back[c][d - 1][:, own]
                    up, down = joint[d], joint[d + 1]
                    if c < len(fields):
                        other = others[c][1 - s]
                        aside = d - 1 if s == 0 else d + 1
                        out = out + level[s, row + d][:, own] * fields[c][s][d][:, own]
                        out = out - (other[d] + other[aside])[:, own]
                        if s == 0:
                            down = down - other[d]
                        else:
                            up = up - other[d]
                    out = out + pltpu.roll(up, LANES - 1, 1)[:, own]
                    out = out + pltpu.roll(down, 1, 1)[:, own]
                    scale = factor[s, row + d][:, own]
                    out = out * (scale * 0.5 if term == 1 else scale)
                    if term > 1 and old[c] is not None:
                        out = out - old[c][s, row + d, part, own]
                    new[c][s, row + d, part, own] = out


def fold(product):
    lanes = product[:, 0:BLOCK]
    for b in range(1, BLOCKS):
        lanes = lanes + product[:, b * BLOCK : (b + 1) * BLOCK]
    return lanes


def trace_row(start, first, second, row, sums):
    own = slice(0, OWN)
    sums = list(sums)
    for h in range(2):
        part = slice(h * 8, (h + 1) * 8)
        for s in range(2):
            v0 = start[s, row, part, own]
            r1 = first[0][s, row, part, own]
            i1 = first[1][s, row, part, own]
            r2 = second[0][s, row, part, own]
            i2 = second[1][s, row, part, own]
            terms = (v0 * v0, v0 * r1, v0 * r2, r1 * r2 + i1 * i2, r2 * r2 + i2 * i2)
            for n, term in enumerate(terms):
                sums[n * 2 + h] = sums[n * 2 + h] + fold(term)
    return tuple(sums)


SUMS = 5


class Rows:
    def __init__(self, ref, first):
        self.ref = ref
        self.first = first

    def __getitem__(self, index):
        s, row, *rest = index
        return self.ref[(s, row - self.first, *rest)]

    def __setitem__(self, index, value):
        s, row, *rest = index
        self.ref[(s, row - self.first, *rest)] = value


class Joined:
    def __init__(self, *pieces):
        self.at = {row: (ref, i) for ref, rows in pieces for i, row in enumerate(rows)}

    def __getitem__(self, index):
        s, row, *rest = index
        ref, i = self.at[row]
        return ref[(s, i, *rest)]

    def __setitem__(self, index, value):
        s, row, *rest = index
        ref, i = self.at[row]
        ref[(s, i, *rest)] = value


OWN_ROWS = range(HALO, HALO + WIDTH_X)
NEAR_ROWS = (2, 3, 12, 13)
FIRST_ROWS = range(5, 11)
FIRST_BORDER = (3, 4, 11, 12)
SECOND_ROWS = range(6, 10)
SECOND_BORDER = (4, 5, 10, 11)


def interior_kernel(
    columns, table, received, disorder, vacancy,
    level, factor, start, real1, imag1, real2, imag2, sums, own_sites, own_start,
):
    own_level, own_factor = level, factor
    level, factor, start = (Rows(ref, HALO) for ref in (level, factor, start))
    real1, imag1 = (Rows(ref, FIRST_ROWS[0]) for ref in (real1, imag1))
    real2, imag2 = (Rows(ref, SECOND_ROWS[0]) for ref in (real2, imag2))
    tile, sites = edge_tiles(columns, table, received)
    slots = [source_of(table, b) for b in range(BLOCKS)]
    for s in range(2):
        kept = fill_sites(
            level, factor, s, range(HALO, HALO + WIDTH_X), disorder[s],
            vacancy[s].astype(F32), sites, 0,
        )
        for x in range(WIDTH_X):
            q = s * WIDTH_X + x
            pieces = [received[slots[b], q * R : (q + 1) * R, :].astype(F32) for b in range(BLOCKS)]
            pieces.append(pltpu.roll(tile, (BLOCK - 4 - 8 * q) % BLOCK, 1))
            value = jnp.concatenate(pieces, axis=1)
            value = value * jnp.concatenate([kept[x], kept[x]], axis=0)
            start[s, HALO + x] = value
            own_start[s, x] = value.astype(BF16)
            own_sites[0, s, x : x + 1, :] = own_level[s, x, 0:1, :]
            own_sites[1, s, x : x + 1, :] = own_factor[s, x, 0:1, :]

    def one(i, carry):
        row = HALO + 1 + 2 * i
        span(level, factor, 1, None, (start, None), (real1, imag1), row)
        return carry

    lax.fori_loop(0, 3, one, 0)

    def two(i, carry):
        row = HALO + 2 + 2 * i
        span(level, factor, 2, (start, None), (real1, imag1), (real2, imag2), row, width=OWN)
        for d in range(2):
            carry = trace_row(start, (real1, imag1), (real2, imag2), row + d, carry)
        return carry

    zero = jnp.zeros((8, BLOCK), F32)
    totals = lax.fori_loop(0, 2, two, (zero,) * (2 * SUMS))
    for i, total in enumerate(totals):
        sums[i * 8 : (i + 1) * 8, :] = total


def border_kernel(
    below, above,
    own_level, own_factor, own_start, own_real1, own_imag1, own_real2, own_imag2, sums_in,
    trace_out,
    near_level, near_factor, near_start, border_real1, border_imag1, border_real2, border_imag2,
):
    level = Joined((own_level, OWN_ROWS), (near_level, NEAR_ROWS))
    factor = Joined((own_factor, OWN_ROWS), (near_factor, NEAR_ROWS))
    start = Joined((own_start, OWN_ROWS), (near_start, NEAR_ROWS))
    real1 = Joined((own_real1, FIRST_ROWS), (border_real1, FIRST_BORDER))
    imag1 = Joined((own_imag1, FIRST_ROWS), (border_imag1, FIRST_BORDER))
    real2 = Joined((own_real2, SECOND_ROWS), (border_real2, SECOND_BORDER))
    imag2 = Joined((own_imag2, SECOND_ROWS), (border_imag2, SECOND_BORDER))
    unpack_rows(below, below, level, factor, start, HALO - NEAR, WIDTH_X - NEAR)
    unpack_rows(above, above, level, factor, start, HALO + WIDTH_X, 0)
    for row in (HALO - 1, HALO + WIDTH_X - 1):
        span(level, factor, 1, None, (start, None), (real1, imag1), row)
    totals = tuple(sums_in[i * 8 : (i + 1) * 8, :] for i in range(2 * SUMS))
    for row in (HALO, HALO + WIDTH_X - 2):
        span(level, factor, 2, (start, None), (real1, imag1), (real2, imag2), row, width=OWN)
        for d in range(2):
            totals = trace_row(start, (real1, imag1), (real2, imag2), row + d, totals)
    norm, one_one, one_two, both, second = (
        jnp.concatenate(totals[2 * n : 2 * n + 2], axis=0) for n in range(SUMS)
    )
    moments = jnp.concatenate(
        [one_one, one_two, 2.0 * both - one_one, 2.0 * second - norm], axis=0
    )
    terms = [term.astype(BF16) for term in bfloat16_terms(moments)]
    total = lax.dot_general(
        jnp.ones((8, 3 * BLOCK), BF16), jnp.concatenate(terms, axis=1),
        (((1,), (1,)), ((), ())), preferred_element_type=F32,
    )
    for i in range(trace_out.shape[0] // 8):
        trace_out[i * 8 : (i + 1) * 8, :] = total


def local_kernel(
    below, above, above_far, below_far, own_sites, own_start,
    local_out, level, factor, start, real1, imag1, real2, imag2, real3, imag3, real4, products,
):
    real4 = Rows(real4, HALO)
    for s in range(2):
        for x in range(WIDTH_X):
            row = HALO + x
            level[s, row] = jnp.broadcast_to(own_sites[0, s, x : x + 1, :], (8, LANES))
            factor[s, row] = jnp.broadcast_to(own_sites[1, s, x : x + 1, :], (8, LANES))
            start[s, row] = own_start[s, x].astype(F32)
    unpack_rows(below_far, below, level, factor, start, 0, WIDTH_X - HALO)
    unpack_rows(below, below, level, factor, start, NEAR, WIDTH_X - NEAR)
    unpack_rows(above, above, level, factor, start, HALO + WIDTH_X, 0)
    unpack_rows(above_far, above, level, factor, start, HALO + WIDTH_X + NEAR, NEAR)

    def one(i, carry):
        span(level, factor, 1, None, (start, None), (real1, imag1), 2 * i + 1)
        return carry

    lax.fori_loop(0, 7, one, 0)

    def two(i, carry):
        span(level, factor, 2, (start, None), (real1, imag1), (real2, imag2), 2 * i + 2)
        return carry

    lax.fori_loop(0, 6, two, 0)

    def three(i, carry):
        span(level, factor, 3, (real1, imag1), (real2, imag2), (real3, imag3), 2 * i + 3)
        return carry

    lax.fori_loop(0, 5, three, 0)

    def four(i, carry):
        row = 2 * i + HALO
        span(level, factor, 4, (real2, imag2), (real3, imag3), (real4, None), row, width=OWN)
        for d in range(2):
            for s in range(2):
                for n, ref in enumerate((real1, real2, real3, real4)):
                    total = None
                    for h in range(2):
                        index = (s, row + d, slice(h * 8, (h + 1) * 8), slice(0, OWN))
                        product = start[index] * ref[index]
                        total = product if h == 0 else total + product
                    for b in range(BLOCKS):
                        products[n, s, b, pl.ds(8 * (2 * i + d), 8), :] = (
                            total[:, b * BLOCK : (b + 1) * BLOCK]
                        )
        return carry

    lax.fori_loop(0, WIDTH_X // 2, four, 0)
    for n in range(TERMS):
        for s in range(2):
            for b in range(BLOCKS):
                total = products[n, s, b, pl.ds(0, WIDTH_X, stride=8), :]
                for r in range(1, 8):
                    total = total + products[n, s, b, pl.ds(r, WIDTH_X, stride=8), :]
                local_out[n, s, :, b * BLOCK : (b + 1) * BLOCK] = total * (1.0 / R)


def total_kernel(sites, shared, out):
    total = jnp.sum(shared[...], axis=0, keepdims=True) * (1.0 / sites)
    for n in range(TERMS):
        out[n : n + 1, :] = total[:, n * R : (n + 1) * R]


def local(stored_vectors, disorder, vacancy, plan):
    columns = lax.axis_size("gy")
    rows = lax.axis_size("gx")
    devices = rows * columns
    vmem = pl.BlockSpec(memory_space=pltpu.VMEM)
    params = pltpu.CompilerParams(vmem_limit_bytes=8 * 1024 * 1024)

    hbm = pl.BlockSpec(memory_space=pltpu.HBM)
    outgoing, table = pl.pallas_call(
        functools.partial(pack_kernel, columns),
        out_shape=(
            jax.ShapeDtypeStruct((columns, SLOT_ROWS, BLOCK), BF16),
            jax.ShapeDtypeStruct((8, BLOCK), jnp.int32),
        ),
        in_specs=[hbm] * 4,
        out_specs=(vmem, vmem),
        scratch_shapes=[
            pltpu.VMEM((1,) + plan.shape, plan.dtype),
            pltpu.VMEM(stored_vectors.shape, stored_vectors.dtype),
            pltpu.VMEM(disorder.shape, disorder.dtype),
            pltpu.VMEM(vacancy.shape, vacancy.dtype),
            pltpu.VMEM((BLOCKS, 2 * R * WIDTH_X, BLOCK), F32),
            pltpu.SemaphoreType.DMA((4,)),
        ],
        compiler_params=pltpu.CompilerParams(vmem_limit_bytes=16 * 1024 * 1024),
        name="pack",
    )(*(
        pltpu.with_memory_space_constraint(x, pltpu.HBM)
        for x in (plan[None], stored_vectors, disorder, vacancy)
    ))
    received = lax.all_to_all(outgoing, "gy", split_axis=0, concat_axis=0, tiled=True)

    near_message = jax.ShapeDtypeStruct((NEAR_MESSAGE, OWN), BF16)
    far_message = jax.ShapeDtypeStruct((FAR_MESSAGE, OWN), BF16)
    low_near, high_near, low_far, high_far = pl.pallas_call(
        functools.partial(arrange_kernel, columns),
        out_shape=(near_message, near_message, far_message, far_message),
        in_specs=[vmem] * 4,
        out_specs=(vmem,) * 4,
        scratch_shapes=[pltpu.VMEM((4, 4 * 2 * NEAR, OWN), F32)],
        compiler_params=params,
        name="arrange",
    )(table, received, disorder, vacancy)
    up = [(i, (i + 1) % rows) for i in range(rows)]
    down = [(target, source) for source, target in up]
    below = lax.ppermute(high_near, "gx", up)
    above = lax.ppermute(low_near, "gx", down)
    below_far = lax.ppermute(high_far, "gx", up)
    above_far = lax.ppermute(low_far, "gx", down)

    def site(count):
        return jax.ShapeDtypeStruct((2, count, 8, LANES), F32)

    def field(count):
        return jax.ShapeDtypeStruct((2, count, R, LANES), F32)

    def scratch(shape):
        return pltpu.VMEM(shape.shape, shape.dtype)

    *inner, own_sites, own_start = pl.pallas_call(
        functools.partial(interior_kernel, columns),
        out_shape=(site(WIDTH_X), site(WIDTH_X), field(WIDTH_X))
        + (field(len(FIRST_ROWS)),) * 2
        + (field(len(SECOND_ROWS)),) * 2
        + (
            jax.ShapeDtypeStruct((2 * SUMS * 8, BLOCK), F32),
            jax.ShapeDtypeStruct((2, 2, WIDTH_X, LANES), F32),
            jax.ShapeDtypeStruct((2, WIDTH_X, R, LANES), BF16),
        ),
        in_specs=[vmem] * 4,
        out_specs=(vmem,) * 10,
        compiler_params=params,
        cost_estimate=pl.CostEstimate(flops=10**7, bytes_accessed=8 * 10**6, transcendentals=0),
        name="interior",
    )(table, received, disorder, vacancy)
    partial = pl.pallas_call(
        border_kernel,
        out_shape=jax.ShapeDtypeStruct((devices, TERMS * R), F32),
        in_specs=[vmem] * 10,
        out_specs=vmem,
        scratch_shapes=[scratch(site(len(NEAR_ROWS)))] * 2
        + [scratch(field(len(NEAR_ROWS)))]
        + [scratch(field(len(FIRST_BORDER)))] * 2
        + [scratch(field(len(SECOND_BORDER)))] * 2,
        compiler_params=params,
        name="border",
    )(below, above, *inner)
    shared = lax.all_to_all(partial, ("gx", "gy"), split_axis=0, concat_axis=0, tiled=True)
    local_moments = pl.pallas_call(
        local_kernel,
        out_shape=jax.ShapeDtypeStruct((TERMS, 2, WIDTH_X, OWN), F32),
        in_specs=[vmem] * 6,
        out_specs=vmem,
        scratch_shapes=[scratch(site(ROWS_X))] * 2
        + [scratch(field(ROWS_X))] * 7
        + [
            scratch(field(WIDTH_X)),
            pltpu.VMEM((TERMS, 2, BLOCKS, 8 * WIDTH_X, BLOCK), F32),
        ],
        compiler_params=pltpu.CompilerParams(vmem_limit_bytes=16 * 1024 * 1024),
        cost_estimate=pl.CostEstimate(flops=10**7, bytes_accessed=8 * 10**6, transcendentals=0),
        name="local_moments",
    )(below, above, above_far, below_far, own_sites, own_start)
    trace = pl.pallas_call(
        functools.partial(total_kernel, 2 * WIDTH_X * rows * OWN * columns),
        out_shape=jax.ShapeDtypeStruct((TERMS, R), F32),
        in_specs=[vmem],
        out_specs=vmem,
        compiler_params=params,
        name="total",
    )(shared)
    return local_moments, trace


def solution(mesh):
    placed = (P(None, None, "gx", "gy"), P(None, "gx", "gy"), P(None, "gx", "gy"), P())
    return jax.shard_map(
        local, mesh=mesh, in_specs=placed,
        out_specs=(P(None, None, "gx", "gy"), P()), check_vma=False,
    )
```
